32 devices in a mesh: group: 1, image: 4 (over z), prow: 4 (over y, x), pcol: 2 (over core).
Axes of the slice: x: 2, y: 2, z: 4, core: 2. Of those that a mesh axis runs over, the one named last changes fastest.
Arguments:
- latent: bfloat16 [4, 32, 64, 640], P(('group', 'image'), 'prow', 'pcol'), may hold values from -6 to 6
- conv_weight: bfloat16 [3, 3, 640, 640], replicated, may hold values from -0.078125 to 0.078125
- w_query: bfloat16 [640, 640], replicated, may hold values from -2 to 2
- w_key: bfloat16 [640, 640], replicated, may hold values from -2 to 2
- w_value: bfloat16 [640, 640], replicated, may hold values from -0.25 to 0.25
- w_out: bfloat16 [640, 640], replicated, may hold values from -0.25 to 0.25
- anchor_index: int32 [4], P('group'), may hold values from 0 to 3, as said below
- block_order: int32 [4, 16], P('group'), may hold values from 0 to 15, each once within a row
- block_count: int32 [4], P('group'), may hold values from 1 to 4, as said below
Outputs:
- features: bfloat16 [4, 32, 64, 640], P(('group', 'image'), 'prow', 'pcol')
- attended: bfloat16 [4, 32, 64, 640], P(('group', 'image'), 'prow', 'pcol')
The draws below stay inside these ranges and needn't reach their ends.
Inputs may be any that keep to these rules, and one draw needn't show every extreme that they name: `anchor_index`: 4 different images of the batch. `block_count`: some anchor has 4 subject blocks.
All inputs are finite; a program needn't handle non-finite values.
Results may differ from the reference program's by a relative error of at most 0.017.
Values may be sent and summed in bfloat16 or wider, within the bound.
No kernel may reach another device: no remote copies, remote signals or barrier semaphores. Data moves between devices by JAX's collectives and lax.ppermute only.
A program may use at most 128 MiB of HBM per device.

```python
import jax
import jax.numpy as jnp
from jax import lax

D = 640
HEADS = 10
HEAD_DIM = 64
PR = 8
PC = 32
BLOCK = 128
ANCHORS = 4
NSEL = 4
IMAGES = 4
LAT_ROWS = 32
LAT_COLS = 64
BLOCKS = 16
N_PROW = 4
N_PCOL = 2


def query_key_pair(key):
    base = jax.random.fold_in(key, 11)
    first, second = jax.random.split(base, 2)
    sigma = (3.0 / D) ** 0.5
    query_weight = sigma * jax.random.truncated_normal(first, -4.0, 4.0, (D, D), jnp.float32)
    key_weight = sigma * jax.random.truncated_normal(second, -4.0, 4.0, (D, D), jnp.float32)
    return (jnp.clip(query_weight, -2.0, 2.0), jnp.clip(key_weight, -2.0, 2.0))


def draw_w_query(key, part):
    return query_key_pair(key)[0].astype(jnp.bfloat16)


def draw_w_key(key, part):
    return query_key_pair(key)[1].astype(jnp.bfloat16)


def draw_anchor_index(key, part):
    order = jax.random.permutation(jax.random.fold_in(key, 3), IMAGES)
    return order[:ANCHORS].astype(jnp.int32)


def draw_block_count(key, part):
    base = jax.random.fold_in(key, 5)
    counts = jax.random.randint(base, (ANCHORS,), 1, NSEL + 1)
    fullest = jax.random.randint(jax.random.fold_in(base, 1), (), 0, ANCHORS)
    counts = jnp.where(jnp.arange(ANCHORS) == fullest, NSEL, counts)
    return counts.astype(jnp.int32)


def block_levels(own_key, dims, cuts, low, largest):
    loudness, own = 1.0, jax.random.fold_in(own_key, 6)
    for axis_at, blocks in cuts:
        steps = jnp.exp(jax.random.uniform(jax.random.fold_in(own, axis_at), (blocks,), jnp.float32, low / len(cuts), largest / len(cuts)))
        loudness = loudness * jnp.repeat(steps, dims[axis_at] // blocks).reshape([-1 if axis == axis_at else 1 for axis in range(len(dims))])
    return loudness


def normal_values(rng, extent, scale, reach, cuts=(), dtype=jnp.bfloat16):
    gain = block_levels(rng, extent, cuts, -0.22, 0.18) if cuts else 1.0
    array = jax.random.normal(rng, extent, jnp.float32) * scale * gain
    return jnp.minimum(jnp.maximum(array, -reach), reach).astype(dtype)


def setup_inputs(seed: int = 0, part: int = 0) -> dict:
    splits = jax.random.split(jax.random.key(seed), 10)
    part_keys = jax.random.split(jax.random.fold_in(splits[9], part), 10)
    return {
        "latent": normal_values(part_keys[0], (IMAGES, LAT_ROWS, LAT_COLS, D), 1.0, 6.0, ((0, 4), (1, 4), (2, 2))),
        "conv_weight": normal_values(splits[1], (3, 3, D, D), (9 * D) ** -0.5, 0.078125),
        "w_query": draw_w_query(jax.random.fold_in(splits[9], 71), part),
        "w_key": draw_w_key(jax.random.fold_in(splits[9], 71), part),
        "w_value": normal_values(splits[4], (D, D), D ** -0.5, 0.25),
        "w_out": normal_values(splits[5], (D, D), D ** -0.5, 0.25),
        "anchor_index": draw_anchor_index(jax.random.fold_in(jax.random.fold_in(splits[9], part), 71), part),
        "block_order": jax.vmap(lambda own: jax.random.permutation(own, BLOCKS))(jax.random.split(part_keys[7], ANCHORS)).reshape((ANCHORS, BLOCKS)).astype(jnp.int32),
        "block_count": draw_block_count(jax.random.fold_in(jax.random.fold_in(splits[9], part), 71), part),
    }


def layer_norm(values):
    centered = values - lax.optimization_barrier(jnp.mean(values, axis=-1, keepdims=True))
    spread = lax.optimization_barrier(jnp.mean(centered * centered, axis=-1, keepdims=True))
    return centered * lax.rsqrt(spread + 1e-05)

def split_heads(matrix):
    return matrix.reshape(matrix.shape[0], HEADS, HEAD_DIM).transpose(1, 0, 2)

def reference(latent, conv_weight, w_query, w_key, w_value, w_out, anchor_index, block_order, block_count):
    activated = jax.nn.silu(latent.astype(jnp.float32)).astype(jnp.bfloat16)
    padded = jnp.pad(activated, ((0, 0), (1, 1), (1, 1), (0, 0)))
    height, breadth, channels = (latent.shape[1], latent.shape[2], latent.shape[3])
    running = latent.astype(jnp.float32)
    for row_tap in range(3):
        for col_tap in range(3):
            window = padded[:, row_tap:row_tap + height, col_tap:col_tap + breadth, :]
            running = running + jnp.dot(window, conv_weight[row_tap, col_tap], preferred_element_type=jnp.float32)
    features = running.astype(jnp.bfloat16)
    tokens = features.reshape(IMAGES, N_PROW, PR, N_PCOL, PC, channels).transpose(0, 1, 3, 2, 4, 5).reshape(IMAGES, -1, channels)
    normed = layer_norm(tokens.astype(jnp.float32)).astype(jnp.bfloat16)
    queries = jnp.dot(normed, w_query, preferred_element_type=jnp.float32).astype(jnp.bfloat16)
    key_rows = jnp.dot(normed, w_key, preferred_element_type=jnp.float32).astype(jnp.bfloat16)
    value_rows = jnp.dot(normed, w_value, preferred_element_type=jnp.float32).astype(jnp.bfloat16)
    picked_keys = []
    picked_values = []
    live_list = []
    for anchor in range(ANCHORS):
        chosen = block_order[anchor, :NSEL]
        source = anchor_index[anchor]
        picked_keys.append(key_rows[source].reshape(BLOCKS, BLOCK, channels)[chosen].reshape(NSEL * BLOCK, channels))
        picked_values.append(value_rows[source].reshape(BLOCKS, BLOCK, channels)[chosen].reshape(NSEL * BLOCK, channels))
        live_slots = jnp.arange(NSEL) < block_count[anchor]
        live_list.append(jnp.repeat(live_slots, BLOCK))
    anchor_keys = jnp.concatenate(picked_keys, axis=0)
    anchor_values = jnp.concatenate(picked_values, axis=0)
    allowed = jnp.concatenate([jnp.ones((BLOCKS * BLOCK,), jnp.bool_)] + live_list)

    def one_head(inputs):
        head_query, head_key, head_value = inputs
        scores = jnp.dot(head_query, head_key.T, preferred_element_type=jnp.float32) * HEAD_DIM ** (-0.5)
        scores = jnp.where(allowed[None, :], scores, -jnp.inf)
        peak = lax.optimization_barrier(jnp.max(scores, axis=1, keepdims=True))
        exponent = jnp.exp(scores - peak)
        probs = (exponent / lax.optimization_barrier(jnp.sum(exponent, axis=1, keepdims=True))).astype(jnp.bfloat16)
        return jnp.dot(probs, head_value, preferred_element_type=jnp.float32).astype(jnp.bfloat16)

    def one_image(inputs):
        image_query, image_key, image_value = inputs
        every_key = jnp.concatenate([image_key, anchor_keys], axis=0)
        every_value = jnp.concatenate([image_value, anchor_values], axis=0)
        head_outs = lax.map(one_head, (split_heads(image_query), split_heads(every_key), split_heads(every_value)))
        merged = head_outs.transpose(1, 0, 2).reshape(-1, channels)
        return jnp.dot(merged, w_out, preferred_element_type=jnp.float32).astype(jnp.bfloat16)
    attended = lax.map(one_image, (queries, key_rows, value_rows))
    attended = attended.reshape(IMAGES, N_PROW, N_PCOL, PR, PC, channels).transpose(0, 1, 3, 2, 4, 5).reshape(IMAGES, height, breadth, channels)
    return (features, attended)
```

```python
import functools

import jax
import jax.numpy as jnp
from jax import lax
from jax.experimental import pallas as pl
from jax.experimental.pallas import tpu as pltpu
from jax.sharding import PartitionSpec as P

HEAD_DIM = 64
BLOCK = 128
NSEL = 4
LANES = 128
F32 = jnp.float32
BF16 = jnp.bfloat16


VMEM = pl.BlockSpec(memory_space=pltpu.VMEM)
SMEM = pl.BlockSpec(memory_space=pltpu.SMEM)
ANY = pl.BlockSpec(memory_space=pl.ANY)


def source_of(index, step, count):
    if count & (count - 1) == 0:
        return index ^ step
    return (index + step) % count


def exchange(block, axis, step):
    count = lax.axis_size(axis)
    return lax.ppermute(block, axis, [(source_of(i, step, count), i) for i in range(count)])


def shifted(block, axis, step):
    count = lax.axis_size(axis)
    return lax.ppermute(block, axis, [((i + step) % count, i) for i in range(count)])


def halo(cells):
    core, cores = lax.axis_index("pcol"), lax.axis_size("pcol")
    rows = lax.axis_size("prow")
    first, last = cells[:, 0], cells[:, -1]
    if cores == 2:
        other = shifted(jnp.where(core == 0, last, first), "pcol", 1)
        zero = jnp.zeros_like(other)
        left = jnp.where(core == 1, other, zero)
        right = jnp.where(core == 0, other, zero)
    else:
        left = lax.ppermute(last, "pcol", [(i, i + 1) for i in range(cores - 1)])
        right = lax.ppermute(first, "pcol", [(i + 1, i) for i in range(cores - 1)])
    low = jnp.concatenate([cells[-1], left[-1:], right[-1:]], axis=0)
    high = jnp.concatenate([cells[0], left[:1], right[:1]], axis=0)
    above = lax.ppermute(low, "prow", [(i, i + 1) for i in range(rows - 1)])
    below = lax.ppermute(high, "prow", [(i + 1, i) for i in range(rows - 1)])
    return left, right, above, below


def conv_kernel(rows, cols, x_ref, left_ref, right_ref, above_ref, below_ref, w_ref,
                features_ref, normed_ref, shift0, shift1, shift2):
    def silu(v):
        v = v.astype(F32)
        return (v / (1.0 + jnp.exp(-v))).astype(BF16).astype(F32)

    side = lax.broadcasted_iota(jnp.int32, (cols, x_ref.shape[1]), 0)
    for r in range(rows + 2):
        if r == 0:
            cells, lcell, rcell = above_ref[:cols], above_ref[cols:cols + 1], above_ref[cols + 1:cols + 2]
        elif r == rows + 1:
            cells, lcell, rcell = below_ref[:cols], below_ref[cols:cols + 1], below_ref[cols + 1:cols + 2]
        else:
            cells = x_ref[(r - 1) * cols:r * cols]
            lcell, rcell = left_ref[r - 1:r], right_ref[r - 1:r]
        cells, lcell, rcell = silu(cells), silu(lcell), silu(rcell)
        at = slice(r * cols, (r + 1) * cols)
        shift1[at] = cells.astype(BF16)
        shift0[at] = jnp.where(side == 0, lcell, pltpu.roll(cells, 1, 0)).astype(BF16)
        shift2[at] = jnp.where(side == cols - 1, rcell, pltpu.roll(cells, cols - 1, 0)).astype(BF16)
    total = x_ref[...].astype(F32)
    for a in range(3):
        for b, shift in enumerate((shift0, shift1, shift2)):
            total = total + jnp.dot(
                shift[a * cols:(a + rows) * cols], w_ref[a, b], preferred_element_type=F32
            )
    features = total.astype(BF16)
    features_ref[...] = features
    values = features.astype(F32)
    centered = values - jnp.mean(values, axis=-1, keepdims=True)
    spread = jnp.mean(centered * centered, axis=-1, keepdims=True)
    normed_ref[...] = (centered * lax.rsqrt(spread + 1e-05)).astype(BF16)


def conv_norm(cells, sides, conv_weight):
    rows, cols, channels = cells.shape
    tokens = rows * cols
    out = jax.ShapeDtypeStruct((tokens, channels), BF16)
    return pl.pallas_call(
        functools.partial(conv_kernel, rows, cols),
        out_shape=(out, out),
        in_specs=[VMEM] * 6,
        out_specs=(VMEM, VMEM),
        scratch_shapes=[pltpu.VMEM(((rows + 2) * cols, channels), BF16)] * 3,
        compiler_params=pltpu.CompilerParams(vmem_limit_bytes=40 << 20),
        cost_estimate=pl.CostEstimate(
            flops=18 * tokens * channels * channels,
            bytes_accessed=18 * channels * channels,
            transcendentals=tokens * channels,
        ),
        name="conv_norm",
    )(cells.reshape(tokens, channels), *sides, conv_weight)


def query_kernel(*refs):
    *normed_refs, w_ref, q_ref = refs
    size = normed_refs[0].shape[0]
    for n, ref in enumerate(normed_refs):
        q = jnp.dot(ref[...], w_ref[...], preferred_element_type=F32).astype(BF16)
        q_ref[n * size:(n + 1) * size] = (q.astype(F32) * HEAD_DIM ** (-0.5)).astype(BF16)


def make_queries(normed_list, w_query):
    size, channels = normed_list[0].shape
    rows = size * len(normed_list)
    return pl.pallas_call(
        query_kernel,
        out_shape=jax.ShapeDtypeStruct((rows, channels), BF16),
        in_specs=[VMEM] * (len(normed_list) + 1),
        out_specs=VMEM,
        cost_estimate=pl.CostEstimate(
            flops=2 * rows * channels * channels, bytes_accessed=2 * channels * (rows + channels),
            transcendentals=0,
        ),
        name="queries",
    )(*normed_list, w_query)


def attention_kernel(tiles, groups, q_ref, mult_ref, *refs):
    key_refs = refs[:tiles]
    wk_ref, wv_ref, out_ref, lse_ref, k_scr, v_scr = refs[tiles:]
    size, channels = key_refs[0].shape
    pairs = channels // LANES
    per = size // groups
    half = LANES // 2
    for t, key_ref in enumerate(key_refs):
        normed = key_ref[...]
        k = jnp.dot(normed, wk_ref[...], preferred_element_type=F32).astype(BF16)
        v = jnp.dot(normed, wv_ref[...], preferred_element_type=F32)
        row = lax.broadcasted_iota(jnp.int32, (size, LANES), 0)
        lane = lax.broadcasted_iota(jnp.int32, (size, LANES), 1)
        mult = jnp.full((size, LANES), mult_ref[t, 0], F32)
        for g in range(1, groups):
            mult = jnp.where(row >= g * per, mult_ref[t, g], mult)
        at = slice(t * size, (t + 1) * size)
        for pair in range(pairs):
            cut = slice(pair * LANES, (pair + 1) * LANES)
            k_scr[pair, at] = k[:, cut]
            scaled = v[:, cut] * mult
            v_scr[2 * pair, at] = jnp.where(lane < half, scaled, mult).astype(BF16)
            v_scr[2 * pair + 1, at] = jnp.where(lane < half, mult, scaled).astype(BF16)
    q_rows = q_ref.shape[0]
    steps = q_rows // size
    lse_ref[...] = jnp.zeros_like(lse_ref)
    lane = lax.broadcasted_iota(jnp.int32, (size, LANES), 1)

    def block(qb, carry):
        rows = pl.ds(pl.multiple_of(qb * size, size), size)
        lse = jnp.zeros((size, LANES), F32)
        for pair in range(pairs):
            q = q_ref[rows, pair * LANES:(pair + 1) * LANES]
            outs, peaks = [], []
            for side in range(2):
                keep = (lane < half) if side == 0 else (lane >= half)
                masked = jnp.where(keep, q, jnp.zeros_like(q))
                scores = lax.dot_general(
                    masked, k_scr[pair], (((1,), (1,)), ((), ())), preferred_element_type=F32
                )
                peak = jnp.max(scores, axis=1, keepdims=True)
                probs = jnp.exp(scores - peak).astype(BF16)
                outs.append(jnp.dot(probs, v_scr[2 * pair + side], preferred_element_type=F32))
                peaks.append(peak)
            sums = pltpu.roll(jnp.where(lane < half, outs[1], outs[0]), half, 1)
            value = jnp.where(lane < half, outs[0], outs[1]) / sums
            level = jnp.where(lane < half, peaks[0], peaks[1]) + jnp.log(sums)
            out_ref[rows, pair * LANES:(pair + 1) * LANES] = value.astype(out_ref.dtype)
            lse = jnp.where(lane == 2 * pair, level[:, :1], lse)
            lse = jnp.where(lane == 2 * pair + 1, level[:, half:half + 1], lse)
        lse_ref[rows] = lse
        return carry

    lax.fori_loop(0, steps, block, 0)


def attend(queries, mult, key_list, w_key, w_value):
    size, channels = key_list[0].shape
    tiles, groups = mult.shape
    rows = queries.shape[0]
    keys = size * tiles
    pairs = channels // LANES
    return pl.pallas_call(
        functools.partial(attention_kernel, tiles, groups),
        out_shape=(
            jax.ShapeDtypeStruct((rows, channels), BF16),
            jax.ShapeDtypeStruct((rows, LANES), F32),
        ),
        in_specs=[VMEM, SMEM] + [VMEM] * (tiles + 2),
        out_specs=(VMEM, VMEM),
        scratch_shapes=[
            pltpu.VMEM((pairs, keys, LANES), BF16),
            pltpu.VMEM((2 * pairs, keys, LANES), BF16),
        ],
        compiler_params=pltpu.CompilerParams(vmem_limit_bytes=40 << 20),
        cost_estimate=pl.CostEstimate(
            flops=4 * keys * channels * channels + 16 * rows * keys * channels,
            bytes_accessed=2 * channels * (2 * rows + keys + 2 * channels),
            transcendentals=rows * keys * channels // HEAD_DIM,
        ),
        name="attend",
    )(queries, mult, *key_list, w_key, w_value)


def spread_heads(levels, pair):
    lane = lax.broadcasted_iota(jnp.int32, (levels.shape[0], LANES), 1)
    return jnp.where(
        lane < LANES // 2, levels[:, 2 * pair:2 * pair + 1], levels[:, 2 * pair + 1:2 * pair + 2]
    )


def merged_pair(parts, pair):
    levels = [spread_heads(level, pair) for _, level in parts]
    peak = functools.reduce(jnp.maximum, levels)
    weights = [jnp.exp(level - peak) for level in levels]
    total = functools.reduce(jnp.add, weights)
    cut = slice(pair * LANES, (pair + 1) * LANES)
    value = functools.reduce(
        jnp.add, [w * part[:, cut].astype(F32) for w, (part, _) in zip(weights, parts)]
    )
    return value / total, peak + jnp.log(total)


def pack_kernel(count, size, *refs):
    parts = [(refs[2 * n], refs[2 * n + 1]) for n in range(count)]
    own_ref, level_ref, *sent = refs[2 * count:]
    channels = own_ref.shape[1]
    pairs = channels // LANES
    lane = lax.broadcasted_iota(jnp.int32, (size, LANES), 1)
    for n in range(1 + len(sent)):
        at = slice(n * size, (n + 1) * size)
        loaded = [(o[at], l[at]) for o, l in parts]
        levels = jnp.zeros((size, LANES), F32)
        for pair in range(pairs):
            value, level = merged_pair(loaded, pair)
            cut = slice(pair * LANES, (pair + 1) * LANES)
            (own_ref if n == 0 else sent[n - 1])[:, cut] = value.astype(BF16)
            levels = jnp.where(lane == 2 * pair, level[:, :1], levels)
            levels = jnp.where(lane == 2 * pair + 1, level[:, LANES // 2:LANES // 2 + 1], levels)
        if n == 0:
            level_ref[...] = levels
        else:
            high = levels.astype(BF16).astype(F32)
            rest = levels - high
            middle = rest.astype(BF16).astype(F32)
            low = rest - middle
            packed = jnp.where(lane < 32, high, jnp.where(
                lane < 64, pltpu.roll(middle, 32, 1), pltpu.roll(low, 64, 1)))
            sent[n - 1][:, channels:] = packed.astype(BF16)


def pack(parts, size, others):
    channels = parts[0][0].shape[1]
    flat = [leaf for part in parts for leaf in part]
    return pl.pallas_call(
        functools.partial(pack_kernel, len(parts), size),
        out_shape=(
            jax.ShapeDtypeStruct((size, channels), BF16),
            jax.ShapeDtypeStruct((size, LANES), F32),
        ) + (jax.ShapeDtypeStruct((size, channels + LANES), BF16),) * others,
        in_specs=[VMEM] * len(flat),
        out_specs=(VMEM,) * (2 + others),
        cost_estimate=pl.CostEstimate(
            flops=1, bytes_accessed=sum(leaf.nbytes for leaf in flat), transcendentals=0
        ),
        name="pack",
    )(*flat)


def finish_kernel(own_ref, level_ref, *refs):
    *received, w_ref, out_ref = refs
    channels = own_ref.shape[1]
    parts = [(own_ref[...], level_ref[...])]
    for ref in received:
        packed = ref[:, channels:].astype(F32)
        levels = packed + pltpu.roll(packed, LANES - 32, 1) + pltpu.roll(packed, LANES - 64, 1)
        parts.append((ref[:, :channels], levels))
    merged = [merged_pair(parts, pair)[0].astype(BF16) for pair in range(channels // LANES)]
    out_ref[...] = jnp.dot(
        jnp.concatenate(merged, axis=1), w_ref[...], preferred_element_type=F32
    ).astype(BF16)


def finish(own, level, received, w_out):
    return pl.pallas_call(
        finish_kernel,
        out_shape=jax.ShapeDtypeStruct(own.shape, BF16),
        in_specs=[VMEM] * (3 + len(received)),
        out_specs=VMEM,
        name="finish",
    )(own, level, *received, w_out)


def pick_kernel(cores, shards, where_ref, *refs):
    sources, outs, sem = refs[:shards], refs[shards:shards + cores], refs[shards + cores]
    core = lax.axis_index("pcol")
    slots = where_ref.shape[1]
    per = outs[0].shape[0] // slots
    for n in range(shards):
        for slot in range(slots):
            @pl.when(where_ref[0, slot] == n)
            def _():
                for s in range(cores):
                    row = where_ref[1, slot] + lax.rem(core + s, cores) * per
                    pltpu.make_async_copy(
                        sources[n].at[pl.ds(pl.multiple_of(row, per), per)],
                        outs[s].at[slot * per:(slot + 1) * per],
                        sem.at[slot, s],
                    ).start()
    for slot in range(slots):
        for s in range(cores):
            pltpu.make_async_copy(
                sources[0].at[:per], outs[s].at[slot * per:(slot + 1) * per], sem.at[slot, s]
            ).wait()


def pick(shards, where, cores):
    channels = shards[0].shape[1]
    slots = where.shape[1]
    rows = slots * BLOCK // cores
    return pl.pallas_call(
        functools.partial(pick_kernel, cores, len(shards)),
        out_shape=(jax.ShapeDtypeStruct((rows, channels), BF16),) * cores,
        in_specs=[SMEM] + [ANY] * len(shards),
        out_specs=(VMEM,) * cores,
        scratch_shapes=[pltpu.SemaphoreType.DMA((slots, cores))],
        name="pick",
    )(where, *shards)


def one_of(table, chosen):
    return jnp.sum(jnp.where(chosen.reshape((-1,) + (1,) * (table.ndim - 1)), table, 0), axis=0)


def shards(
    latent, conv_weight, w_query, w_key, w_value, w_out, anchor_index, block_order, block_count
):
    tile_rows, tile_cols, channels = latent.shape[1:]
    tokens = tile_rows * tile_cols
    cores, prows, images = (lax.axis_size(a) for a in ("pcol", "prow", "image"))
    core, prow, image = (lax.axis_index(a) for a in ("pcol", "prow", "image"))
    anchors = anchor_index.shape[0]
    every_image = images == anchors
    per_patch = tokens // BLOCK
    slot = jnp.arange(NSEL)
    order = block_order[:, :NSEL]

    features, normed = conv_norm(latent[0], halo(latent[0]), conv_weight)
    siblings = [shifted(normed, "pcol", s) for s in range(1, cores)]
    plane = [normed] + [exchange(normed, "prow", s) for s in range(1, prows)]
    queries = make_queries([normed] + siblings, w_query)

    held = jnp.stack([source_of(prow, s, prows) for s in range(prows)])
    blocks = (held[:, None] * cores + core) * per_patch + jnp.arange(per_patch)
    if every_image:
        mine = anchor_index == image
        my_order, my_count = one_of(order, mine), one_of(block_count, mine)
        live = slot < my_count
        again = jnp.any((blocks[..., None] == my_order) & live, axis=-1)
        own_mult = 1.0 + again.astype(F32)
    else:
        own_mult = jnp.ones(blocks.shape, F32)

    parts = [attend(queries, own_mult[:1], plane[:1], w_key, w_value)]
    if prows > 1:
        parts.append(attend(queries, own_mult[1:], plane[1:], w_key, w_value))

    def picked(wanted):
        patch = wanted // per_patch
        place = jnp.stack([
            source_of(patch // cores, prow, prows) if prows & (prows - 1) == 0
            else (patch // cores - prow) % prows,
            wanted % per_patch * BLOCK,
        ])
        views = pick(plane, place, cores)
        rows = views[0].reshape(NSEL, -1, channels)
        holder = patch % cores
        for s in range(1, cores):
            seen = shifted(views[s], "pcol", cores - s).reshape(rows.shape)
            rows = jnp.where((holder == (core - s) % cores)[:, None, None], seen, rows)
        return rows.reshape(-1, channels)

    if every_image:
        share = picked(jnp.where(live, my_order, my_order[0]))
        sources = [exchange(share, "image", s) for s in range(1, images)]
        counts = jnp.stack([
            one_of(block_count, anchor_index == source_of(image, s, images))
            for s in range(1, images)
        ])
    else:
        size = NSEL * BLOCK // cores
        share = size // prows
        received = []
        for anchor in range(anchors):
            live = slot < block_count[anchor]
            rows = picked(jnp.where(live, order[anchor], order[anchor, 0]))
            part = lax.dynamic_slice_in_dim(rows, prow * share, share, 0)
            part = jnp.where(image == anchor_index[anchor], part, jnp.zeros_like(part))
            received.append(lax.psum(part, "image"))
        joined = lax.all_gather(jnp.stack(received), "prow", axis=1, tiled=True)
        sources = [joined[anchor] for anchor in range(anchors)]
        counts = block_count
    anchor_mult = (slot < counts[:, None]).astype(F32)
    if sources:
        parts.append(attend(queries, anchor_mult, sources, w_key, w_value))

    own, level, *sent = pack(parts, tokens, cores - 1)
    received = [shifted(block, "pcol", cores - s) for s, block in enumerate(sent, 1)]
    attended = finish(own, level, received, w_out)
    return features.reshape(latent.shape), attended.reshape(latent.shape)


def solution(mesh):
    tiled = P(("group", "image"), "prow", "pcol", None)
    return jax.shard_map(
        shards,
        mesh=mesh,
        in_specs=(tiled, P(), P(), P(), P(), P(), P("group"), P("group", None), P("group")),
        out_specs=(tiled, tiled),
        check_vma=False,
    )
```

```python
import functools

import jax
import jax.numpy as jnp
from jax import lax
from jax.experimental import pallas as pl
from jax.experimental.pallas import tpu as pltpu
from jax.sharding import PartitionSpec as P

HEAD_DIM = 64
BLOCK = 128
NSEL = 4
LANES = 128
SUBLANES = 8
ONES = 16
F32 = jnp.float32
BF16 = jnp.bfloat16
MIB = 1 << 20


VMEM = pl.BlockSpec(memory_space=pltpu.VMEM)
SMEM = pl.BlockSpec(memory_space=pltpu.SMEM)
ANY = pl.BlockSpec(memory_space=pl.ANY)


def shape(*dims, dtype=BF16):
    return jax.ShapeDtypeStruct(dims, dtype)


def cost(flops, moved, exps=0):
    return pl.CostEstimate(flops=flops, bytes_accessed=moved, transcendentals=exps)


def grant(mib):
    return pltpu.CompilerParams(vmem_limit_bytes=mib * MIB)


def source_of(index, step, count):
    if count & (count - 1) == 0:
        return index ^ step
    return lax.rem(index + step, count) if not isinstance(index, int) else (index + step) % count


def step_of(index, source, count):
    if count & (count - 1) == 0:
        return index ^ source
    return lax.rem(source - index + count, count)


def exchange(block, axis, step):
    count = lax.axis_size(axis)
    return lax.ppermute(block, axis, [(source_of(i, step, count), i) for i in range(count)])


def shifted(block, axis, step):
    count = lax.axis_size(axis)
    return lax.ppermute(block, axis, [((i + step) % count, i) for i in range(count)])


def halo(cells):
    core, cores = lax.axis_index("pcol"), lax.axis_size("pcol")
    rows, cols = lax.axis_size("prow"), cells.shape[1]
    if cores == 2:
        inner = lax.dynamic_index_in_dim(cells, jnp.where(core == 0, cols - 1, 0), 1, keepdims=False)
        other = shifted(inner, "pcol", 1)
        zero = jnp.zeros_like(other)
        left = jnp.where(core == 1, other, zero)
        right = jnp.where(core == 0, other, zero)
    else:
        left = lax.ppermute(cells[:, -1], "pcol", [(i, i + 1) for i in range(cores - 1)])
        right = lax.ppermute(cells[:, 0], "pcol", [(i + 1, i) for i in range(cores - 1)])
    low = jnp.concatenate([cells[-1], left[-1:], right[-1:]], axis=0)
    high = jnp.concatenate([cells[0], left[:1], right[:1]], axis=0)
    above = lax.ppermute(low, "prow", [(i, i + 1) for i in range(rows - 1)])
    below = lax.ppermute(high, "prow", [(i + 1, i) for i in range(rows - 1)])
    return left, right, above, below


def stage_kernel(*refs):
    count = len(refs) // 2
    copies = [
        pltpu.make_async_copy(refs[n], refs[count + n], refs[-1].at[n]) for n in range(count)
    ]
    for copy in copies:
        copy.start()
    for copy in copies:
        copy.wait()


def stage(*arrays):
    return pl.pallas_call(
        stage_kernel,
        out_shape=tuple(shape(*a.shape, dtype=a.dtype) for a in arrays),
        in_specs=[ANY] * len(arrays),
        out_specs=(VMEM,) * len(arrays),
        scratch_shapes=[pltpu.SemaphoreType.DMA((len(arrays),))],
        compiler_params=grant(16),
        cost_estimate=cost(0, 2 * sum(a.nbytes for a in arrays)),
        name="stage",
    )(*arrays)


def conv_kernel(rows, cols, cores, x_ref, left_ref, right_ref, above_ref, below_ref, w_ref, *refs):
    features_ref, *half_refs, shift0, shift1, shift2 = refs

    def silu(v):
        v = v.astype(F32)
        return (v / (1.0 + jnp.exp(-v))).astype(BF16).astype(F32)

    side = lax.broadcasted_iota(jnp.int32, (cols, x_ref.shape[1]), 0)
    for r in range(rows + 2):
        if r == 0 or r == rows + 1:
            ref = above_ref if r == 0 else below_ref
            cells, lcell, rcell = ref[:cols], ref[cols:cols + 1], ref[cols + 1:cols + 2]
        else:
            cells = x_ref[(r - 1) * cols:r * cols]
            lcell, rcell = left_ref[r - 1:r], right_ref[r - 1:r]
        cells, lcell, rcell = silu(cells), silu(lcell), silu(rcell)
        at = slice(r * cols, (r + 1) * cols)
        shift1[at] = cells.astype(BF16)
        shift0[at] = jnp.where(side == 0, lcell, pltpu.roll(cells, 1, 0)).astype(BF16)
        shift2[at] = jnp.where(side == cols - 1, rcell, pltpu.roll(cells, cols - 1, 0)).astype(BF16)
    total = x_ref[...].astype(F32)
    for a in range(3):
        for b, shift in enumerate((shift0, shift1, shift2)):
            total = total + jnp.dot(
                shift[a * cols:(a + rows) * cols], w_ref[a, b], preferred_element_type=F32
            )
    features = total.astype(BF16)
    features_ref[...] = features
    values = features.astype(F32)
    centered = values - jnp.mean(values, axis=-1, keepdims=True)
    spread = jnp.mean(centered * centered, axis=-1, keepdims=True)
    normed = (centered * lax.rsqrt(spread + 1e-05)).astype(BF16)
    core = lax.axis_index("pcol")
    per = BLOCK // cores
    for b in range(rows * cols // BLOCK):
        for h in range(cores):
            rows_of = normed[b * BLOCK + h * per:b * BLOCK + (h + 1) * per]
            for s, ref in enumerate(half_refs):
                @pl.when(lax.rem(core + s, cores) == h)
                def _():
                    ref[b * per:(b + 1) * per] = rows_of


def conv_norm(cells, sides, conv_weight, cores):
    rows, cols, channels = cells.shape
    tokens = rows * cols
    return pl.pallas_call(
        functools.partial(conv_kernel, rows, cols, cores),
        out_shape=(shape(tokens, channels),) + (shape(tokens // cores, channels),) * cores,
        in_specs=[VMEM] * 6,
        out_specs=(VMEM,) * (1 + cores),
        scratch_shapes=[pltpu.VMEM(((rows + 2) * cols, channels), BF16)] * 3,
        compiler_params=grant(24),
        cost_estimate=cost(18 * tokens * channels**2, 18 * channels**2, tokens * channels),
        name="conv_norm",
    )(cells.reshape(tokens, channels), *sides, conv_weight)


class Table:
    def __init__(self, ref, anchors, images):
        self.ref, self.anchors, self.images = ref, anchors, images
        self.every_image = anchors == images

    @staticmethod
    def build(anchor_index, block_count, order):
        return jnp.concatenate([anchor_index, block_count, order.reshape(-1)])

    def anchor_at(self, image):
        found = jnp.int32(0)
        for a in range(1, self.anchors):
            found = jnp.where(self.ref[a] == image, a, found)
        return found

    def count(self, anchor):
        return self.ref[self.anchors + anchor]

    def block(self, anchor, slot):
        return self.ref[2 * self.anchors + anchor * NSEL + slot]

    def own_times(self, step, group, cores, prows, per_patch):
        if not self.every_image:
            return jnp.float32(1.0)
        s, b = divmod(group, per_patch)
        patch = source_of(lax.axis_index("prow"), step, prows) * cores
        block = (patch + lax.rem(lax.axis_index("pcol") + s, cores)) * per_patch + b
        anchor = self.anchor_at(lax.axis_index("image"))
        times = jnp.float32(1.0)
        for slot in range(NSEL):
            hit = (slot < self.count(anchor)) & (self.block(anchor, slot) == block)
            times = jnp.where(hit, 2.0, times)
        return times

    def anchor_times(self, source, slot):
        if self.every_image:
            image = source_of(lax.axis_index("image"), source + 1, self.images)
            source = self.anchor_at(image)
        return jnp.where(slot < self.count(source), 1.0, 0.0).astype(F32)


def project_tile(normed, at, times, wk_ref, wvt_ref, k_scr, v_scr):
    size, channels = normed.shape
    k = jnp.dot(normed, wk_ref[...], preferred_element_type=F32).astype(BF16)
    for pair in range(channels // LANES):
        k_scr[pair, at] = k[:, pair * LANES:(pair + 1) * LANES]
    v = lax.dot_general(
        wvt_ref[...], normed, (((1,), (1,)), ((), ())), preferred_element_type=F32
    )
    per = size // len(times)
    lane = lax.broadcasted_iota(jnp.int32, (1, size), 1)
    mult = jnp.full((1, size), times[0], F32)
    for g in range(1, len(times)):
        mult = jnp.where(lane >= g * per, times[g], mult)
    v = (v * mult).astype(BF16)
    ones = jnp.broadcast_to(mult, (ONES, size)).astype(BF16)
    for head in range(channels // HEAD_DIM):
        v_scr[head, :HEAD_DIM, at] = v[head * HEAD_DIM:(head + 1) * HEAD_DIM]
        v_scr[head, HEAD_DIM:, at] = ones


def attend_heads(q_ref, k_scr, v_scr, out_ref, level_ref, width):
    queries = q_ref.shape[1]
    zeros = jnp.zeros((HEAD_DIM, width), BF16)

    def pair_step(pair, carry):
        for side in range(2):
            for qb in range(queries // width):
                cols = slice(qb * width, (qb + 1) * width)
                base = pl.multiple_of(pair * LANES + side * HEAD_DIM, HEAD_DIM)
                q = q_ref[pl.ds(base, HEAD_DIM), cols]
                q = jnp.concatenate([q, zeros] if side == 0 else [zeros, q], axis=0)
                scores = jnp.dot(k_scr[pair], q, preferred_element_type=F32)
                peak = jnp.max(scores, axis=0, keepdims=True)
                probs = jnp.exp(scores - peak).astype(BF16)
                value = jnp.dot(v_scr[2 * pair + side], probs, preferred_element_type=F32)
                total = value[HEAD_DIM:HEAD_DIM + 1]
                out_ref[pl.ds(base, HEAD_DIM), cols] = (
                    value[:HEAD_DIM] * (1.0 / total)
                ).astype(out_ref.dtype)
                level_ref[2 * pair + side, :, cols] = jnp.broadcast_to(
                    peak + jnp.log(total), (SUBLANES, width)
                )
        return carry

    lax.fori_loop(0, q_ref.shape[0] // LANES, pair_step, 0)


def own_kernel(info, n_parts, table_ref, *refs):
    anchors, images, cores, prows, per_patch = info
    part_refs, key_ref = refs[:n_parts], refs[n_parts]
    wq_ref, wk_ref, wv_ref, q_ref, out_ref, level_ref, k_scr, v_scr = refs[n_parts + 1:]
    table = Table(table_ref, anchors, images)
    at = 0
    for ref in part_refs:
        q = lax.dot_general(
            wq_ref[...], ref[...], (((1,), (1,)), ((), ())), preferred_element_type=F32
        ).astype(BF16)
        q_ref[:, at:at + ref.shape[0]] = (q.astype(F32) * HEAD_DIM ** (-0.5)).astype(BF16)
        at += ref.shape[0]
    times = [table.own_times(0, g, cores, prows, per_patch) for g in range(cores * per_patch)]
    size = key_ref.shape[0]
    project_tile(key_ref[...], slice(0, size), times, wk_ref, wv_ref, k_scr, v_scr)
    attend_heads(q_ref, k_scr, v_scr, out_ref, level_ref, size)


def key_scratch(keys, channels):
    return [
        pltpu.VMEM((channels // LANES, keys, LANES), BF16),
        pltpu.VMEM((channels // HEAD_DIM, HEAD_DIM + ONES, keys), BF16),
    ]


def attend_cost(rows, keys, channels, extra=0):
    return cost(
        4 * keys * channels**2 + 16 * rows * keys * channels + extra,
        2 * channels * (2 * rows + keys),
        rows * keys * channels // HEAD_DIM,
    )


def attend_own(info, table, parts, key, w_query, w_key, w_value):
    size, channels = key.shape
    rows = sum(part.shape[0] for part in parts)
    return pl.pallas_call(
        functools.partial(own_kernel, info, len(parts)),
        out_shape=(
            shape(channels, rows), shape(channels, rows),
            shape(channels // HEAD_DIM, SUBLANES, rows, dtype=F32),
        ),
        in_specs=[SMEM] + [VMEM] * (len(parts) + 4),
        out_specs=(VMEM,) * 3,
        scratch_shapes=key_scratch(size, channels),
        compiler_params=grant(24),
        cost_estimate=attend_cost(rows, size, channels, 2 * rows * channels**2),
        name="attend_own",
    )(table, *parts, key, w_query, w_key, w_value)


def plane_kernel(info, tiles, table_ref, q_ref, *refs):
    anchors, images, cores, prows, per_patch = info
    key_refs = refs[:tiles]
    wk_ref, wv_ref, out_ref, level_ref, k_scr, v_scr = refs[tiles:]
    table = Table(table_ref, anchors, images)
    size = key_refs[0].shape[0]
    for t, ref in enumerate(key_refs):
        times = [
            table.own_times(t + 1, g, cores, prows, per_patch) for g in range(cores * per_patch)
        ]
        at = slice(t * size, (t + 1) * size)
        project_tile(ref[...], at, times, wk_ref, wv_ref, k_scr, v_scr)
    attend_heads(q_ref, k_scr, v_scr, out_ref, level_ref, size)


def attend_plane(info, table, queries, keys, w_key, w_value):
    size, channels = keys[0].shape
    rows = queries.shape[1]
    return pl.pallas_call(
        functools.partial(plane_kernel, info, len(keys)),
        out_shape=(
            shape(channels, rows), shape(channels // HEAD_DIM, SUBLANES, rows, dtype=F32),
        ),
        in_specs=[SMEM] + [VMEM] * (len(keys) + 3),
        out_specs=(VMEM,) * 2,
        scratch_shapes=key_scratch(size * len(keys), channels),
        compiler_params=grant(24),
        cost_estimate=attend_cost(rows, size * len(keys), channels),
        name="attend_plane",
    )(table, queries, *keys, w_key, w_value)


def merge_head(parts, head, cols):
    rows = slice(head * HEAD_DIM, (head + 1) * HEAD_DIM)
    levels = [level(head, cols) for _, level in parts]
    peak = functools.reduce(jnp.maximum, levels)
    weights = [jnp.exp(level - peak) for level in levels]
    total = functools.reduce(jnp.add, weights)
    value = functools.reduce(
        jnp.add, [w * ref[rows, cols].astype(F32) for w, (ref, _) in zip(weights, parts)]
    )
    return value * (1.0 / total), peak + jnp.log(total)


def anchor_kernel(info, tiles, earlier, groups, table_ref, q_ref, *refs):
    anchors, images, cores, prows, per_patch = info
    key_refs, refs = refs[:tiles], refs[tiles:]
    early_refs, refs = refs[:2 * earlier], refs[2 * earlier:]
    wk_ref, wv_ref, *out_refs = refs[:2 + groups + 1]
    out_scr, level_scr, k_scr, v_scr = refs[3 + groups:]
    own_ref, own_level_ref, *sent_refs = out_refs
    table = Table(table_ref, anchors, images)
    size = key_refs[0].shape[0]
    for t, ref in enumerate(key_refs):
        times = [table.anchor_times(t, slot) for slot in range(NSEL)]
        at = slice(t * size, (t + 1) * size)
        project_tile(ref[...], at, times, wk_ref, wv_ref, k_scr, v_scr)
    attend_heads(q_ref, k_scr, v_scr, out_scr, level_scr, size)
    channels = q_ref.shape[0]
    width = q_ref.shape[1] // groups
    pairs = list(zip(early_refs[::2], early_refs[1::2])) + [(out_scr, level_scr)]
    parts = [
        (ref, lambda head, cols, level=level: level[head, 0:1, cols]) for ref, level in pairs
    ]
    heads = channels // HEAD_DIM
    row = lax.broadcasted_iota(jnp.int32, (2 * SUBLANES, width), 0)
    for n in range(groups):
        cols = slice(n * width, (n + 1) * width)
        ref = own_ref if n == 0 else sent_refs[n - 1]
        levels = jnp.zeros((2 * SUBLANES, width), F32)
        for head in range(heads):
            value, level = merge_head(parts, head, cols)
            ref[head * HEAD_DIM:(head + 1) * HEAD_DIM] = value.astype(BF16)
            levels = jnp.where(row == head, level, levels)
        if n == 0:
            own_level_ref[...] = levels
        else:
            for term in range(3):
                high = levels.astype(BF16)
                at = channels + term * 2 * SUBLANES
                ref[at:at + 2 * SUBLANES] = high
                levels = levels - high.astype(F32)


def attend_anchors(info, table, queries, keys, earlier, w_key, w_value, groups):
    size, channels = keys[0].shape
    rows = queries.shape[1]
    width = rows // groups
    flat = [leaf for part in earlier for leaf in part]
    heads = channels // HEAD_DIM
    return pl.pallas_call(
        functools.partial(anchor_kernel, info, len(keys), len(earlier), groups),
        out_shape=(shape(channels, width), shape(2 * SUBLANES, width, dtype=F32))
        + (shape(channels + 6 * SUBLANES, width),) * (groups - 1),
        in_specs=[SMEM] + [VMEM] * (len(keys) + len(flat) + 3),
        out_specs=(VMEM,) * (1 + groups),
        scratch_shapes=[
            pltpu.VMEM((channels, rows), BF16), pltpu.VMEM((heads, SUBLANES, rows), F32),
        ] + key_scratch(size * len(keys), channels),
        compiler_params=grant(24),
        cost_estimate=attend_cost(rows, size * len(keys), channels),
        name="attend_anchors",
    )(table, queries, *keys, *flat, w_key, w_value)


def finish_kernel(cores, own_ref, level_ref, *refs):
    *received, w_ref, out_ref, merged = refs
    channels, tokens = own_ref.shape

    def row_of(ref, base, terms):
        def level(head, cols):
            return functools.reduce(jnp.add, [
                ref[base + t * 2 * SUBLANES:base + (t + 1) * 2 * SUBLANES].astype(F32)
                for t in range(terms)
            ])[head:head + 1]
        return level

    parts = [(own_ref, row_of(level_ref, 0, 1))]
    parts += [(ref, row_of(ref, channels, 3)) for ref in received]
    every = slice(0, tokens)
    for head in range(channels // HEAD_DIM):
        value, _ = merge_head(parts, head, every)
        merged[head * HEAD_DIM:(head + 1) * HEAD_DIM] = value.astype(BF16)
    out = lax.dot_general(
        merged[...], w_ref[...], (((0,), (0,)), ((), ())), preferred_element_type=F32
    ).astype(BF16)
    core = lax.axis_index("pcol")
    per = BLOCK // cores
    blocks = tokens // BLOCK
    for s in range(cores):
        for b in range(blocks):
            at = b * BLOCK + lax.rem(core + s, cores) * per
            out_ref[pl.ds(pl.multiple_of(at, per), per)] = out[
                (s * blocks + b) * per:(s * blocks + b + 1) * per
            ]


def finish(own, level, received, w_out, cores):
    channels, tokens = own.shape
    return pl.pallas_call(
        functools.partial(finish_kernel, cores),
        out_shape=shape(tokens, channels),
        in_specs=[VMEM] * (3 + len(received)),
        out_specs=VMEM,
        scratch_shapes=[pltpu.VMEM((channels, tokens), BF16)],
        compiler_params=grant(16),
        cost_estimate=cost(2 * tokens * channels**2, 2 * channels * (channels + 3 * tokens)),
        name="finish",
    )(own, level, *received, w_out)


def pick_kernel(info, anchor, table_ref, *refs):
    anchors, images, cores, prows, per_patch = info
    *sources, out_ref = refs
    table = Table(table_ref, anchors, images)
    core, prow = lax.axis_index("pcol"), lax.axis_index("prow")
    if anchor is None:
        anchor = table.anchor_at(lax.axis_index("image"))
    per = BLOCK // cores
    for slot in range(NSEL):
        block = table.block(anchor, jnp.where(slot < table.count(anchor), slot, 0))
        patch, inner = lax.div(block, per_patch), lax.rem(block, per_patch)
        held = step_of(prow, lax.div(patch, cores), prows)
        part = lax.rem(lax.rem(patch, cores) - core + cores, cores)
        at = pl.multiple_of((part * per_patch + inner) * per, per)
        for n, ref in enumerate(sources):
            @pl.when(held == n)
            def _():
                out_ref[slot * per:(slot + 1) * per] = ref[pl.ds(at, per)]


def pick(info, anchor, table, sources):
    channels = sources[0].shape[1]
    rows = NSEL * BLOCK // info[2]
    return pl.pallas_call(
        functools.partial(pick_kernel, info, anchor),
        out_shape=shape(rows, channels),
        in_specs=[SMEM] + [VMEM] * len(sources),
        out_specs=VMEM,
        compiler_params=grant(8),
        name="pick",
    )(table, *sources)


def shards(
    latent, conv_weight, w_query, w_key, w_value, w_out, anchor_index, block_order, block_count
):
    tile_rows, tile_cols, channels = latent.shape[1:]
    cores, prows, images = (lax.axis_size(a) for a in ("pcol", "prow", "image"))
    prow, image = lax.axis_index("prow"), lax.axis_index("image")
    anchors = anchor_index.shape[0]
    per_patch = tile_rows * tile_cols // BLOCK
    info = (anchors, images, cores, prows, per_patch)
    table = Table.build(anchor_index, block_count, block_order[:, :NSEL])
    wq, wv = w_query.T, w_value.T

    (staged,) = stage(conv_weight)
    features, *parts = conv_norm(latent[0], halo(latent[0]), staged, cores)
    keys, queries = [parts[0]], list(parts)
    for s in range(1, cores):
        theirs = [None] * cores
        for t in [cores - s] + [t for t in range(cores) if t != cores - s]:
            theirs[t] = shifted(parts[t], "pcol", s)
        keys.append(theirs[cores - s])
        queries += theirs
    key = jnp.concatenate(keys, axis=0)
    plane = [exchange(key, "prow", s) for s in range(1, prows)]
    q, value, level = attend_own(info, table, queries, key, wq, w_key, wv)
    done = [(value, level)]

    if anchors == images:
        share = pick(info, None, table, [key] + plane)
        sources = [exchange(share, "image", s) for s in range(1, images)]
    else:
        size = NSEL * BLOCK // cores
        share = size // prows
        received = []
        for anchor in range(anchors):
            rows = pick(info, anchor, table, [key] + plane)
            part = lax.dynamic_slice_in_dim(rows, prow * share, share, 0)
            part = jnp.where(image == anchor_index[anchor], part, jnp.zeros_like(part))
            received.append(lax.psum(part, "image"))
        joined = lax.all_gather(jnp.stack(received), "prow", axis=1, tiled=True)
        sources = [joined[anchor] for anchor in range(anchors)]
    if plane:
        done.append(attend_plane(info, table, q, plane, w_key, wv))
    own, level, *sent = attend_anchors(info, table, q, sources, done, w_key, wv, cores)
    received = [shifted(block, "pcol", cores - s) for s, block in enumerate(sent, 1)]
    attended = finish(own, level, received, w_out, cores)
    return features.reshape(latent.shape), attended.reshape(latent.shape)


def solution(mesh):
    tiled = P(("group", "image"), "prow", "pcol", None)
    return jax.shard_map(
        shards,
        mesh=mesh,
        in_specs=(tiled, P(), P(), P(), P(), P(), P("group"), P("group", None), P("group")),
        out_specs=(tiled, tiled),
        check_vma=False,
    )
```

```python
import functools

import jax
import jax.numpy as jnp
from jax import lax
from jax.experimental import pallas as pl
from jax.experimental.pallas import tpu as pltpu
from jax.sharding import PartitionSpec as P

HEAD_DIM = 64
BLOCK = 128
NSEL = 4
LANES = 128
SUBLANES = 8
ONES = 16
F32 = jnp.float32
BF16 = jnp.bfloat16
MIB = 1 << 20


VMEM = pl.BlockSpec(memory_space=pltpu.VMEM)
SMEM = pl.BlockSpec(memory_space=pltpu.SMEM)
ANY = pl.BlockSpec(memory_space=pl.ANY)


def shape(*dims, dtype=BF16):
    return jax.ShapeDtypeStruct(dims, dtype)


def cost(flops, moved, exps=0):
    return pl.CostEstimate(flops=flops, bytes_accessed=moved, transcendentals=exps)


def grant(mib):
    return pltpu.CompilerParams(vmem_limit_bytes=mib * MIB)


def source_of(index, step, count):
    if count & (count - 1) == 0:
        return index ^ step
    return lax.rem(index + step, count) if not isinstance(index, int) else (index + step) % count


def step_of(index, source, count):
    if count & (count - 1) == 0:
        return index ^ source
    return lax.rem(source - index + count, count)


def exchange(block, axis, step):
    count = lax.axis_size(axis)
    return lax.ppermute(block, axis, [(source_of(i, step, count), i) for i in range(count)])


def shifted(block, axis, step):
    count = lax.axis_size(axis)
    return lax.ppermute(block, axis, [((i + step) % count, i) for i in range(count)])


def halo(cells):
    core, cores = lax.axis_index("pcol"), lax.axis_size("pcol")
    rows, cols = lax.axis_size("prow"), cells.shape[1]
    if cores == 2:
        inner = lax.dynamic_index_in_dim(cells, jnp.where(core == 0, cols - 1, 0), 1, keepdims=False)
        other = shifted(inner, "pcol", 1)
        zero = jnp.zeros_like(other)
        left = jnp.where(core == 1, other, zero)
        right = jnp.where(core == 0, other, zero)
    else:
        left = lax.ppermute(cells[:, -1], "pcol", [(i, i + 1) for i in range(cores - 1)])
        right = lax.ppermute(cells[:, 0], "pcol", [(i + 1, i) for i in range(cores - 1)])
    low = jnp.concatenate([cells[-1], left[-1:], right[-1:]], axis=0)
    high = jnp.concatenate([cells[0], left[:1], right[:1]], axis=0)
    odd = lax.rem(lax.axis_index("prow"), 2) == 1
    swaps = []
    for first in range(2):
        pairs = [(i, i + 1) for i in range(first, rows - 1, 2)]
        block = jnp.where(odd, high, low) if first == 0 else jnp.where(odd, low, high)
        swaps.append(lax.ppermute(block, "prow", pairs + [(j, i) for i, j in pairs]))
    above = jnp.where(odd, swaps[0], swaps[1])
    below = jnp.where(odd, swaps[1], swaps[0])
    return left, right, above, below


def stage_kernel(*refs):
    count = len(refs) // 2
    copies = [
        pltpu.make_async_copy(refs[n], refs[count + n], refs[-1].at[n]) for n in range(count)
    ]
    for copy in copies:
        copy.start()
    for copy in copies:
        copy.wait()


def stage(*arrays):
    return pl.pallas_call(
        stage_kernel,
        out_shape=tuple(shape(*a.shape, dtype=a.dtype) for a in arrays),
        in_specs=[ANY] * len(arrays),
        out_specs=(VMEM,) * len(arrays),
        scratch_shapes=[pltpu.SemaphoreType.DMA((len(arrays),))],
        compiler_params=grant(16),
        cost_estimate=cost(0, 2 * sum(a.nbytes for a in arrays)),
        name="stage",
    )(*arrays)


def conv_kernel(rows, cols, cores, x_ref, left_ref, right_ref, above_ref, below_ref, w_ref, *refs):
    features_ref, *half_refs, shift0, shift1, shift2 = refs

    def silu(v):
        v = v.astype(F32)
        return (v / (1.0 + jnp.exp(-v))).astype(BF16).astype(F32)

    side = lax.broadcasted_iota(jnp.int32, (cols, x_ref.shape[1]), 0)
    for r in range(rows + 2):
        if r == 0 or r == rows + 1:
            ref = above_ref if r == 0 else below_ref
            cells, lcell, rcell = ref[:cols], ref[cols:cols + 1], ref[cols + 1:cols + 2]
        else:
            cells = x_ref[(r - 1) * cols:r * cols]
            lcell, rcell = left_ref[r - 1:r], right_ref[r - 1:r]
        cells, lcell, rcell = silu(cells), silu(lcell), silu(rcell)
        at = slice(r * cols, (r + 1) * cols)
        shift1[at] = cells.astype(BF16)
        shift0[at] = jnp.where(side == 0, lcell, pltpu.roll(cells, 1, 0)).astype(BF16)
        shift2[at] = jnp.where(side == cols - 1, rcell, pltpu.roll(cells, cols - 1, 0)).astype(BF16)
    total = x_ref[...].astype(F32)
    for a in range(3):
        for b, shift in enumerate((shift0, shift1, shift2)):
            total = total + jnp.dot(
                shift[a * cols:(a + rows) * cols], w_ref[a, b], preferred_element_type=F32
            )
    features = total.astype(BF16)
    features_ref[...] = features
    values = features.astype(F32)
    centered = values - jnp.mean(values, axis=-1, keepdims=True)
    spread = jnp.mean(centered * centered, axis=-1, keepdims=True)
    normed = (centered * lax.rsqrt(spread + 1e-05)).astype(BF16)
    core = lax.axis_index("pcol")
    per = BLOCK // cores
    for b in range(rows * cols // BLOCK):
        for h in range(cores):
            rows_of = normed[b * BLOCK + h * per:b * BLOCK + (h + 1) * per]
            for s, ref in enumerate(half_refs):
                @pl.when(lax.rem(core + s, cores) == h)
                def _():
                    ref[b * per:(b + 1) * per] = rows_of


def conv_norm(cells, sides, conv_weight, cores):
    rows, cols, channels = cells.shape
    tokens = rows * cols
    return pl.pallas_call(
        functools.partial(conv_kernel, rows, cols, cores),
        out_shape=(shape(tokens, channels),) + (shape(tokens // cores, channels),) * cores,
        in_specs=[VMEM] * 6,
        out_specs=(VMEM,) * (1 + cores),
        scratch_shapes=[pltpu.VMEM(((rows + 2) * cols, channels), BF16)] * 3,
        compiler_params=grant(24),
        cost_estimate=cost(18 * tokens * channels**2, 18 * channels**2, tokens * channels),
        name="conv_norm",
    )(cells.reshape(tokens, channels), *sides, conv_weight)


class Table:
    def __init__(self, ref, anchors, images):
        self.ref, self.anchors, self.images = ref, anchors, images
        self.every_image = anchors == images

    @staticmethod
    def build(anchor_index, block_count, order):
        return jnp.concatenate([anchor_index, block_count, order.reshape(-1)])

    def anchor_at(self, image):
        found = jnp.int32(0)
        for a in range(1, self.anchors):
            found = jnp.where(self.ref[a] == image, a, found)
        return found

    def count(self, anchor):
        return self.ref[self.anchors + anchor]

    def block(self, anchor, slot):
        return self.ref[2 * self.anchors + anchor * NSEL + slot]

    def own_times(self, step, group, cores, prows, per_patch):
        if not self.every_image:
            return jnp.float32(1.0)
        s, b = divmod(group, per_patch)
        patch = source_of(lax.axis_index("prow"), step, prows) * cores
        block = (patch + lax.rem(lax.axis_index("pcol") + s, cores)) * per_patch + b
        anchor = self.anchor_at(lax.axis_index("image"))
        times = jnp.float32(1.0)
        for slot in range(NSEL):
            hit = (slot < self.count(anchor)) & (self.block(anchor, slot) == block)
            times = jnp.where(hit, 2.0, times)
        return times

    def anchor_times(self, source, slot):
        if self.every_image:
            image = source_of(lax.axis_index("image"), source + 1, self.images)
            source = self.anchor_at(image)
        return jnp.where(slot < self.count(source), 1.0, 0.0).astype(F32)


def project(normed, times, wk_ref, wvt_ref, k_scr, v_scr):
    keys, channels = normed.shape
    k = jnp.dot(normed, wk_ref[...], preferred_element_type=F32).astype(BF16)
    for pair in range(channels // LANES):
        k_scr[pair] = k[:, pair * LANES:(pair + 1) * LANES]
    v = lax.dot_general(
        wvt_ref[...], normed, (((1,), (1,)), ((), ())), preferred_element_type=F32
    )
    per = keys // len(times)
    lane = lax.broadcasted_iota(jnp.int32, (1, keys), 1)
    mult = jnp.full((1, keys), times[0], F32)
    for g in range(1, len(times)):
        mult = jnp.where(lane >= g * per, times[g], mult)
    v = (v * mult).astype(BF16)
    ones = jnp.broadcast_to(mult, (ONES, keys)).astype(BF16)
    for head in range(channels // HEAD_DIM):
        v_scr[head, :HEAD_DIM] = v[head * HEAD_DIM:(head + 1) * HEAD_DIM]
        v_scr[head, HEAD_DIM:] = ones


def attend_heads(q_ref, k_scr, v_scr, out_ref, level_ref, width):
    zeros = jnp.zeros((HEAD_DIM, width), BF16)
    items = [
        (head, slice(at, at + width))
        for head in range(q_ref.shape[0] // HEAD_DIM)
        for at in range(0, q_ref.shape[1], width)
    ]

    def scores_of(head, cols):
        q = q_ref[head * HEAD_DIM:(head + 1) * HEAD_DIM, cols]
        q = jnp.concatenate([q, zeros] if head % 2 == 0 else [zeros, q], axis=0)
        return jnp.dot(k_scr[head // 2], q, preferred_element_type=F32)

    ahead = scores_of(*items[0])
    for n, (head, cols) in enumerate(items):
        scores = ahead
        if n + 1 < len(items):
            ahead = scores_of(*items[n + 1])
        peak = jnp.max(scores, axis=0, keepdims=True)
        probs = jnp.exp(scores - peak).astype(BF16)
        value = jnp.dot(v_scr[head], probs, preferred_element_type=F32)
        total = value[HEAD_DIM:HEAD_DIM + 1]
        out_ref[head * HEAD_DIM:(head + 1) * HEAD_DIM, cols] = (
            value[:HEAD_DIM] * (1.0 / total)
        ).astype(out_ref.dtype)
        level_ref[head, :, cols] = jnp.broadcast_to(peak + jnp.log(total), (SUBLANES, width))


def own_kernel(info, n_parts, table_ref, *refs):
    anchors, images, cores, prows, per_patch = info
    part_refs, key_ref = refs[:n_parts], refs[n_parts]
    wq_ref, wk_ref, wv_ref, q_ref, out_ref, level_ref, k_scr, v_scr = refs[n_parts + 1:]
    table = Table(table_ref, anchors, images)
    at = 0
    for ref in part_refs:
        q = lax.dot_general(
            wq_ref[...], ref[...], (((1,), (1,)), ((), ())), preferred_element_type=F32
        ).astype(BF16)
        q_ref[:, at:at + ref.shape[0]] = (q.astype(F32) * HEAD_DIM ** (-0.5)).astype(BF16)
        at += ref.shape[0]
    times = [table.own_times(0, g, cores, prows, per_patch) for g in range(cores * per_patch)]
    project(key_ref[...], times, wk_ref, wv_ref, k_scr, v_scr)
    attend_heads(q_ref, k_scr, v_scr, out_ref, level_ref, part_refs[0].shape[0] * cores)


def key_scratch(keys, channels):
    return [
        pltpu.VMEM((channels // LANES, keys, LANES), BF16),
        pltpu.VMEM((channels // HEAD_DIM, HEAD_DIM + ONES, keys), BF16),
    ]


def attend_cost(rows, keys, channels, extra=0):
    return cost(
        4 * keys * channels**2 + 16 * rows * keys * channels + extra,
        2 * channels * (2 * rows + keys),
        rows * keys * channels // HEAD_DIM,
    )


def attend_own(info, table, parts, key, w_query, w_key, w_value):
    size, channels = key.shape
    rows = sum(part.shape[0] for part in parts)
    return pl.pallas_call(
        functools.partial(own_kernel, info, len(parts)),
        out_shape=(
            shape(channels, rows), shape(channels, rows),
            shape(channels // HEAD_DIM, SUBLANES, rows, dtype=F32),
        ),
        in_specs=[SMEM] + [VMEM] * (len(parts) + 4),
        out_specs=(VMEM,) * 3,
        scratch_shapes=key_scratch(size, channels),
        compiler_params=grant(24),
        cost_estimate=attend_cost(rows, size, channels, 2 * rows * channels**2),
        name="attend_own",
    )(table, *parts, key, w_query, w_key, w_value)


def plane_kernel(info, tiles, table_ref, q_ref, *refs):
    anchors, images, cores, prows, per_patch = info
    key_refs = refs[:tiles]
    wk_ref, wv_ref, out_ref, level_ref, k_scr, v_scr = refs[tiles:]
    table = Table(table_ref, anchors, images)
    times = [
        table.own_times(t + 1, g, cores, prows, per_patch)
        for t in range(tiles) for g in range(cores * per_patch)
    ]
    normed = jnp.concatenate([ref[...] for ref in key_refs], axis=0)
    project(normed, times, wk_ref, wv_ref, k_scr, v_scr)
    attend_heads(q_ref, k_scr, v_scr, out_ref, level_ref, q_ref.shape[1] // cores)


def attend_plane(info, table, queries, keys, w_key, w_value):
    size, channels = keys[0].shape
    rows = queries.shape[1]
    return pl.pallas_call(
        functools.partial(plane_kernel, info, len(keys)),
        out_shape=(
            shape(channels, rows), shape(channels // HEAD_DIM, SUBLANES, rows, dtype=F32),
        ),
        in_specs=[SMEM] + [VMEM] * (len(keys) + 3),
        out_specs=(VMEM,) * 2,
        scratch_shapes=key_scratch(size * len(keys), channels),
        compiler_params=grant(24),
        cost_estimate=attend_cost(rows, size * len(keys), channels),
        name="attend_plane",
    )(table, queries, *keys, w_key, w_value)


def merge_head(parts, head, cols):
    rows = slice(head * HEAD_DIM, (head + 1) * HEAD_DIM)
    levels = [level(head, cols) for _, level in parts]
    peak = functools.reduce(jnp.maximum, levels)
    weights = [jnp.exp(level - peak) for level in levels]
    total = functools.reduce(jnp.add, weights)
    value = functools.reduce(
        jnp.add, [w * ref[rows, cols].astype(F32) for w, (ref, _) in zip(weights, parts)]
    )
    return value * (1.0 / total), peak + jnp.log(total)


def anchor_kernel(info, tiles, earlier, groups, table_ref, q_ref, *refs):
    anchors, images, cores, prows, per_patch = info
    key_refs, refs = refs[:tiles], refs[tiles:]
    early_refs, refs = refs[:2 * earlier], refs[2 * earlier:]
    wk_ref, wv_ref, *out_refs = refs[:2 + groups + 1]
    out_scr, level_scr, k_scr, v_scr = refs[3 + groups:]
    own_ref, own_level_ref, *sent_refs = out_refs
    table = Table(table_ref, anchors, images)
    if table.every_image:
        each = NSEL // prows
        times = [
            table.anchor_times(s, source_of(lax.axis_index("prow"), t, prows) * each + slot)
            for t in range(tiles) for s in range(images - 1) for slot in range(each)
        ]
    else:
        times = [table.anchor_times(t, slot) for t in range(tiles) for slot in range(NSEL)]
    normed = jnp.concatenate([ref[...] for ref in key_refs], axis=0)
    project(normed, times, wk_ref, wv_ref, k_scr, v_scr)
    channels = q_ref.shape[0]
    width = q_ref.shape[1] // groups
    attend_heads(q_ref, k_scr, v_scr, out_scr, level_scr, width)
    pairs = list(zip(early_refs[::2], early_refs[1::2])) + [(out_scr, level_scr)]
    parts = [
        (ref, lambda head, cols, level=level: level[head, 0:1, cols]) for ref, level in pairs
    ]
    heads = channels // HEAD_DIM
    row = lax.broadcasted_iota(jnp.int32, (2 * SUBLANES, width), 0)
    for n in range(groups):
        cols = slice(n * width, (n + 1) * width)
        ref = own_ref if n == 0 else sent_refs[n - 1]
        levels = jnp.zeros((2 * SUBLANES, width), F32)
        for head in range(heads):
            value, level = merge_head(parts, head, cols)
            ref[head * HEAD_DIM:(head + 1) * HEAD_DIM] = value.astype(BF16)
            levels = jnp.where(row == head, level, levels)
        if n == 0:
            own_level_ref[...] = levels
        else:
            for term in range(3):
                high = levels.astype(BF16)
                at = channels + term * 2 * SUBLANES
                ref[at:at + 2 * SUBLANES] = high
                levels = levels - high.astype(F32)


def attend_anchors(info, table, queries, keys, earlier, w_key, w_value, groups):
    size, channels = keys[0].shape
    rows = queries.shape[1]
    width = rows // groups
    flat = [leaf for part in earlier for leaf in part]
    heads = channels // HEAD_DIM
    return pl.pallas_call(
        functools.partial(anchor_kernel, info, len(keys), len(earlier), groups),
        out_shape=(shape(channels, width), shape(2 * SUBLANES, width, dtype=F32))
        + (shape(channels + 6 * SUBLANES, width),) * (groups - 1),
        in_specs=[SMEM] + [VMEM] * (len(keys) + len(flat) + 3),
        out_specs=(VMEM,) * (1 + groups),
        scratch_shapes=[
            pltpu.VMEM((channels, rows), BF16), pltpu.VMEM((heads, SUBLANES, rows), F32),
        ] + key_scratch(size * len(keys), channels),
        compiler_params=grant(24),
        cost_estimate=attend_cost(rows, size * len(keys), channels),
        name="attend_anchors",
    )(table, queries, *keys, *flat, w_key, w_value)


def finish_kernel(cores, own_ref, level_ref, *refs):
    *received, w_ref, out_ref, merged = refs
    channels, tokens = own_ref.shape

    def row_of(ref, base, terms):
        def level(head, cols):
            return functools.reduce(jnp.add, [
                ref[base + t * 2 * SUBLANES:base + (t + 1) * 2 * SUBLANES].astype(F32)
                for t in range(terms)
            ])[head:head + 1]
        return level

    parts = [(own_ref, row_of(level_ref, 0, 1))]
    parts += [(ref, row_of(ref, channels, 3)) for ref in received]
    every = slice(0, tokens)
    for head in range(channels // HEAD_DIM):
        value, _ = merge_head(parts, head, every)
        merged[head * HEAD_DIM:(head + 1) * HEAD_DIM] = value.astype(BF16)
    out = lax.dot_general(
        merged[...], w_ref[...], (((0,), (0,)), ((), ())), preferred_element_type=F32
    ).astype(BF16)
    core = lax.axis_index("pcol")
    per = BLOCK // cores
    blocks = tokens // BLOCK
    for s in range(cores):
        for b in range(blocks):
            at = b * BLOCK + lax.rem(core + s, cores) * per
            out_ref[pl.ds(pl.multiple_of(at, per), per)] = out[
                (s * blocks + b) * per:(s * blocks + b + 1) * per
            ]


def finish(own, level, received, w_out, cores):
    channels, tokens = own.shape
    return pl.pallas_call(
        functools.partial(finish_kernel, cores),
        out_shape=shape(tokens, channels),
        in_specs=[VMEM] * (3 + len(received)),
        out_specs=VMEM,
        scratch_shapes=[pltpu.VMEM((channels, tokens), BF16)],
        compiler_params=grant(16),
        cost_estimate=cost(2 * tokens * channels**2, 2 * channels * (channels + 3 * tokens)),
        name="finish",
    )(own, level, *received, w_out)


def pick_kernel(info, anchor, table_ref, *refs):
    anchors, images, cores, prows, per_patch = info
    *sources, out_ref = refs
    table = Table(table_ref, anchors, images)
    core, prow = lax.axis_index("pcol"), lax.axis_index("prow")
    if anchor is None:
        anchor = table.anchor_at(lax.axis_index("image"))
    per = BLOCK // cores
    for n_slot in range(NSEL // prows):
        slot = prow * (NSEL // prows) + n_slot
        block = table.block(anchor, jnp.where(slot < table.count(anchor), slot, 0))
        patch, inner = lax.div(block, per_patch), lax.rem(block, per_patch)
        held = step_of(prow, lax.div(patch, cores), prows)
        part = lax.rem(lax.rem(patch, cores) - core + cores, cores)
        at = pl.multiple_of((part * per_patch + inner) * per, per)
        for n, ref in enumerate(sources):
            @pl.when(held == n)
            def _():
                out_ref[n_slot * per:(n_slot + 1) * per] = ref[pl.ds(at, per)]


def pick(info, anchor, table, sources):
    channels = sources[0].shape[1]
    rows = NSEL // info[3] * (BLOCK // info[2])
    return pl.pallas_call(
        functools.partial(pick_kernel, info, anchor),
        out_shape=shape(rows, channels),
        in_specs=[SMEM] + [VMEM] * len(sources),
        out_specs=VMEM,
        compiler_params=grant(8),
        name="pick",
    )(table, *sources)


def shards(
    latent, conv_weight, w_query, w_key, w_value, w_out, anchor_index, block_order, block_count
):
    tile_rows, tile_cols, channels = latent.shape[1:]
    cores, prows, images = (lax.axis_size(a) for a in ("pcol", "prow", "image"))
    image = lax.axis_index("image")
    anchors = anchor_index.shape[0]
    per_patch = tile_rows * tile_cols // BLOCK
    info = (anchors, images, cores, prows, per_patch)
    table = Table.build(anchor_index, block_count, block_order[:, :NSEL])
    wq, wv = w_query.T, w_value.T

    (staged,) = stage(conv_weight)
    features, *parts = conv_norm(latent[0], halo(latent[0]), staged, cores)
    keys, queries = [parts[0]], list(parts)
    for s in range(1, cores):
        theirs = [None] * cores
        for t in [cores - s] + [t for t in range(cores) if t != cores - s]:
            theirs[t] = shifted(parts[t], "pcol", s)
        keys.append(theirs[cores - s])
        queries += theirs
    key = jnp.concatenate(keys, axis=0)
    plane = [exchange(key, "prow", s) for s in range(1, prows)]
    q, value, level = attend_own(info, table, queries, key, wq, w_key, wv)
    done = [(value, level)]

    if anchors == images:
        share = pick(info, None, table, [key] + plane)
        local = jnp.concatenate([exchange(share, "image", s) for s in range(1, images)], axis=0)
        sources = [local] + [exchange(local, "prow", s) for s in range(1, prows)]
    else:
        received = []
        for anchor in range(anchors):
            share = pick(info, anchor, table, [key] + plane)
            share = jnp.where(image == anchor_index[anchor], share, jnp.zeros_like(share))
            received.append(lax.psum(share, "image"))
        joined = lax.all_gather(jnp.stack(received), "prow", axis=1, tiled=True)
        sources = [joined[anchor] for anchor in range(anchors)]
    if plane:
        done.append(attend_plane(info, table, q, plane, w_key, wv))
    own, level, *sent = attend_anchors(info, table, q, sources, done, w_key, wv, cores)
    received = [shifted(block, "pcol", cores - s) for s, block in enumerate(sent, 1)]
    attended = finish(own, level, received, w_out, cores)
    return features.reshape(latent.shape), attended.reshape(latent.shape)


def solution(mesh):
    tiled = P(("group", "image"), "prow", "pcol", None)
    return jax.shard_map(
        shards,
        mesh=mesh,
        in_specs=(tiled, P(), P(), P(), P(), P(), P("group"), P("group", None), P("group")),
        out_specs=(tiled, tiled),
        check_vma=False,
    )
```

```python
import functools

import jax
import jax.numpy as jnp
from jax import lax
from jax.experimental import pallas as pl
from jax.experimental.pallas import tpu as pltpu
from jax.sharding import PartitionSpec as P

HEAD_DIM = 64
BLOCK = 128
NSEL = 4
LANES = 128
SUBLANES = 8
ONES = 16
F32 = jnp.float32
BF16 = jnp.bfloat16
MIB = 1 << 20


VMEM = pl.BlockSpec(memory_space=pltpu.VMEM)
SMEM = pl.BlockSpec(memory_space=pltpu.SMEM)
HBM = pl.BlockSpec(memory_space=pltpu.HBM)


def shape(*dims, dtype=BF16):
    return jax.ShapeDtypeStruct(dims, dtype)


def cost(flops, moved, exps=0):
    return pl.CostEstimate(flops=flops, bytes_accessed=moved, transcendentals=exps)


def grant(mib):
    return pltpu.CompilerParams(vmem_limit_bytes=mib * MIB)


def source_of(index, step, count):
    if count & (count - 1) == 0:
        return index ^ step
    return lax.rem(index + step, count) if not isinstance(index, int) else (index + step) % count


def target_of(index, step, count):
    if count & (count - 1) == 0:
        return index ^ step
    return lax.rem(index - step + count, count)


def step_of(index, source, count):
    if count & (count - 1) == 0:
        return index ^ source
    return lax.rem(source - index + count, count)


def exchange(block, axis, step):
    count = lax.axis_size(axis)
    return lax.ppermute(block, axis, [(source_of(i, step, count), i) for i in range(count)])


def shifted(block, axis, step):
    count = lax.axis_size(axis)
    return lax.ppermute(block, axis, [((i + step) % count, i) for i in range(count)])


def halo(cells):
    core, cores = lax.axis_index("pcol"), lax.axis_size("pcol")
    rows, cols = lax.axis_size("prow"), cells.shape[1]
    if cores == 2:
        inner = lax.dynamic_index_in_dim(cells, jnp.where(core == 0, cols - 1, 0), 1, keepdims=False)
        other = shifted(inner, "pcol", 1)
        zero = jnp.zeros_like(other)
        left = jnp.where(core == 1, other, zero)
        right = jnp.where(core == 0, other, zero)
    else:
        left = lax.ppermute(cells[:, -1], "pcol", [(i, i + 1) for i in range(cores - 1)])
        right = lax.ppermute(cells[:, 0], "pcol", [(i + 1, i) for i in range(cores - 1)])
    low = jnp.concatenate([cells[-1], left[-1:], right[-1:]], axis=0)
    high = jnp.concatenate([cells[0], left[:1], right[:1]], axis=0)
    odd = lax.rem(lax.axis_index("prow"), 2) == 1
    swaps = []
    for first in range(2):
        pairs = [(i, i + 1) for i in range(first, rows - 1, 2)]
        block = jnp.where(odd, high, low) if first == 0 else jnp.where(odd, low, high)
        swaps.append(lax.ppermute(block, "prow", pairs + [(j, i) for i, j in pairs]))
    above = jnp.where(odd, swaps[0], swaps[1])
    below = jnp.where(odd, swaps[1], swaps[0])
    return left, right, above, below


def conv_kernel(rows, cols, cores, x_ref, left_ref, right_ref, above_ref, below_ref, w_ref, *refs):
    features_ref, *half_refs, shift0, shift1, shift2, taps, sem = refs
    copies = [
        pltpu.make_async_copy(w_ref.at[n // 3, n % 3], taps.at[n], sem.at[n]) for n in range(9)
    ]
    for copy in copies:
        copy.start()

    def silu(v):
        v = v.astype(F32)
        return (v / (1.0 + jnp.exp(-v))).astype(BF16).astype(F32)

    side = lax.broadcasted_iota(jnp.int32, (cols, x_ref.shape[1]), 0)
    for r in range(rows + 2):
        if r == 0 or r == rows + 1:
            ref = above_ref if r == 0 else below_ref
            cells, lcell, rcell = ref[:cols], ref[cols:cols + 1], ref[cols + 1:cols + 2]
        else:
            cells = x_ref[(r - 1) * cols:r * cols]
            lcell, rcell = left_ref[r - 1:r], right_ref[r - 1:r]
        cells, lcell, rcell = silu(cells), silu(lcell), silu(rcell)
        at = slice(r * cols, (r + 1) * cols)
        shift1[at] = cells.astype(BF16)
        shift0[at] = jnp.where(side == 0, lcell, pltpu.roll(cells, 1, 0)).astype(BF16)
        shift2[at] = jnp.where(side == cols - 1, rcell, pltpu.roll(cells, cols - 1, 0)).astype(BF16)
    total = x_ref[...].astype(F32)
    for a in range(3):
        for b, shift in enumerate((shift0, shift1, shift2)):
            copies[3 * a + b].wait()
            total = total + jnp.dot(
                shift[a * cols:(a + rows) * cols], taps[3 * a + b], preferred_element_type=F32
            )
    features = total.astype(BF16)
    features_ref[...] = features
    values = features.astype(F32)
    centered = values - jnp.mean(values, axis=-1, keepdims=True)
    spread = jnp.mean(centered * centered, axis=-1, keepdims=True)
    normed = (centered * lax.rsqrt(spread + 1e-05)).astype(BF16)
    core = lax.axis_index("pcol")
    per = BLOCK // cores
    for b in range(rows * cols // BLOCK):
        for h in range(cores):
            rows_of = normed[b * BLOCK + h * per:b * BLOCK + (h + 1) * per]
            for s, ref in enumerate(half_refs):
                @pl.when(lax.rem(core + s, cores) == h)
                def _():
                    ref[b * per:(b + 1) * per] = rows_of


def conv_norm(cells, sides, conv_weight, cores):
    rows, cols, channels = cells.shape
    tokens = rows * cols
    return pl.pallas_call(
        functools.partial(conv_kernel, rows, cols, cores),
        out_shape=(shape(tokens, channels),) + (shape(tokens // cores, channels),) * cores,
        in_specs=[VMEM] * 5 + [HBM],
        out_specs=(VMEM,) * (1 + cores),
        scratch_shapes=[pltpu.VMEM(((rows + 2) * cols, channels), BF16)] * 3 + [
            pltpu.VMEM((9, channels, channels), BF16), pltpu.SemaphoreType.DMA((9,)),
        ],
        compiler_params=grant(58),
        cost_estimate=cost(18 * tokens * channels**2, 18 * channels**2, tokens * channels),
        name="conv_norm",
    )(cells.reshape(tokens, channels), *sides, conv_weight)


class Table:
    def __init__(self, ref, anchors, images):
        self.ref, self.anchors, self.images = ref, anchors, images
        self.every_image = anchors == images

    @staticmethod
    def build(anchor_index, block_count, order):
        return jnp.concatenate([anchor_index, block_count, order.reshape(-1)])

    def anchor_at(self, image):
        found = jnp.int32(0)
        for a in range(1, self.anchors):
            found = jnp.where(self.ref[a] == image, a, found)
        return found

    def count(self, anchor):
        return self.ref[self.anchors + anchor]

    def block(self, anchor, slot):
        return self.ref[2 * self.anchors + anchor * NSEL + slot]

    def own_times(self, step, group, cores, prows, per_patch):
        if not self.every_image:
            return jnp.float32(1.0)
        s, b = divmod(group, per_patch)
        patch = source_of(lax.axis_index("prow"), step, prows) * cores
        block = (patch + lax.rem(lax.axis_index("pcol") + s, cores)) * per_patch + b
        anchor = self.anchor_at(lax.axis_index("image"))
        times = jnp.float32(1.0)
        for slot in range(NSEL):
            hit = (slot < self.count(anchor)) & (self.block(anchor, slot) == block)
            times = jnp.where(hit, 2.0, times)
        return times

    def anchor_times(self, source, slot):
        if self.every_image:
            image = source_of(lax.axis_index("image"), source + 1, self.images)
            source = self.anchor_at(image)
        return jnp.where(slot < self.count(source), 1.0, 0.0).astype(F32)


def project(normed, times, wk_ref, wvt_ref, k_scr, v_scr):
    keys, channels = normed.shape
    k = jnp.dot(normed, wk_ref[...], preferred_element_type=F32).astype(BF16)
    for pair in range(channels // LANES):
        k_scr[pair] = k[:, pair * LANES:(pair + 1) * LANES]
    v = lax.dot_general(
        wvt_ref[...], normed, (((1,), (1,)), ((), ())), preferred_element_type=F32
    )
    per = keys // len(times)
    lane = lax.broadcasted_iota(jnp.int32, (1, keys), 1)
    mult = jnp.full((1, keys), times[0], F32)
    for g in range(1, len(times)):
        mult = jnp.where(lane >= g * per, times[g], mult)
    v = (v * mult).astype(BF16)
    ones = jnp.broadcast_to(mult, (ONES, keys)).astype(BF16)
    for head in range(channels // HEAD_DIM):
        v_scr[head, :HEAD_DIM] = v[head * HEAD_DIM:(head + 1) * HEAD_DIM]
        v_scr[head, HEAD_DIM:] = ones


def attend_heads(q_ref, k_scr, v_scr, out_ref, level_ref, width):
    zeros = jnp.zeros((HEAD_DIM, width), BF16)
    items = [
        (head, slice(at, at + width))
        for head in range(q_ref.shape[0] // HEAD_DIM)
        for at in range(0, q_ref.shape[1], width)
    ]

    def scores_of(head, cols):
        q = q_ref[head * HEAD_DIM:(head + 1) * HEAD_DIM, cols]
        q = jnp.concatenate([q, zeros] if head % 2 == 0 else [zeros, q], axis=0)
        return jnp.dot(k_scr[head // 2], q, preferred_element_type=F32)

    ahead = scores_of(*items[0])
    for n, (head, cols) in enumerate(items):
        scores = ahead
        if n + 1 < len(items):
            ahead = scores_of(*items[n + 1])
        peak = jnp.max(scores, axis=0, keepdims=True)
        probs = jnp.exp(scores - peak).astype(BF16)
        value = jnp.dot(v_scr[head], probs, preferred_element_type=F32)
        total = value[HEAD_DIM:HEAD_DIM + 1]
        out_ref[head * HEAD_DIM:(head + 1) * HEAD_DIM, cols] = (
            value[:HEAD_DIM] * (1.0 / total)
        ).astype(out_ref.dtype)
        level_ref[head, :, cols] = jnp.broadcast_to(peak + jnp.log(total), (SUBLANES, width))


def own_kernel(info, n_parts, table_ref, *refs):
    anchors, images, cores, prows, per_patch = info
    part_refs, key_ref = refs[:n_parts], refs[n_parts]
    wq_ref, wk_ref, wv_ref, q_ref, out_ref, level_ref, k_scr, v_scr = refs[n_parts + 1:]
    table = Table(table_ref, anchors, images)
    at = 0
    for ref in part_refs:
        q = lax.dot_general(
            wq_ref[...], ref[...], (((1,), (1,)), ((), ())), preferred_element_type=F32
        ).astype(BF16)
        q_ref[:, at:at + ref.shape[0]] = (q.astype(F32) * HEAD_DIM ** (-0.5)).astype(BF16)
        at += ref.shape[0]
    times = [table.own_times(0, g, cores, prows, per_patch) for g in range(cores * per_patch)]
    project(key_ref[...], times, wk_ref, wv_ref, k_scr, v_scr)
    attend_heads(q_ref, k_scr, v_scr, out_ref, level_ref, part_refs[0].shape[0] * cores)


def key_scratch(keys, channels):
    return [
        pltpu.VMEM((channels // LANES, keys, LANES), BF16),
        pltpu.VMEM((channels // HEAD_DIM, HEAD_DIM + ONES, keys), BF16),
    ]


def attend_cost(rows, keys, channels, extra=0):
    return cost(
        4 * keys * channels**2 + 16 * rows * keys * channels + extra,
        2 * channels * (2 * rows + keys),
        rows * keys * channels // HEAD_DIM,
    )


def attend_own(info, table, parts, key, w_query, w_key, w_value):
    size, channels = key.shape
    rows = sum(part.shape[0] for part in parts)
    return pl.pallas_call(
        functools.partial(own_kernel, info, len(parts)),
        out_shape=(
            shape(channels, rows), shape(channels, rows),
            shape(channels // HEAD_DIM, SUBLANES, rows, dtype=F32),
        ),
        in_specs=[SMEM] + [VMEM] * (len(parts) + 4),
        out_specs=(VMEM,) * 3,
        scratch_shapes=key_scratch(size, channels),
        compiler_params=grant(24),
        cost_estimate=attend_cost(rows, size, channels, 2 * rows * channels**2),
        name="attend_own",
    )(table, *parts, key, w_query, w_key, w_value)


def plane_kernel(info, tiles, table_ref, q_ref, *refs):
    anchors, images, cores, prows, per_patch = info
    key_refs = refs[:tiles]
    wk_ref, wv_ref, out_ref, level_ref, k_scr, v_scr = refs[tiles:]
    table = Table(table_ref, anchors, images)
    times = [
        table.own_times(t + 1, g, cores, prows, per_patch)
        for t in range(tiles) for g in range(cores * per_patch)
    ]
    normed = jnp.concatenate([ref[...] for ref in key_refs], axis=0)
    project(normed, times, wk_ref, wv_ref, k_scr, v_scr)
    attend_heads(q_ref, k_scr, v_scr, out_ref, level_ref, q_ref.shape[1] // cores)


def attend_plane(info, table, queries, keys, w_key, w_value):
    size, channels = keys[0].shape
    rows = queries.shape[1]
    return pl.pallas_call(
        functools.partial(plane_kernel, info, len(keys)),
        out_shape=(
            shape(channels, rows), shape(channels // HEAD_DIM, SUBLANES, rows, dtype=F32),
        ),
        in_specs=[SMEM] + [VMEM] * (len(keys) + 3),
        out_specs=(VMEM,) * 2,
        scratch_shapes=key_scratch(size * len(keys), channels),
        compiler_params=grant(24),
        cost_estimate=attend_cost(rows, size * len(keys), channels),
        name="attend_plane",
    )(table, queries, *keys, w_key, w_value)


def merge_head(parts, head, cols):
    rows = slice(head * HEAD_DIM, (head + 1) * HEAD_DIM)
    levels = [level(head, cols) for _, level in parts]
    peak = functools.reduce(jnp.maximum, levels)
    weights = [jnp.exp(level - peak) for level in levels]
    total = functools.reduce(jnp.add, weights)
    value = functools.reduce(
        jnp.add, [w * ref[rows, cols].astype(F32) for w, (ref, _) in zip(weights, parts)]
    )
    return value * (1.0 / total), peak + jnp.log(total)


def anchor_kernel(info, tiles, earlier, groups, table_ref, q_ref, *refs):
    anchors, images, _, prows, _ = info
    key_refs, refs = refs[:tiles], refs[tiles:]
    early_refs, refs = refs[:2 * earlier], refs[2 * earlier:]
    wk_ref, wv_ref, *out_refs = refs[:2 + groups + 1]
    out_scr, level_scr, k_scr, v_scr = refs[3 + groups:]
    own_ref, own_level_ref, *sent_refs = out_refs
    table = Table(table_ref, anchors, images)
    if table.every_image:
        each = NSEL // prows
        times = [
            table.anchor_times(s, source_of(lax.axis_index("prow"), t, prows) * each + slot)
            for t in range(tiles) for s in range(images - 1) for slot in range(each)
        ]
    else:
        times = [table.anchor_times(t, slot) for t in range(tiles) for slot in range(NSEL)]
    normed = jnp.concatenate([ref[...] for ref in key_refs], axis=0)
    project(normed, times, wk_ref, wv_ref, k_scr, v_scr)
    channels = q_ref.shape[0]
    width = q_ref.shape[1] // groups
    attend_heads(q_ref, k_scr, v_scr, out_scr, level_scr, width)
    pairs = list(zip(early_refs[::2], early_refs[1::2])) + [(out_scr, level_scr)]
    parts = [
        (ref, lambda head, cols, level=level: level[head, 0:1, cols]) for ref, level in pairs
    ]
    heads = channels // HEAD_DIM
    row = lax.broadcasted_iota(jnp.int32, (2 * SUBLANES, width), 0)
    for n in range(groups):
        cols = slice(n * width, (n + 1) * width)
        ref = own_ref if n == 0 else sent_refs[n - 1]
        levels = jnp.zeros((2 * SUBLANES, width), F32)
        for head in range(heads):
            value, level = merge_head(parts, head, cols)
            ref[head * HEAD_DIM:(head + 1) * HEAD_DIM] = value.astype(BF16)
            levels = jnp.where(row == head, level, levels)
        if n == 0:
            own_level_ref[...] = levels
        else:
            for term in range(3):
                high = levels.astype(BF16)
                at = channels + term * 2 * SUBLANES
                ref[at:at + 2 * SUBLANES] = high
                levels = levels - high.astype(F32)


def attend_anchors(info, table, queries, keys, earlier, w_key, w_value, groups):
    size, channels = keys[0].shape
    rows = queries.shape[1]
    width = rows // groups
    flat = [leaf for part in earlier for leaf in part]
    heads = channels // HEAD_DIM
    return pl.pallas_call(
        functools.partial(anchor_kernel, info, len(keys), len(earlier), groups),
        out_shape=(shape(channels, width), shape(2 * SUBLANES, width, dtype=F32))
        + (shape(channels + 6 * SUBLANES, width),) * (groups - 1),
        in_specs=[SMEM] + [VMEM] * (len(keys) + len(flat) + 3),
        out_specs=(VMEM,) * (1 + groups),
        scratch_shapes=[
            pltpu.VMEM((channels, rows), BF16), pltpu.VMEM((heads, SUBLANES, rows), F32),
        ] + key_scratch(size * len(keys), channels),
        compiler_params=grant(24),
        cost_estimate=attend_cost(rows, size * len(keys), channels),
        name="attend_anchors",
    )(table, queries, *keys, *flat, w_key, w_value)


def finish_kernel(cores, own_ref, level_ref, *refs):
    *received, w_ref, out_ref, merged = refs
    channels, tokens = own_ref.shape

    def row_of(ref, base, terms):
        def level(head, cols):
            return functools.reduce(jnp.add, [
                ref[base + t * 2 * SUBLANES:base + (t + 1) * 2 * SUBLANES].astype(F32)
                for t in range(terms)
            ])[head:head + 1]

        return level

    parts = [(own_ref, row_of(level_ref, 0, 1))]
    parts += [(ref, row_of(ref, channels, 3)) for ref in received]
    every = slice(0, tokens)
    for head in range(channels // HEAD_DIM):
        value, _ = merge_head(parts, head, every)
        merged[head * HEAD_DIM:(head + 1) * HEAD_DIM] = value.astype(BF16)
    out = lax.dot_general(
        merged[...], w_ref[...], (((0,), (0,)), ((), ())), preferred_element_type=F32
    ).astype(BF16)
    core = lax.axis_index("pcol")
    per = BLOCK // cores
    blocks = tokens // BLOCK
    for s in range(cores):
        for b in range(blocks):
            at = b * BLOCK + lax.rem(core + s, cores) * per
            out_ref[pl.ds(pl.multiple_of(at, per), per)] = out[
                (s * blocks + b) * per:(s * blocks + b + 1) * per
            ]


def finish(own, level, received, w_out, cores):
    channels, tokens = own.shape
    return pl.pallas_call(
        functools.partial(finish_kernel, cores),
        out_shape=shape(tokens, channels),
        in_specs=[VMEM] * (3 + len(received)),
        out_specs=VMEM,
        scratch_shapes=[pltpu.VMEM((channels, tokens), BF16)],
        compiler_params=grant(16),
        cost_estimate=cost(2 * tokens * channels**2, 2 * channels * (channels + 3 * tokens)),
        name="finish",
    )(own, level, *received, w_out)


def slot_place(table, anchor, slot, info):
    cores, per_patch = info[2], info[4]
    per = BLOCK // cores
    block = table.block(anchor, jnp.where(slot < table.count(anchor), slot, 0))
    patch, inner = lax.div(block, per_patch), lax.rem(block, per_patch)
    part = lax.rem(lax.rem(patch, cores) - lax.axis_index("pcol") + cores, cores)
    return lax.div(patch, cores), pl.multiple_of((part * per_patch + inner) * per, per)


def offer_kernel(info, table_ref, key_ref, *out_refs):
    anchors, images, cores, prows, _ = info
    table = Table(table_ref, anchors, images)
    anchor = table.anchor_at(lax.axis_index("image"))
    per, each = BLOCK // cores, NSEL // prows
    for step, ref in enumerate(out_refs):
        target = target_of(lax.axis_index("prow"), step, prows)
        for n in range(each):
            _, at = slot_place(table, anchor, target * each + n, info)
            ref[n * per:(n + 1) * per] = key_ref[pl.ds(at, per)]


def offer(info, table, key):
    rows = NSEL // info[3] * (BLOCK // info[2])
    return pl.pallas_call(
        functools.partial(offer_kernel, info),
        out_shape=(shape(rows, key.shape[1]),) * info[3],
        in_specs=[SMEM, VMEM],
        out_specs=(VMEM,) * info[3],
        compiler_params=grant(8),
        name="offer",
    )(table, key)


def accept_kernel(info, table_ref, *refs):
    anchors, images, cores, prows, _ = info
    *offers, out_ref = refs
    table = Table(table_ref, anchors, images)
    anchor = table.anchor_at(lax.axis_index("image"))
    prow = lax.axis_index("prow")
    per, each = BLOCK // cores, NSEL // prows
    for n in range(each):
        holder, _ = slot_place(table, anchor, prow * each + n, info)
        rows = slice(n * per, (n + 1) * per)
        for step, ref in enumerate(offers):
            @pl.when(step_of(prow, holder, prows) == step)
            def _():
                out_ref[rows] = ref[rows]


def accept(info, table, offers):
    return pl.pallas_call(
        functools.partial(accept_kernel, info),
        out_shape=shape(*offers[0].shape),
        in_specs=[SMEM] + [VMEM] * len(offers),
        out_specs=VMEM,
        compiler_params=grant(8),
        name="accept",
    )(table, *offers)


def anchor_rows(key, anchor_index, block_order, block_count, cores, per_patch):
    per = BLOCK // cores
    live = jnp.arange(NSEL) < block_count[:, None]
    block = jnp.where(live, block_order[:, :NSEL], block_order[:, :1])
    patch = block // per_patch
    part = (patch % cores - lax.axis_index("pcol")) % cores
    rows = key.reshape(-1, per, key.shape[1])[part * per_patch + block % per_patch]
    held = (patch // cores == lax.axis_index("prow")) & (
        anchor_index == lax.axis_index("image"))[:, None]
    rows = jnp.where(held[..., None, None], rows, jnp.zeros_like(rows))
    return lax.psum(rows.reshape(len(block), NSEL * per, -1), ("image", "prow"))


def shards(
    latent, conv_weight, w_query, w_key, w_value, w_out, anchor_index, block_order, block_count
):
    tile_rows, tile_cols, _ = latent.shape[1:]
    cores, prows, images = (lax.axis_size(a) for a in ("pcol", "prow", "image"))
    anchors = anchor_index.shape[0]
    per_patch = tile_rows * tile_cols // BLOCK
    info = (anchors, images, cores, prows, per_patch)
    table = Table.build(anchor_index, block_count, block_order[:, :NSEL])
    sides, wq, wv = lax.optimization_barrier((halo(latent[0]), w_query.T, w_value.T))
    features, *parts = conv_norm(latent[0], sides, conv_weight, cores)
    keys, queries = [parts[0]], list(parts)
    for s in range(1, cores):
        theirs = [None] * cores
        for t in [cores - s] + [t for t in range(cores) if t != cores - s]:
            theirs[t] = shifted(parts[t], "pcol", s)
        keys.append(theirs[cores - s])
        queries += theirs
    key = jnp.concatenate(keys, axis=0)
    every_image = anchors == images
    if every_image:
        mine, *offers = offer(info, table, key)
        offers = [mine] + [exchange(rows, "prow", s) for s, rows in enumerate(offers, 1)]
    plane = [exchange(key, "prow", s) for s in range(1, prows)]
    q, value, level = attend_own(info, table, queries, key, wq, w_key, wv)
    done = [(value, level)]
    if every_image:
        share = accept(info, table, offers)
        across = []
        for s in range(1, images):
            across.append(exchange(share, "image", s))
        local = jnp.concatenate(across, axis=0)
        sources = [local] + [exchange(local, "prow", s) for s in range(1, prows)]
    else:
        joined = anchor_rows(key, anchor_index, block_order, block_count, cores, per_patch)
        sources = [joined[anchor] for anchor in range(anchors)]
    if plane:
        done.append(attend_plane(info, table, q, plane, w_key, wv))
    own, level, *sent = attend_anchors(info, table, q, sources, done, w_key, wv, cores)
    received = [shifted(block, "pcol", cores - s) for s, block in enumerate(sent, 1)]
    attended = finish(own, level, received, w_out, cores)
    return features.reshape(latent.shape), attended.reshape(latent.shape)


def solution(mesh):
    tiled = P(("group", "image"), "prow", "pcol", None)
    return jax.shard_map(
        shards,
        mesh=mesh,
        in_specs=(tiled, P(), P(), P(), P(), P(), P("group"), P("group", None), P("group")),
        out_specs=(tiled, tiled),
        check_vma=False,
    )
```

```python
import functools

import jax
import jax.numpy as jnp
from jax import lax
from jax.experimental import pallas as pl
from jax.experimental.pallas import tpu as pltpu
from jax.sharding import PartitionSpec as P

HEAD_DIM = 64
BLOCK = 128
NSEL = 4
LANES = 128
SUBLANES = 8
ONES = 16
AHEAD = 2
EDGE_FLOPS = 4 * 10**9
CONV_MIB = 52
F32 = jnp.float32
BF16 = jnp.bfloat16
MIB = 1 << 20


VMEM = pl.BlockSpec(memory_space=pltpu.VMEM)
HBM = pl.BlockSpec(memory_space=pltpu.HBM)
SMEM = pl.BlockSpec(memory_space=pltpu.SMEM)


def shape(*dims, dtype=BF16):
    return jax.ShapeDtypeStruct(dims, dtype)


def cost(flops, moved, exps=0):
    return pl.CostEstimate(flops=flops, bytes_accessed=moved, transcendentals=exps)


def grant(mib):
    return pltpu.CompilerParams(vmem_limit_bytes=mib * MIB)


def source_of(index, step, count):
    if count & (count - 1) == 0:
        return index ^ step
    return lax.rem(index + step, count) if not isinstance(index, int) else (index + step) % count


def target_of(index, step, count):
    if count & (count - 1) == 0:
        return index ^ step
    return lax.rem(index - step + count, count)


def step_of(index, source, count):
    if count & (count - 1) == 0:
        return index ^ source
    return lax.rem(source - index + count, count)


def exchange(block, axis, step):
    count = lax.axis_size(axis)
    return lax.ppermute(block, axis, [(source_of(i, step, count), i) for i in range(count)])


def shifted(block, axis, step):
    count = lax.axis_size(axis)
    return lax.ppermute(block, axis, [((i + step) % count, i) for i in range(count)])


def edges_kernel(x_ref, first_ref, last_ref, top_ref, bottom_ref):
    rows, cols, _ = x_ref.shape
    part = 2 * SUBLANES
    first_ref[...] = x_ref[:, :part].astype(F32)[:, 0].astype(BF16)
    last_ref[...] = x_ref[:, cols - part:].astype(F32)[:, part - 1].astype(BF16)
    top_ref[...] = x_ref[0]
    bottom_ref[...] = x_ref[rows - 1]


def edges(cells):
    rows, cols, channels = cells.shape
    return pl.pallas_call(
        edges_kernel,
        out_shape=(shape(rows, channels),) * 2 + (shape(cols, channels),) * 2,
        in_specs=[VMEM],
        out_specs=(VMEM,) * 4,
        compiler_params=grant(8),
        cost_estimate=cost(EDGE_FLOPS, cells.nbytes),
        name="edges",
    )(cells)


def halo(cells):
    first, last, top, bottom = edges(cells)
    core, cores = lax.axis_index("pcol"), lax.axis_size("pcol")
    rows = lax.axis_size("prow")
    if cores == 2:
        other = shifted(jnp.where(core == 0, last, first), "pcol", 1)
        zero = jnp.zeros_like(other)
        left = jnp.where(core == 1, other, zero)
        right = jnp.where(core == 0, other, zero)
    else:
        left = lax.ppermute(last, "pcol", [(i, i + 1) for i in range(cores - 1)])
        right = lax.ppermute(first, "pcol", [(i + 1, i) for i in range(cores - 1)])
    low = jnp.concatenate([bottom, left[-1:], right[-1:]], axis=0)
    high = jnp.concatenate([top, left[:1], right[:1]], axis=0)
    odd = lax.rem(lax.axis_index("prow"), 2) == 1
    swaps = []
    for first in range(2):
        pairs = [(i, i + 1) for i in range(first, rows - 1, 2)]
        block = jnp.where(odd, high, low) if first == 0 else jnp.where(odd, low, high)
        swaps.append(lax.ppermute(block, "prow", pairs + [(j, i) for i, j in pairs]))
    above = jnp.where(odd, swaps[0], swaps[1])
    below = jnp.where(odd, swaps[1], swaps[0])
    return left, right, above, below


def conv_kernel(rows, cols, cores, x_ref, left_ref, right_ref, above_ref, below_ref, w_ref, *refs):
    features_ref, *half_refs, shift0, shift1, shift2, taps, sem = refs
    copies = [
        pltpu.make_async_copy(w_ref.at[rows_of], taps.at[rows_of], sem.at[n])
        for n, rows_of in enumerate((slice(0, 1), slice(1, 3)))
    ]
    for copy in copies:
        copy.start()

    def silu(v):
        v = v.astype(F32)
        return (v / (1.0 + jnp.exp(-v))).astype(BF16).astype(F32)

    side = lax.broadcasted_iota(jnp.int32, (cols, x_ref.shape[1]), 0)
    for r in range(rows + 2):
        if r == 0 or r == rows + 1:
            ref = above_ref if r == 0 else below_ref
            cells, lcell, rcell = ref[:cols], ref[cols:cols + 1], ref[cols + 1:cols + 2]
        else:
            cells = x_ref[(r - 1) * cols:r * cols]
            lcell, rcell = left_ref[r - 1:r], right_ref[r - 1:r]
        cells, lcell, rcell = silu(cells), silu(lcell), silu(rcell)
        at = slice(r * cols, (r + 1) * cols)
        shift1[at] = cells.astype(BF16)
        shift0[at] = jnp.where(side == 0, lcell, pltpu.roll(cells, 1, 0)).astype(BF16)
        shift2[at] = jnp.where(side == cols - 1, rcell, pltpu.roll(cells, cols - 1, 0)).astype(BF16)
    total = x_ref[...].astype(F32)
    for a in range(3):
        if a < 2:
            copies[a].wait()
        for b, shift in enumerate((shift0, shift1, shift2)):
            total = total + jnp.dot(
                shift[a * cols:(a + rows) * cols], taps[a, b], preferred_element_type=F32
            )
    features = total.astype(BF16)
    features_ref[...] = features
    values = features.astype(F32)
    centered = values - jnp.mean(values, axis=-1, keepdims=True)
    spread = jnp.mean(centered * centered, axis=-1, keepdims=True)
    normed = (centered * lax.rsqrt(spread + 1e-05)).astype(BF16)
    core = lax.axis_index("pcol")
    per = BLOCK // cores
    for b in range(rows * cols // BLOCK):
        for h in range(cores):
            rows_of = normed[b * BLOCK + h * per:b * BLOCK + (h + 1) * per]
            for s, ref in enumerate(half_refs):
                @pl.when(lax.rem(core + s, cores) == h)
                def _():
                    ref[b * per:(b + 1) * per] = rows_of


def conv_norm(cells, sides, conv_weight, cores):
    rows, cols, channels = cells.shape
    tokens = rows * cols
    return pl.pallas_call(
        functools.partial(conv_kernel, rows, cols, cores),
        out_shape=(shape(tokens, channels),) + (shape(tokens // cores, channels),) * cores,
        in_specs=[VMEM] * 5 + [HBM],
        out_specs=(VMEM,) * (1 + cores),
        scratch_shapes=[pltpu.VMEM(((rows + 2) * cols, channels), BF16)] * 3 + [
            pltpu.VMEM((3, 3, channels, channels), BF16), pltpu.SemaphoreType.DMA((2,)),
        ],
        compiler_params=grant(CONV_MIB),
        cost_estimate=cost(18 * tokens * channels**2, 18 * channels**2, tokens * channels),
        name="conv_norm",
    )(cells.reshape(tokens, channels), *sides, conv_weight)


class Table:
    def __init__(self, ref, anchors, images):
        self.ref, self.anchors, self.images = ref, anchors, images
        self.every_image = anchors == images

    @staticmethod
    def build(anchor_index, block_count, order):
        return jnp.concatenate([anchor_index, block_count, order.reshape(-1)])

    def anchor_at(self, image):
        found = jnp.int32(0)
        for a in range(1, self.anchors):
            found = jnp.where(self.ref[a] == image, a, found)
        return found

    def count(self, anchor):
        return self.ref[self.anchors + anchor]

    def block(self, anchor, slot):
        return self.ref[2 * self.anchors + anchor * NSEL + slot]

    def own_times(self, step, group, cores, prows, per_patch):
        if not self.every_image:
            return jnp.float32(1.0)
        s, b = divmod(group, per_patch)
        patch = source_of(lax.axis_index("prow"), step, prows) * cores
        block = (patch + lax.rem(lax.axis_index("pcol") + s, cores)) * per_patch + b
        anchor = self.anchor_at(lax.axis_index("image"))
        times = jnp.float32(1.0)
        for slot in range(NSEL):
            hit = (slot < self.count(anchor)) & (self.block(anchor, slot) == block)
            times = jnp.where(hit, 2.0, times)
        return times

    def anchor_times(self, source, slot):
        if self.every_image:
            image = source_of(lax.axis_index("image"), source + 1, self.images)
            source = self.anchor_at(image)
        return jnp.where(slot < self.count(source), 1.0, 0.0).astype(F32)


def project(normed, times, wk_ref, wv_ref, k_scr, v_scr):
    keys, channels = normed.shape
    k = jnp.dot(normed, wk_ref[...], preferred_element_type=F32).astype(BF16)
    for pair in range(channels // LANES):
        k_scr[pair] = k[:, pair * LANES:(pair + 1) * LANES]
    v = jnp.dot(normed, wv_ref[...], preferred_element_type=F32).astype(BF16).T
    per = keys // len(times)
    lane = lax.broadcasted_iota(jnp.int32, (1, keys), 1)
    mult = jnp.full((1, keys), times[0], F32)
    for g in range(1, len(times)):
        mult = jnp.where(lane >= g * per, times[g], mult)
    v = v * mult.astype(BF16)
    ones = jnp.broadcast_to(mult, (ONES, keys)).astype(BF16)
    for head in range(channels // HEAD_DIM):
        v_scr[head, :HEAD_DIM] = v[head * HEAD_DIM:(head + 1) * HEAD_DIM]
        v_scr[head, HEAD_DIM:] = ones


def attend_heads(q_ref, k_scr, v_scr, out_ref, level_ref, width):
    zeros = jnp.zeros((HEAD_DIM, width), BF16)
    items = [
        (head, slice(at, at + width))
        for head in range(q_ref.shape[0] // HEAD_DIM)
        for at in range(0, q_ref.shape[1], width)
    ]

    def scores_of(head, cols):
        q = q_ref[head * HEAD_DIM:(head + 1) * HEAD_DIM, cols]
        q = jnp.concatenate([q, zeros] if head % 2 == 0 else [zeros, q], axis=0)
        return jnp.dot(k_scr[head // 2], q, preferred_element_type=F32)

    ahead = [scores_of(*item) for item in items[:AHEAD]]
    for n, (head, cols) in enumerate(items):
        scores = ahead.pop(0)
        if n + AHEAD < len(items):
            ahead.append(scores_of(*items[n + AHEAD]))
        peak = jnp.max(scores, axis=0, keepdims=True)
        probs = jnp.exp(scores - peak).astype(BF16)
        value = jnp.dot(v_scr[head], probs, preferred_element_type=F32)
        total = value[HEAD_DIM:HEAD_DIM + 1]
        out_ref[head * HEAD_DIM:(head + 1) * HEAD_DIM, cols] = (
            value[:HEAD_DIM] * (1.0 / total)
        ).astype(out_ref.dtype)
        level_ref[head, :, cols] = jnp.broadcast_to(peak + jnp.log(total), (SUBLANES, width))


def own_kernel(info, n_parts, table_ref, *refs):
    anchors, images, cores, prows, per_patch = info
    part_refs, key_ref = refs[:n_parts], refs[n_parts]
    wq_ref, wk_ref, wv_ref, q_ref, out_ref, level_ref, k_scr, v_scr = refs[n_parts + 1:]
    table = Table(table_ref, anchors, images)
    at = 0
    for ref in part_refs:
        q = jnp.dot(ref[...], wq_ref[...], preferred_element_type=F32).astype(BF16)
        q_ref[:, at:at + ref.shape[0]] = q.T * BF16(HEAD_DIM ** (-0.5))
        at += ref.shape[0]
    times = [table.own_times(0, g, cores, prows, per_patch) for g in range(cores * per_patch)]
    project(key_ref[...], times, wk_ref, wv_ref, k_scr, v_scr)
    attend_heads(q_ref, k_scr, v_scr, out_ref, level_ref, part_refs[0].shape[0] * cores)


def key_scratch(keys, channels):
    return [
        pltpu.VMEM((channels // LANES, keys, LANES), BF16),
        pltpu.VMEM((channels // HEAD_DIM, HEAD_DIM + ONES, keys), BF16),
    ]


def attend_cost(rows, keys, channels, extra=0):
    return cost(
        4 * keys * channels**2 + 16 * rows * keys * channels + extra,
        2 * channels * (2 * rows + keys),
        rows * keys * channels // HEAD_DIM,
    )


def attend_own(info, table, parts, key, w_query, w_key, w_value):
    size, channels = key.shape
    rows = sum(part.shape[0] for part in parts)
    return pl.pallas_call(
        functools.partial(own_kernel, info, len(parts)),
        out_shape=(
            shape(channels, rows), shape(channels, rows),
            shape(channels // HEAD_DIM, SUBLANES, rows, dtype=F32),
        ),
        in_specs=[SMEM] + [VMEM] * (len(parts) + 4),
        out_specs=(VMEM,) * 3,
        scratch_shapes=key_scratch(size, channels),
        compiler_params=grant(24),
        cost_estimate=attend_cost(rows, size, channels, 2 * rows * channels**2),
        name="attend_own",
    )(table, *parts, key, w_query, w_key, w_value)


def plane_kernel(info, tiles, table_ref, q_ref, *refs):
    anchors, images, cores, prows, per_patch = info
    key_refs = refs[:tiles]
    wk_ref, wv_ref, out_ref, level_ref, k_scr, v_scr = refs[tiles:]
    table = Table(table_ref, anchors, images)
    times = [
        table.own_times(t + 1, g, cores, prows, per_patch)
        for t in range(tiles) for g in range(cores * per_patch)
    ]
    normed = jnp.concatenate([ref[...] for ref in key_refs], axis=0)
    project(normed, times, wk_ref, wv_ref, k_scr, v_scr)
    attend_heads(q_ref, k_scr, v_scr, out_ref, level_ref, q_ref.shape[1] // cores)


def attend_plane(info, table, queries, keys, w_key, w_value):
    size, channels = keys[0].shape
    rows = queries.shape[1]
    return pl.pallas_call(
        functools.partial(plane_kernel, info, len(keys)),
        out_shape=(
            shape(channels, rows), shape(channels // HEAD_DIM, SUBLANES, rows, dtype=F32),
        ),
        in_specs=[SMEM] + [VMEM] * (len(keys) + 3),
        out_specs=(VMEM,) * 2,
        scratch_shapes=key_scratch(size * len(keys), channels),
        compiler_params=grant(24),
        cost_estimate=attend_cost(rows, size * len(keys), channels),
        name="attend_plane",
    )(table, queries, *keys, w_key, w_value)


def merge_head(parts, head, cols):
    rows = slice(head * HEAD_DIM, (head + 1) * HEAD_DIM)
    levels = [level(head, cols) for _, level in parts]
    peak = functools.reduce(jnp.maximum, levels)
    weights = [jnp.exp(level - peak) for level in levels]
    total = functools.reduce(jnp.add, weights)
    value = functools.reduce(
        jnp.add, [w * ref[rows, cols].astype(F32) for w, (ref, _) in zip(weights, parts)]
    )
    return value * (1.0 / total), peak + jnp.log(total)


def anchor_kernel(info, tiles, earlier, groups, table_ref, q_ref, *refs):
    anchors, images, _, prows, _ = info
    key_refs, refs = refs[:tiles], refs[tiles:]
    early_refs, refs = refs[:2 * earlier], refs[2 * earlier:]
    wk_ref, wv_ref, *out_refs = refs[:2 + groups + 1]
    out_scr, level_scr, k_scr, v_scr = refs[3 + groups:]
    own_ref, own_level_ref, *sent_refs = out_refs
    table = Table(table_ref, anchors, images)
    if table.every_image:
        each = NSEL // prows
        times = [
            table.anchor_times(s, source_of(lax.axis_index("prow"), t, prows) * each + slot)
            for t in range(tiles) for s in range(images - 1) for slot in range(each)
        ]
    else:
        times = [table.anchor_times(t, slot) for t in range(tiles) for slot in range(NSEL)]
    normed = jnp.concatenate([ref[...] for ref in key_refs], axis=0)
    project(normed, times, wk_ref, wv_ref, k_scr, v_scr)
    channels = q_ref.shape[0]
    width = q_ref.shape[1] // groups
    attend_heads(q_ref, k_scr, v_scr, out_scr, level_scr, width)
    pairs = list(zip(early_refs[::2], early_refs[1::2])) + [(out_scr, level_scr)]
    parts = [
        (ref, lambda head, cols, level=level: level[head, 0:1, cols]) for ref, level in pairs
    ]
    heads = channels // HEAD_DIM
    row = lax.broadcasted_iota(jnp.int32, (2 * SUBLANES, width), 0)
    for n in range(groups):
        cols = slice(n * width, (n + 1) * width)
        ref = own_ref if n == 0 else sent_refs[n - 1]
        levels = jnp.zeros((2 * SUBLANES, width), F32)
        for head in range(heads):
            value, level = merge_head(parts, head, cols)
            ref[head * HEAD_DIM:(head + 1) * HEAD_DIM] = value.astype(BF16)
            levels = jnp.where(row == head, level, levels)
        if n == 0:
            own_level_ref[...] = levels
        else:
            for term in range(3):
                high = levels.astype(BF16)
                at = channels + term * 2 * SUBLANES
                ref[at:at + 2 * SUBLANES] = high
                levels = levels - high.astype(F32)


def attend_anchors(info, table, queries, keys, earlier, w_key, w_value, groups):
    size, channels = keys[0].shape
    rows = queries.shape[1]
    width = rows // groups
    flat = [leaf for part in earlier for leaf in part]
    heads = channels // HEAD_DIM
    return pl.pallas_call(
        functools.partial(anchor_kernel, info, len(keys), len(earlier), groups),
        out_shape=(shape(channels, width), shape(2 * SUBLANES, width, dtype=F32))
        + (shape(channels + 6 * SUBLANES, width),) * (groups - 1),
        in_specs=[SMEM] + [VMEM] * (len(keys) + len(flat) + 3),
        out_specs=(VMEM,) * (1 + groups),
        scratch_shapes=[
            pltpu.VMEM((channels, rows), BF16), pltpu.VMEM((heads, SUBLANES, rows), F32),
        ] + key_scratch(size * len(keys), channels),
        compiler_params=grant(24),
        cost_estimate=attend_cost(rows, size * len(keys), channels),
        name="attend_anchors",
    )(table, queries, *keys, *flat, w_key, w_value)


def finish_kernel(cores, own_ref, level_ref, *refs):
    *received, w_ref, out_ref, merged = refs
    channels, tokens = own_ref.shape

    def row_of(ref, base, terms):
        def level(head, cols):
            return functools.reduce(jnp.add, [
                ref[base + t * 2 * SUBLANES:base + (t + 1) * 2 * SUBLANES].astype(F32)
                for t in range(terms)
            ])[head:head + 1]

        return level

    parts = [(own_ref, row_of(level_ref, 0, 1))]
    parts += [(ref, row_of(ref, channels, 3)) for ref in received]
    every = slice(0, tokens)
    for head in range(channels // HEAD_DIM):
        value, _ = merge_head(parts, head, every)
        merged[head * HEAD_DIM:(head + 1) * HEAD_DIM] = value.astype(BF16)
    out = lax.dot_general(
        merged[...], w_ref[...], (((0,), (0,)), ((), ())), preferred_element_type=F32
    ).astype(BF16)
    core = lax.axis_index("pcol")
    per = BLOCK // cores
    blocks = tokens // BLOCK
    for s in range(cores):
        for b in range(blocks):
            at = b * BLOCK + lax.rem(core + s, cores) * per
            out_ref[pl.ds(pl.multiple_of(at, per), per)] = out[
                (s * blocks + b) * per:(s * blocks + b + 1) * per
            ]


def finish(own, level, received, w_out, cores):
    channels, tokens = own.shape
    return pl.pallas_call(
        functools.partial(finish_kernel, cores),
        out_shape=shape(tokens, channels),
        in_specs=[VMEM] * (3 + len(received)),
        out_specs=VMEM,
        scratch_shapes=[pltpu.VMEM((channels, tokens), BF16)],
        compiler_params=grant(16),
        cost_estimate=cost(2 * tokens * channels**2, 2 * channels * (channels + 3 * tokens)),
        name="finish",
    )(own, level, *received, w_out)


def slot_place(table, anchor, slot, info):
    cores, per_patch = info[2], info[4]
    per = BLOCK // cores
    block = table.block(anchor, jnp.where(slot < table.count(anchor), slot, 0))
    patch, inner = lax.div(block, per_patch), lax.rem(block, per_patch)
    part = lax.rem(lax.rem(patch, cores) - lax.axis_index("pcol") + cores, cores)
    return lax.div(patch, cores), pl.multiple_of((part * per_patch + inner) * per, per)


def offer_kernel(info, table_ref, key_ref, *out_refs):
    anchors, images, cores, prows, _ = info
    table = Table(table_ref, anchors, images)
    anchor = table.anchor_at(lax.axis_index("image"))
    per, each = BLOCK // cores, NSEL // prows
    for step, ref in enumerate(out_refs):
        target = target_of(lax.axis_index("prow"), step, prows)
        for n in range(each):
            _, at = slot_place(table, anchor, target * each + n, info)
            ref[n * per:(n + 1) * per] = key_ref[pl.ds(at, per)]


def offer(info, table, key):
    rows = NSEL // info[3] * (BLOCK // info[2])
    return pl.pallas_call(
        functools.partial(offer_kernel, info),
        out_shape=(shape(rows, key.shape[1]),) * info[3],
        in_specs=[SMEM, VMEM],
        out_specs=(VMEM,) * info[3],
        compiler_params=grant(8),
        name="offer",
    )(table, key)


def accept_kernel(info, table_ref, *refs):
    anchors, images, cores, prows, _ = info
    *offers, out_ref = refs
    table = Table(table_ref, anchors, images)
    anchor = table.anchor_at(lax.axis_index("image"))
    prow = lax.axis_index("prow")
    per, each = BLOCK // cores, NSEL // prows
    for n in range(each):
        holder, _ = slot_place(table, anchor, prow * each + n, info)
        rows = slice(n * per, (n + 1) * per)
        for step, ref in enumerate(offers):
            @pl.when(step_of(prow, holder, prows) == step)
            def _():
                out_ref[rows] = ref[rows]


def accept(info, table, offers):
    return pl.pallas_call(
        functools.partial(accept_kernel, info),
        out_shape=shape(*offers[0].shape),
        in_specs=[SMEM] + [VMEM] * len(offers),
        out_specs=VMEM,
        compiler_params=grant(8),
        name="accept",
    )(table, *offers)


def anchor_rows(key, anchor_index, block_order, block_count, cores, per_patch):
    per = BLOCK // cores
    live = jnp.arange(NSEL) < block_count[:, None]
    block = jnp.where(live, block_order[:, :NSEL], block_order[:, :1])
    patch = block // per_patch
    part = (patch % cores - lax.axis_index("pcol")) % cores
    rows = key.reshape(-1, per, key.shape[1])[part * per_patch + block % per_patch]
    held = (patch // cores == lax.axis_index("prow")) & (
        anchor_index == lax.axis_index("image"))[:, None]
    rows = jnp.where(held[..., None, None], rows, jnp.zeros_like(rows))
    return lax.psum(rows.reshape(len(block), NSEL * per, -1), ("image", "prow"))


def shards(
    latent, conv_weight, w_query, w_key, w_value, w_out, anchor_index, block_order, block_count
):
    tile_rows, tile_cols, _ = latent.shape[1:]
    cores, prows, images = (lax.axis_size(a) for a in ("pcol", "prow", "image"))
    anchors = anchor_index.shape[0]
    per_patch = tile_rows * tile_cols // BLOCK
    info = (anchors, images, cores, prows, per_patch)
    table = Table.build(anchor_index, block_count, block_order[:, :NSEL])
    features, *parts = conv_norm(latent[0], halo(latent[0]), conv_weight, cores)
    keys, queries = [parts[0]], list(parts)
    for s in range(1, cores):
        theirs = [None] * cores
        for t in [cores - s] + [t for t in range(cores) if t != cores - s]:
            theirs[t] = shifted(parts[t], "pcol", s)
        keys.append(theirs[cores - s])
        queries += theirs
    key = jnp.concatenate(keys, axis=0)
    every_image = anchors == images
    if every_image:
        mine, *offers = offer(info, table, key)
        offers = [mine] + [exchange(rows, "prow", s) for s, rows in enumerate(offers, 1)]
    plane = [exchange(key, "prow", s) for s in range(1, prows)]
    q, value, level = attend_own(info, table, queries, key, w_query, w_key, w_value)
    done = [(value, level)]
    if every_image:
        share = accept(info, table, offers)
        across = []
        for s in range(1, images):
            across.append(exchange(share, "image", s))
        local = jnp.concatenate(across, axis=0)
        sources = [local] + [exchange(local, "prow", s) for s in range(1, prows)]
    else:
        joined = anchor_rows(key, anchor_index, block_order, block_count, cores, per_patch)
        sources = [joined[anchor] for anchor in range(anchors)]
    if plane:
        done.append(attend_plane(info, table, q, plane, w_key, w_value))
    own, level, *sent = attend_anchors(info, table, q, sources, done, w_key, w_value, cores)
    received = [shifted(block, "pcol", cores - s) for s, block in enumerate(sent, 1)]
    attended = finish(own, level, received, w_out, cores)
    return features.reshape(latent.shape), attended.reshape(latent.shape)


def solution(mesh):
    tiled = P(("group", "image"), "prow", "pcol", None)
    return jax.shard_map(
        shards,
        mesh=mesh,
        in_specs=(tiled, P(), P(), P(), P(), P(), P("group"), P("group", None), P("group")),
        out_specs=(tiled, tiled),
        check_vma=False,
    )
```

```python
import functools

import jax
import jax.numpy as jnp
from jax import lax
from jax.experimental import pallas as pl
from jax.experimental.pallas import tpu as pltpu
from jax.sharding import PartitionSpec as P

HEAD_DIM = 64
BLOCK = 128
NSEL = 4
LANES = 128
SUBLANES = 8
ONES = 16
AHEAD = 2
EDGE_FLOPS = 4 * 10**9
STAGE_MIB = 46
F32 = jnp.float32
BF16 = jnp.bfloat16
MIB = 1 << 20


VMEM = pl.BlockSpec(memory_space=pltpu.VMEM)
ANY = pl.BlockSpec(memory_space=pl.ANY)
SMEM = pl.BlockSpec(memory_space=pltpu.SMEM)


def shape(*dims, dtype=BF16):
    return jax.ShapeDtypeStruct(dims, dtype)


def cost(flops, moved, exps=0):
    return pl.CostEstimate(flops=flops, bytes_accessed=moved, transcendentals=exps)


def grant(mib):
    return pltpu.CompilerParams(vmem_limit_bytes=mib * MIB)


def source_of(index, step, count):
    if count & (count - 1) == 0:
        return index ^ step
    return lax.rem(index + step, count) if not isinstance(index, int) else (index + step) % count


def target_of(index, step, count):
    if count & (count - 1) == 0:
        return index ^ step
    return lax.rem(index - step + count, count)


def step_of(index, source, count):
    if count & (count - 1) == 0:
        return index ^ source
    return lax.rem(source - index + count, count)


def exchange(block, axis, step):
    count = lax.axis_size(axis)
    return lax.ppermute(block, axis, [(source_of(i, step, count), i) for i in range(count)])


def shifted(block, axis, step):
    count = lax.axis_size(axis)
    return lax.ppermute(block, axis, [((i + step) % count, i) for i in range(count)])


def edges_kernel(x_ref, first_ref, last_ref, top_ref, bottom_ref):
    rows, cols, _ = x_ref.shape
    part = 2 * SUBLANES
    first_ref[...] = x_ref[:, :part].astype(F32)[:, 0].astype(BF16)
    last_ref[...] = x_ref[:, cols - part:].astype(F32)[:, part - 1].astype(BF16)
    top_ref[...] = x_ref[0]
    bottom_ref[...] = x_ref[rows - 1]


def edges(cells):
    rows, cols, channels = cells.shape
    return pl.pallas_call(
        edges_kernel,
        out_shape=(shape(rows, channels),) * 2 + (shape(cols, channels),) * 2,
        in_specs=[VMEM],
        out_specs=(VMEM,) * 4,
        compiler_params=grant(8),
        cost_estimate=cost(EDGE_FLOPS, cells.nbytes),
        name="edges",
    )(cells)


def halo(cells):
    first, last, top, bottom = edges(cells)
    core, cores = lax.axis_index("pcol"), lax.axis_size("pcol")
    rows = lax.axis_size("prow")
    if cores == 2:
        other = shifted(jnp.where(core == 0, last, first), "pcol", 1)
        zero = jnp.zeros_like(other)
        left = jnp.where(core == 1, other, zero)
        right = jnp.where(core == 0, other, zero)
    else:
        left = lax.ppermute(last, "pcol", [(i, i + 1) for i in range(cores - 1)])
        right = lax.ppermute(first, "pcol", [(i + 1, i) for i in range(cores - 1)])
    low = jnp.concatenate([bottom, left[-1:], right[-1:]], axis=0)
    high = jnp.concatenate([top, left[:1], right[:1]], axis=0)
    odd = lax.rem(lax.axis_index("prow"), 2) == 1
    swaps = []
    for first in range(2):
        pairs = [(i, i + 1) for i in range(first, rows - 1, 2)]
        block = jnp.where(odd, high, low) if first == 0 else jnp.where(odd, low, high)
        swaps.append(lax.ppermute(block, "prow", pairs + [(j, i) for i, j in pairs]))
    above = jnp.where(odd, swaps[0], swaps[1])
    below = jnp.where(odd, swaps[1], swaps[0])
    return left, right, above, below


def stage_kernel(in_ref, out_ref, sem):
    copy = pltpu.make_async_copy(in_ref, out_ref, sem)
    copy.start()
    copy.wait()


def stage(array):
    return pl.pallas_call(
        stage_kernel,
        out_shape=shape(*array.shape),
        in_specs=[ANY],
        out_specs=VMEM,
        scratch_shapes=[pltpu.SemaphoreType.DMA],
        compiler_params=grant(STAGE_MIB),
        cost_estimate=cost(0, 2 * array.nbytes),
        name="stage",
    )(array)


def conv_kernel(rows, cols, cores, x_ref, left_ref, right_ref, above_ref, below_ref, w_ref, *refs):
    features_ref, *half_refs, shift0, shift1, shift2 = refs

    def silu(v):
        v = v.astype(F32)
        return (v / (1.0 + jnp.exp(-v))).astype(BF16).astype(F32)

    side = lax.broadcasted_iota(jnp.int32, (cols, x_ref.shape[1]), 0)
    for r in range(rows + 2):
        if r == 0 or r == rows + 1:
            ref = above_ref if r == 0 else below_ref
            cells, lcell, rcell = ref[:cols], ref[cols:cols + 1], ref[cols + 1:cols + 2]
        else:
            cells = x_ref[(r - 1) * cols:r * cols]
            lcell, rcell = left_ref[r - 1:r], right_ref[r - 1:r]
        cells, lcell, rcell = silu(cells), silu(lcell), silu(rcell)
        at = slice(r * cols, (r + 1) * cols)
        shift1[at] = cells.astype(BF16)
        shift0[at] = jnp.where(side == 0, lcell, pltpu.roll(cells, 1, 0)).astype(BF16)
        shift2[at] = jnp.where(side == cols - 1, rcell, pltpu.roll(cells, cols - 1, 0)).astype(BF16)
    total = x_ref[...].astype(F32)
    for a in range(3):
        for b, shift in enumerate((shift0, shift1, shift2)):
            total = total + jnp.dot(
                shift[a * cols:(a + rows) * cols], w_ref[a, b], preferred_element_type=F32
            )
    features = total.astype(BF16)
    features_ref[...] = features
    values = features.astype(F32)
    centered = values - jnp.mean(values, axis=-1, keepdims=True)
    spread = jnp.mean(centered * centered, axis=-1, keepdims=True)
    normed = (centered * lax.rsqrt(spread + 1e-05)).astype(BF16)
    core = lax.axis_index("pcol")
    per = BLOCK // cores
    for b in range(rows * cols // BLOCK):
        for h in range(cores):
            rows_of = normed[b * BLOCK + h * per:b * BLOCK + (h + 1) * per]
            for s, ref in enumerate(half_refs):
                @pl.when(lax.rem(core + s, cores) == h)
                def _():
                    ref[b * per:(b + 1) * per] = rows_of


def conv_norm(cells, sides, conv_weight, cores):
    rows, cols, channels = cells.shape
    tokens = rows * cols
    return pl.pallas_call(
        functools.partial(conv_kernel, rows, cols, cores),
        out_shape=(shape(tokens, channels),) + (shape(tokens // cores, channels),) * cores,
        in_specs=[VMEM] * 6,
        out_specs=(VMEM,) * (1 + cores),
        scratch_shapes=[pltpu.VMEM(((rows + 2) * cols, channels), BF16)] * 3,
        compiler_params=grant(24),
        cost_estimate=cost(18 * tokens * channels**2, 18 * channels**2, tokens * channels),
        name="conv_norm",
    )(cells.reshape(tokens, channels), *sides, conv_weight)


class Table:
    def __init__(self, ref, anchors, images):
        self.ref, self.anchors, self.images = ref, anchors, images
        self.every_image = anchors == images

    @staticmethod
    def build(anchor_index, block_count, order):
        return jnp.concatenate([anchor_index, block_count, order.reshape(-1)])

    def anchor_at(self, image):
        found = jnp.int32(0)
        for a in range(1, self.anchors):
            found = jnp.where(self.ref[a] == image, a, found)
        return found

    def count(self, anchor):
        return self.ref[self.anchors + anchor]

    def block(self, anchor, slot):
        return self.ref[2 * self.anchors + anchor * NSEL + slot]

    def own_times(self, step, group, cores, prows, per_patch):
        if not self.every_image:
            return jnp.float32(1.0)
        s, b = divmod(group, per_patch)
        patch = source_of(lax.axis_index("prow"), step, prows) * cores
        block = (patch + lax.rem(lax.axis_index("pcol") + s, cores)) * per_patch + b
        anchor = self.anchor_at(lax.axis_index("image"))
        times = jnp.float32(1.0)
        for slot in range(NSEL):
            hit = (slot < self.count(anchor)) & (self.block(anchor, slot) == block)
            times = jnp.where(hit, 2.0, times)
        return times

    def anchor_times(self, source, slot):
        if self.every_image:
            image = source_of(lax.axis_index("image"), source + 1, self.images)
            source = self.anchor_at(image)
        return jnp.where(slot < self.count(source), 1.0, 0.0).astype(F32)


def project(normed, times, wk_ref, wv_ref, k_scr, v_scr):
    keys, channels = normed.shape
    k = jnp.dot(normed, wk_ref[...], preferred_element_type=F32).astype(BF16)
    for pair in range(channels // LANES):
        k_scr[pair] = k[:, pair * LANES:(pair + 1) * LANES]
    v = jnp.dot(normed, wv_ref[...], preferred_element_type=F32).astype(BF16).T
    per = keys // len(times)
    lane = lax.broadcasted_iota(jnp.int32, (1, keys), 1)
    mult = jnp.full((1, keys), times[0], F32)
    for g in range(1, len(times)):
        mult = jnp.where(lane >= g * per, times[g], mult)
    v = v * mult.astype(BF16)
    ones = jnp.broadcast_to(mult, (ONES, keys)).astype(BF16)
    for head in range(channels // HEAD_DIM):
        v_scr[head, :HEAD_DIM] = v[head * HEAD_DIM:(head + 1) * HEAD_DIM]
        v_scr[head, HEAD_DIM:] = ones


def attend_heads(q_ref, k_scr, v_scr, out_ref, level_ref, width):
    zeros = jnp.zeros((HEAD_DIM, width), BF16)
    items = [
        (head, slice(at, at + width))
        for head in range(q_ref.shape[0] // HEAD_DIM)
        for at in range(0, q_ref.shape[1], width)
    ]

    def scores_of(head, cols):
        q = q_ref[head * HEAD_DIM:(head + 1) * HEAD_DIM, cols]
        q = jnp.concatenate([q, zeros] if head % 2 == 0 else [zeros, q], axis=0)
        return jnp.dot(k_scr[head // 2], q, preferred_element_type=F32)

    ahead = [scores_of(*item) for item in items[:AHEAD]]
    for n, (head, cols) in enumerate(items):
        scores = ahead.pop(0)
        if n + AHEAD < len(items):
            ahead.append(scores_of(*items[n + AHEAD]))
        peak = jnp.max(scores, axis=0, keepdims=True)
        probs = jnp.exp(scores - peak).astype(BF16)
        value = jnp.dot(v_scr[head], probs, preferred_element_type=F32)
        total = value[HEAD_DIM:HEAD_DIM + 1]
        out_ref[head * HEAD_DIM:(head + 1) * HEAD_DIM, cols] = (
            value[:HEAD_DIM] * (1.0 / total)
        ).astype(out_ref.dtype)
        level_ref[head, :, cols] = jnp.broadcast_to(peak + jnp.log(total), (SUBLANES, width))


def own_kernel(info, n_parts, table_ref, *refs):
    anchors, images, cores, prows, per_patch = info
    part_refs, key_ref = refs[:n_parts], refs[n_parts]
    wq_ref, wk_ref, wv_ref, q_ref, out_ref, level_ref, k_scr, v_scr = refs[n_parts + 1:]
    table = Table(table_ref, anchors, images)
    at = 0
    for ref in part_refs:
        q = jnp.dot(ref[...], wq_ref[...], preferred_element_type=F32).astype(BF16)
        q_ref[:, at:at + ref.shape[0]] = q.T * BF16(HEAD_DIM ** (-0.5))
        at += ref.shape[0]
    times = [table.own_times(0, g, cores, prows, per_patch) for g in range(cores * per_patch)]
    project(key_ref[...], times, wk_ref, wv_ref, k_scr, v_scr)
    attend_heads(q_ref, k_scr, v_scr, out_ref, level_ref, part_refs[0].shape[0] * cores)


def key_scratch(keys, channels):
    return [
        pltpu.VMEM((channels // LANES, keys, LANES), BF16),
        pltpu.VMEM((channels // HEAD_DIM, HEAD_DIM + ONES, keys), BF16),
    ]


def attend_cost(rows, keys, channels, extra=0):
    return cost(
        4 * keys * channels**2 + 16 * rows * keys * channels + extra,
        2 * channels * (2 * rows + keys),
        rows * keys * channels // HEAD_DIM,
    )


def attend_own(info, table, parts, key, w_query, w_key, w_value):
    size, channels = key.shape
    rows = sum(part.shape[0] for part in parts)
    return pl.pallas_call(
        functools.partial(own_kernel, info, len(parts)),
        out_shape=(
            shape(channels, rows), shape(channels, rows),
            shape(channels // HEAD_DIM, SUBLANES, rows, dtype=F32),
        ),
        in_specs=[SMEM] + [VMEM] * (len(parts) + 4),
        out_specs=(VMEM,) * 3,
        scratch_shapes=key_scratch(size, channels),
        compiler_params=grant(24),
        cost_estimate=attend_cost(rows, size, channels, 2 * rows * channels**2),
        name="attend_own",
    )(table, *parts, key, w_query, w_key, w_value)


def plane_kernel(info, tiles, table_ref, q_ref, *refs):
    anchors, images, cores, prows, per_patch = info
    key_refs = refs[:tiles]
    wk_ref, wv_ref, out_ref, level_ref, k_scr, v_scr = refs[tiles:]
    table = Table(table_ref, anchors, images)
    times = [
        table.own_times(t + 1, g, cores, prows, per_patch)
        for t in range(tiles) for g in range(cores * per_patch)
    ]
    normed = jnp.concatenate([ref[...] for ref in key_refs], axis=0)
    project(normed, times, wk_ref, wv_ref, k_scr, v_scr)
    attend_heads(q_ref, k_scr, v_scr, out_ref, level_ref, q_ref.shape[1] // cores)


def attend_plane(info, table, queries, keys, w_key, w_value):
    size, channels = keys[0].shape
    rows = queries.shape[1]
    return pl.pallas_call(
        functools.partial(plane_kernel, info, len(keys)),
        out_shape=(
            shape(channels, rows), shape(channels // HEAD_DIM, SUBLANES, rows, dtype=F32),
        ),
        in_specs=[SMEM] + [VMEM] * (len(keys) + 3),
        out_specs=(VMEM,) * 2,
        scratch_shapes=key_scratch(size * len(keys), channels),
        compiler_params=grant(24),
        cost_estimate=attend_cost(rows, size * len(keys), channels),
        name="attend_plane",
    )(table, queries, *keys, w_key, w_value)


def merge_head(parts, head, cols):
    rows = slice(head * HEAD_DIM, (head + 1) * HEAD_DIM)
    levels = [level(head, cols) for _, level in parts]
    peak = functools.reduce(jnp.maximum, levels)
    weights = [jnp.exp(level - peak) for level in levels]
    total = functools.reduce(jnp.add, weights)
    value = functools.reduce(
        jnp.add, [w * ref[rows, cols].astype(F32) for w, (ref, _) in zip(weights, parts)]
    )
    return value * (1.0 / total), peak + jnp.log(total)


def anchor_kernel(info, tiles, earlier, groups, table_ref, q_ref, *refs):
    anchors, images, _, prows, _ = info
    key_refs, refs = refs[:tiles], refs[tiles:]
    early_refs, refs = refs[:2 * earlier], refs[2 * earlier:]
    wk_ref, wv_ref, *out_refs = refs[:2 + groups + 1]
    out_scr, level_scr, k_scr, v_scr = refs[3 + groups:]
    own_ref, own_level_ref, *sent_refs = out_refs
    table = Table(table_ref, anchors, images)
    if table.every_image:
        each = NSEL // prows
        times = [
            table.anchor_times(s, source_of(lax.axis_index("prow"), t, prows) * each + slot)
            for t in range(tiles) for s in range(images - 1) for slot in range(each)
        ]
    else:
        times = [table.anchor_times(t, slot) for t in range(tiles) for slot in range(NSEL)]
    normed = jnp.concatenate([ref[...] for ref in key_refs], axis=0)
    project(normed, times, wk_ref, wv_ref, k_scr, v_scr)
    channels = q_ref.shape[0]
    width = q_ref.shape[1] // groups
    attend_heads(q_ref, k_scr, v_scr, out_scr, level_scr, width)
    pairs = list(zip(early_refs[::2], early_refs[1::2])) + [(out_scr, level_scr)]
    parts = [
        (ref, lambda head, cols, level=level: level[head, 0:1, cols]) for ref, level in pairs
    ]
    heads = channels // HEAD_DIM
    row = lax.broadcasted_iota(jnp.int32, (2 * SUBLANES, width), 0)
    for n in range(groups):
        cols = slice(n * width, (n + 1) * width)
        ref = own_ref if n == 0 else sent_refs[n - 1]
        levels = jnp.zeros((2 * SUBLANES, width), F32)
        for head in range(heads):
            value, level = merge_head(parts, head, cols)
            ref[head * HEAD_DIM:(head + 1) * HEAD_DIM] = value.astype(BF16)
            levels = jnp.where(row == head, level, levels)
        if n == 0:
            own_level_ref[...] = levels
        else:
            for term in range(3):
                high = levels.astype(BF16)
                at = channels + term * 2 * SUBLANES
                ref[at:at + 2 * SUBLANES] = high
                levels = levels - high.astype(F32)


def attend_anchors(info, table, queries, keys, earlier, w_key, w_value, groups):
    size, channels = keys[0].shape
    rows = queries.shape[1]
    width = rows // groups
    flat = [leaf for part in earlier for leaf in part]
    heads = channels // HEAD_DIM
    return pl.pallas_call(
        functools.partial(anchor_kernel, info, len(keys), len(earlier), groups),
        out_shape=(shape(channels, width), shape(2 * SUBLANES, width, dtype=F32))
        + (shape(channels + 6 * SUBLANES, width),) * (groups - 1),
        in_specs=[SMEM] + [VMEM] * (len(keys) + len(flat) + 3),
        out_specs=(VMEM,) * (1 + groups),
        scratch_shapes=[
            pltpu.VMEM((channels, rows), BF16), pltpu.VMEM((heads, SUBLANES, rows), F32),
        ] + key_scratch(size * len(keys), channels),
        compiler_params=grant(24),
        cost_estimate=attend_cost(rows, size * len(keys), channels),
        name="attend_anchors",
    )(table, queries, *keys, *flat, w_key, w_value)


def finish_kernel(cores, own_ref, level_ref, *refs):
    *received, w_ref, out_ref, merged = refs
    channels, tokens = own_ref.shape

    def row_of(ref, base, terms):
        def level(head, cols):
            return functools.reduce(jnp.add, [
                ref[base + t * 2 * SUBLANES:base + (t + 1) * 2 * SUBLANES].astype(F32)
                for t in range(terms)
            ])[head:head + 1]

        return level

    parts = [(own_ref, row_of(level_ref, 0, 1))]
    parts += [(ref, row_of(ref, channels, 3)) for ref in received]
    every = slice(0, tokens)
    for head in range(channels // HEAD_DIM):
        value, _ = merge_head(parts, head, every)
        merged[head * HEAD_DIM:(head + 1) * HEAD_DIM] = value.astype(BF16)
    out = lax.dot_general(
        merged[...], w_ref[...], (((0,), (0,)), ((), ())), preferred_element_type=F32
    ).astype(BF16)
    core = lax.axis_index("pcol")
    per = BLOCK // cores
    blocks = tokens // BLOCK
    for s in range(cores):
        for b in range(blocks):
            at = b * BLOCK + lax.rem(core + s, cores) * per
            out_ref[pl.ds(pl.multiple_of(at, per), per)] = out[
                (s * blocks + b) * per:(s * blocks + b + 1) * per
            ]


def finish(own, level, received, w_out, cores):
    channels, tokens = own.shape
    return pl.pallas_call(
        functools.partial(finish_kernel, cores),
        out_shape=shape(tokens, channels),
        in_specs=[VMEM] * (3 + len(received)),
        out_specs=VMEM,
        scratch_shapes=[pltpu.VMEM((channels, tokens), BF16)],
        compiler_params=grant(16),
        cost_estimate=cost(2 * tokens * channels**2, 2 * channels * (channels + 3 * tokens)),
        name="finish",
    )(own, level, *received, w_out)


def slot_place(table, anchor, slot, info):
    cores, per_patch = info[2], info[4]
    per = BLOCK // cores
    block = table.block(anchor, jnp.where(slot < table.count(anchor), slot, 0))
    patch, inner = lax.div(block, per_patch), lax.rem(block, per_patch)
    part = lax.rem(lax.rem(patch, cores) - lax.axis_index("pcol") + cores, cores)
    return lax.div(patch, cores), pl.multiple_of((part * per_patch + inner) * per, per)


def offer_kernel(info, table_ref, key_ref, *out_refs):
    anchors, images, cores, prows, _ = info
    table = Table(table_ref, anchors, images)
    anchor = table.anchor_at(lax.axis_index("image"))
    per, each = BLOCK // cores, NSEL // prows
    for step, ref in enumerate(out_refs):
        target = target_of(lax.axis_index("prow"), step, prows)
        for n in range(each):
            _, at = slot_place(table, anchor, target * each + n, info)
            ref[n * per:(n + 1) * per] = key_ref[pl.ds(at, per)]


def offer(info, table, key):
    rows = NSEL // info[3] * (BLOCK // info[2])
    return pl.pallas_call(
        functools.partial(offer_kernel, info),
        out_shape=(shape(rows, key.shape[1]),) * info[3],
        in_specs=[SMEM, VMEM],
        out_specs=(VMEM,) * info[3],
        compiler_params=grant(8),
        name="offer",
    )(table, key)


def accept_kernel(info, table_ref, *refs):
    anchors, images, cores, prows, _ = info
    *offers, out_ref = refs
    table = Table(table_ref, anchors, images)
    anchor = table.anchor_at(lax.axis_index("image"))
    prow = lax.axis_index("prow")
    per, each = BLOCK // cores, NSEL // prows
    for n in range(each):
        holder, _ = slot_place(table, anchor, prow * each + n, info)
        rows = slice(n * per, (n + 1) * per)
        for step, ref in enumerate(offers):
            @pl.when(step_of(prow, holder, prows) == step)
            def _():
                out_ref[rows] = ref[rows]


def accept(info, table, offers):
    return pl.pallas_call(
        functools.partial(accept_kernel, info),
        out_shape=shape(*offers[0].shape),
        in_specs=[SMEM] + [VMEM] * len(offers),
        out_specs=VMEM,
        compiler_params=grant(8),
        name="accept",
    )(table, *offers)


def anchor_rows(key, anchor_index, block_order, block_count, cores, per_patch):
    per = BLOCK // cores
    live = jnp.arange(NSEL) < block_count[:, None]
    block = jnp.where(live, block_order[:, :NSEL], block_order[:, :1])
    patch = block // per_patch
    part = (patch % cores - lax.axis_index("pcol")) % cores
    rows = key.reshape(-1, per, key.shape[1])[part * per_patch + block % per_patch]
    held = (patch // cores == lax.axis_index("prow")) & (
        anchor_index == lax.axis_index("image"))[:, None]
    rows = jnp.where(held[..., None, None], rows, jnp.zeros_like(rows))
    return lax.psum(rows.reshape(len(block), NSEL * per, -1), ("image", "prow"))


def shards(
    latent, conv_weight, w_query, w_key, w_value, w_out, anchor_index, block_order, block_count
):
    tile_rows, tile_cols, _ = latent.shape[1:]
    cores, prows, images = (lax.axis_size(a) for a in ("pcol", "prow", "image"))
    anchors = anchor_index.shape[0]
    per_patch = tile_rows * tile_cols // BLOCK
    info = (anchors, images, cores, prows, per_patch)
    features, *parts = conv_norm(latent[0], halo(latent[0]), stage(conv_weight), cores)
    parts, *anchoring = lax.optimization_barrier((parts, anchor_index, block_count, block_order))
    anchor_index, block_count, block_order = anchoring
    table = Table.build(anchor_index, block_count, block_order[:, :NSEL])
    keys, queries = [parts[0]], list(parts)
    for s in range(1, cores):
        theirs = [None] * cores
        for t in [cores - s] + [t for t in range(cores) if t != cores - s]:
            theirs[t] = shifted(parts[t], "pcol", s)
        keys.append(theirs[cores - s])
        queries += theirs
    key = jnp.concatenate(keys, axis=0)
    every_image = anchors == images
    if every_image:
        mine, *offers = offer(info, table, key)
        offers = [mine] + [exchange(rows, "prow", s) for s, rows in enumerate(offers, 1)]
    plane = [exchange(key, "prow", s) for s in range(1, prows)]
    q, value, level = attend_own(info, table, queries, key, w_query, w_key, w_value)
    done = [(value, level)]
    if every_image:
        share = accept(info, table, offers)
        across = []
        for s in range(1, images):
            across.append(exchange(share, "image", s))
        local = jnp.concatenate(across, axis=0)
        sources = [local] + [exchange(local, "prow", s) for s in range(1, prows)]
    else:
        joined = anchor_rows(key, anchor_index, block_order, block_count, cores, per_patch)
        sources = [joined[anchor] for anchor in range(anchors)]
    if plane:
        done.append(attend_plane(info, table, q, plane, w_key, w_value))
    own, level, *sent = attend_anchors(info, table, q, sources, done, w_key, w_value, cores)
    received = [shifted(block, "pcol", cores - s) for s, block in enumerate(sent, 1)]
    attended = finish(own, level, received, w_out, cores)
    return features.reshape(latent.shape), attended.reshape(latent.shape)


def solution(mesh):
    tiled = P(("group", "image"), "prow", "pcol", None)
    return jax.shard_map(
        shards,
        mesh=mesh,
        in_specs=(tiled, P(), P(), P(), P(), P(), P("group"), P("group", None), P("group")),
        out_specs=(tiled, tiled),
        check_vma=False,
    )
```

```python
import functools

import jax
import jax.numpy as jnp
from jax import lax
from jax.experimental import pallas as pl
from jax.experimental.pallas import tpu as pltpu
from jax.sharding import PartitionSpec as P

HEAD_DIM = 64
BLOCK = 128
NSEL = 4
LANES = 128
SUBLANES = 8
ONES = 16
AHEAD = 2
EDGE_FLOPS = 4 * 10**9
STAGE_MIB = 46
F32 = jnp.float32
BF16 = jnp.bfloat16
MIB = 1 << 20


VMEM = pl.BlockSpec(memory_space=pltpu.VMEM)
ANY = pl.BlockSpec(memory_space=pl.ANY)
SMEM = pl.BlockSpec(memory_space=pltpu.SMEM)


def shape(*dims, dtype=BF16):
    return jax.ShapeDtypeStruct(dims, dtype)


def cost(flops, moved, exps=0):
    return pl.CostEstimate(flops=flops, bytes_accessed=moved, transcendentals=exps)


def grant(mib):
    return pltpu.CompilerParams(vmem_limit_bytes=mib * MIB)


def source_of(index, step, count):
    if count & (count - 1) == 0:
        return index ^ step
    return lax.rem(index + step, count) if not isinstance(index, int) else (index + step) % count


def target_of(index, step, count):
    if count & (count - 1) == 0:
        return index ^ step
    return lax.rem(index - step + count, count)


def step_of(index, source, count):
    if count & (count - 1) == 0:
        return index ^ source
    return lax.rem(source - index + count, count)


def exchange(block, axis, step):
    count = lax.axis_size(axis)
    return lax.ppermute(block, axis, [(source_of(i, step, count), i) for i in range(count)])


def shifted(block, axis, step):
    count = lax.axis_size(axis)
    return lax.ppermute(block, axis, [((i + step) % count, i) for i in range(count)])


def crossed(core, entry, prows):
    if prows != 4 or entry not in (1, 2):
        return entry
    return jnp.where(lax.rem(core, 2) == 1, 3 - entry, entry)


def gathered(block):
    prows, cores = lax.axis_size("prow"), lax.axis_size("pcol")
    if prows != 4:
        return [exchange(block, "prow", s) for s in range(1, prows)]

    def hop(rows, entry):
        return lax.ppermute(rows, ("prow", "pcol"), [
            ((p ^ (entry if c % 2 == 0 else 3 - entry)) * cores + c, p * cores + c)
            for p in range(prows) for c in range(cores)
        ])

    near, side = hop(block, 1), hop(block, 2)
    return [near, side, hop(near, 2)]


def edges_kernel(x_ref, first_ref, last_ref, top_ref, bottom_ref):
    rows, cols, _ = x_ref.shape
    part = 2 * SUBLANES
    first_ref[...] = x_ref[:, :part].astype(F32)[:, 0].astype(BF16)
    last_ref[...] = x_ref[:, cols - part:].astype(F32)[:, part - 1].astype(BF16)
    top_ref[...] = x_ref[0]
    bottom_ref[...] = x_ref[rows - 1]


def edges(cells):
    rows, cols, channels = cells.shape
    return pl.pallas_call(
        edges_kernel,
        out_shape=(shape(rows, channels),) * 2 + (shape(cols, channels),) * 2,
        in_specs=[VMEM],
        out_specs=(VMEM,) * 4,
        compiler_params=grant(8),
        cost_estimate=cost(EDGE_FLOPS, cells.nbytes),
        name="edges",
    )(cells)


def halo(cells):
    first, last, top, bottom = edges(cells)
    core, cores = lax.axis_index("pcol"), lax.axis_size("pcol")
    rows = lax.axis_size("prow")
    if cores == 2:
        other = shifted(jnp.where(core == 0, last, first), "pcol", 1)
        zero = jnp.zeros_like(other)
        left = jnp.where(core == 1, other, zero)
        right = jnp.where(core == 0, other, zero)
    else:
        left = lax.ppermute(last, "pcol", [(i, i + 1) for i in range(cores - 1)])
        right = lax.ppermute(first, "pcol", [(i + 1, i) for i in range(cores - 1)])
    low = jnp.concatenate([bottom, left[-1:], right[-1:]], axis=0)
    high = jnp.concatenate([top, left[:1], right[:1]], axis=0)
    odd = lax.rem(lax.axis_index("prow"), 2) == 1
    swaps = []
    for first in range(2):
        pairs = [(i, i + 1) for i in range(first, rows - 1, 2)]
        block = jnp.where(odd, high, low) if first == 0 else jnp.where(odd, low, high)
        swaps.append(lax.ppermute(block, "prow", pairs + [(j, i) for i, j in pairs]))
    above = jnp.where(odd, swaps[0], swaps[1])
    below = jnp.where(odd, swaps[1], swaps[0])
    return left, right, above, below


def stage_kernel(in_ref, out_ref, sem):
    copy = pltpu.make_async_copy(in_ref, out_ref, sem)
    copy.start()
    copy.wait()


def stage(array):
    return pl.pallas_call(
        stage_kernel,
        out_shape=shape(*array.shape),
        in_specs=[ANY],
        out_specs=VMEM,
        scratch_shapes=[pltpu.SemaphoreType.DMA],
        compiler_params=grant(STAGE_MIB),
        cost_estimate=cost(0, 2 * array.nbytes),
        name="stage",
    )(array)


def conv_kernel(rows, cols, cores, x_ref, left_ref, right_ref, above_ref, below_ref, w_ref, *refs):
    features_ref, *half_refs, shift0, shift1, shift2 = refs

    def silu(v):
        v = v.astype(F32)
        return (v / (1.0 + jnp.exp(-v))).astype(BF16).astype(F32)

    side = lax.broadcasted_iota(jnp.int32, (cols, x_ref.shape[1]), 0)
    for r in range(rows + 2):
        if r == 0 or r == rows + 1:
            ref = above_ref if r == 0 else below_ref
            cells, lcell, rcell = ref[:cols], ref[cols:cols + 1], ref[cols + 1:cols + 2]
        else:
            cells = x_ref[(r - 1) * cols:r * cols]
            lcell, rcell = left_ref[r - 1:r], right_ref[r - 1:r]
        cells, lcell, rcell = silu(cells), silu(lcell), silu(rcell)
        at = slice(r * cols, (r + 1) * cols)
        shift1[at] = cells.astype(BF16)
        shift0[at] = jnp.where(side == 0, lcell, pltpu.roll(cells, 1, 0)).astype(BF16)
        shift2[at] = jnp.where(side == cols - 1, rcell, pltpu.roll(cells, cols - 1, 0)).astype(BF16)
    total = x_ref[...].astype(F32)
    for a in range(3):
        for b, shift in enumerate((shift0, shift1, shift2)):
            total = total + jnp.dot(
                shift[a * cols:(a + rows) * cols], w_ref[a, b], preferred_element_type=F32
            )
    features = total.astype(BF16)
    features_ref[...] = features
    values = features.astype(F32)
    centered = values - jnp.mean(values, axis=-1, keepdims=True)
    spread = jnp.mean(centered * centered, axis=-1, keepdims=True)
    normed = (centered * lax.rsqrt(spread + 1e-05)).astype(BF16)
    core = lax.axis_index("pcol")
    per = BLOCK // cores
    for b in range(rows * cols // BLOCK):
        for h in range(cores):
            rows_of = normed[b * BLOCK + h * per:b * BLOCK + (h + 1) * per]
            for s, ref in enumerate(half_refs):
                @pl.when(lax.rem(core + s, cores) == h)
                def _():
                    ref[b * per:(b + 1) * per] = rows_of


def conv_norm(cells, sides, conv_weight, cores):
    rows, cols, channels = cells.shape
    tokens = rows * cols
    return pl.pallas_call(
        functools.partial(conv_kernel, rows, cols, cores),
        out_shape=(shape(tokens, channels),) + (shape(tokens // cores, channels),) * cores,
        in_specs=[VMEM] * 6,
        out_specs=(VMEM,) * (1 + cores),
        scratch_shapes=[pltpu.VMEM(((rows + 2) * cols, channels), BF16)] * 3,
        compiler_params=grant(24),
        cost_estimate=cost(18 * tokens * channels**2, 18 * channels**2, tokens * channels),
        name="conv_norm",
    )(cells.reshape(tokens, channels), *sides, conv_weight)


class Table:
    def __init__(self, ref, anchors, images):
        self.ref, self.anchors, self.images = ref, anchors, images
        self.every_image = anchors == images

    @staticmethod
    def build(anchor_index, block_count, order):
        return jnp.concatenate([anchor_index, block_count, order.reshape(-1)])

    def anchor_at(self, image):
        found = jnp.int32(0)
        for a in range(1, self.anchors):
            found = jnp.where(self.ref[a] == image, a, found)
        return found

    def count(self, anchor):
        return self.ref[self.anchors + anchor]

    def block(self, anchor, slot):
        return self.ref[2 * self.anchors + anchor * NSEL + slot]

    def own_times(self, step, group, cores, prows, per_patch):
        if not self.every_image:
            return jnp.float32(1.0)
        s, b = divmod(group, per_patch)
        core = lax.axis_index("pcol")
        patch = source_of(lax.axis_index("prow"), crossed(core, step, prows), prows) * cores
        block = (patch + lax.rem(core + s, cores)) * per_patch + b
        anchor = self.anchor_at(lax.axis_index("image"))
        times = jnp.float32(1.0)
        for slot in range(NSEL):
            hit = (slot < self.count(anchor)) & (self.block(anchor, slot) == block)
            times = jnp.where(hit, 2.0, times)
        return times

    def anchor_times(self, source, slot):
        if self.every_image:
            image = source_of(lax.axis_index("image"), source + 1, self.images)
            source = self.anchor_at(image)
        return jnp.where(slot < self.count(source), 1.0, 0.0).astype(F32)


def project(normed, times, wk_ref, wv_ref, k_scr, v_scr):
    keys, channels = normed.shape
    k = jnp.dot(normed, wk_ref[...], preferred_element_type=F32).astype(BF16)
    for pair in range(channels // LANES):
        k_scr[pair] = k[:, pair * LANES:(pair + 1) * LANES]
    v = jnp.dot(normed, wv_ref[...], preferred_element_type=F32).astype(BF16).T
    per = keys // len(times)
    lane = lax.broadcasted_iota(jnp.int32, (1, keys), 1)
    mult = jnp.full((1, keys), times[0], F32)
    for g in range(1, len(times)):
        mult = jnp.where(lane >= g * per, times[g], mult)
    v = v * mult.astype(BF16)
    ones = jnp.broadcast_to(mult, (ONES, keys)).astype(BF16)
    for head in range(channels // HEAD_DIM):
        v_scr[head, :HEAD_DIM] = v[head * HEAD_DIM:(head + 1) * HEAD_DIM]
        v_scr[head, HEAD_DIM:] = ones


def attend_heads(q_ref, k_scr, v_scr, out_ref, level_ref, width):
    zeros = jnp.zeros((HEAD_DIM, width), BF16)
    items = [
        (head, slice(at, at + width))
        for head in range(q_ref.shape[0] // HEAD_DIM)
        for at in range(0, q_ref.shape[1], width)
    ]

    def scores_of(head, cols):
        q = q_ref[head * HEAD_DIM:(head + 1) * HEAD_DIM, cols]
        q = jnp.concatenate([q, zeros] if head % 2 == 0 else [zeros, q], axis=0)
        return jnp.dot(k_scr[head // 2], q, preferred_element_type=F32)

    ahead = [scores_of(*item) for item in items[:AHEAD]]
    for n, (head, cols) in enumerate(items):
        scores = ahead.pop(0)
        if n + AHEAD < len(items):
            ahead.append(scores_of(*items[n + AHEAD]))
        peak = jnp.max(scores, axis=0, keepdims=True)
        probs = jnp.exp(scores - peak).astype(BF16)
        value = jnp.dot(v_scr[head], probs, preferred_element_type=F32)
        total = value[HEAD_DIM:HEAD_DIM + 1]
        out_ref[head * HEAD_DIM:(head + 1) * HEAD_DIM, cols] = (
            value[:HEAD_DIM] * (1.0 / total)
        ).astype(out_ref.dtype)
        level_ref[head, :, cols] = jnp.broadcast_to(peak + jnp.log(total), (SUBLANES, width))


def own_kernel(info, n_parts, table_ref, *refs):
    anchors, images, cores, prows, per_patch = info
    part_refs, key_ref = refs[:n_parts], refs[n_parts]
    wq_ref, wk_ref, wv_ref, q_ref, out_ref, level_ref, k_scr, v_scr = refs[n_parts + 1:]
    table = Table(table_ref, anchors, images)
    at = 0
    for ref in part_refs:
        q = jnp.dot(ref[...], wq_ref[...], preferred_element_type=F32).astype(BF16)
        q_ref[:, at:at + ref.shape[0]] = q.T * BF16(HEAD_DIM ** (-0.5))
        at += ref.shape[0]
    times = [table.own_times(0, g, cores, prows, per_patch) for g in range(cores * per_patch)]
    project(key_ref[...], times, wk_ref, wv_ref, k_scr, v_scr)
    attend_heads(q_ref, k_scr, v_scr, out_ref, level_ref, part_refs[0].shape[0] * cores)


def key_scratch(keys, channels):
    return [
        pltpu.VMEM((channels // LANES, keys, LANES), BF16),
        pltpu.VMEM((channels // HEAD_DIM, HEAD_DIM + ONES, keys), BF16),
    ]


def attend_cost(rows, keys, channels, extra=0):
    return cost(
        4 * keys * channels**2 + 16 * rows * keys * channels + extra,
        2 * channels * (2 * rows + keys),
        rows * keys * channels // HEAD_DIM,
    )


def attend_own(info, table, parts, key, w_query, w_key, w_value):
    size, channels = key.shape
    rows = sum(part.shape[0] for part in parts)
    return pl.pallas_call(
        functools.partial(own_kernel, info, len(parts)),
        out_shape=(
            shape(channels, rows), shape(channels, rows),
            shape(channels // HEAD_DIM, SUBLANES, rows, dtype=F32),
        ),
        in_specs=[SMEM] + [VMEM] * (len(parts) + 4),
        out_specs=(VMEM,) * 3,
        scratch_shapes=key_scratch(size, channels),
        compiler_params=grant(24),
        cost_estimate=attend_cost(rows, size, channels, 2 * rows * channels**2),
        name="attend_own",
    )(table, *parts, key, w_query, w_key, w_value)


def plane_kernel(info, tiles, table_ref, q_ref, *refs):
    anchors, images, cores, prows, per_patch = info
    key_refs = refs[:tiles]
    wk_ref, wv_ref, out_ref, level_ref, k_scr, v_scr = refs[tiles:]
    table = Table(table_ref, anchors, images)
    times = [
        table.own_times(t + 1, g, cores, prows, per_patch)
        for t in range(tiles) for g in range(cores * per_patch)
    ]
    normed = jnp.concatenate([ref[...] for ref in key_refs], axis=0)
    project(normed, times, wk_ref, wv_ref, k_scr, v_scr)
    attend_heads(q_ref, k_scr, v_scr, out_ref, level_ref, q_ref.shape[1] // cores)


def attend_plane(info, table, queries, keys, w_key, w_value):
    size, channels = keys[0].shape
    rows = queries.shape[1]
    return pl.pallas_call(
        functools.partial(plane_kernel, info, len(keys)),
        out_shape=(
            shape(channels, rows), shape(channels // HEAD_DIM, SUBLANES, rows, dtype=F32),
        ),
        in_specs=[SMEM] + [VMEM] * (len(keys) + 3),
        out_specs=(VMEM,) * 2,
        scratch_shapes=key_scratch(size * len(keys), channels),
        compiler_params=grant(24),
        cost_estimate=attend_cost(rows, size * len(keys), channels),
        name="attend_plane",
    )(table, queries, *keys, w_key, w_value)


def merge_head(parts, head, cols):
    rows = slice(head * HEAD_DIM, (head + 1) * HEAD_DIM)
    levels = [level(head, cols) for _, level in parts]
    peak = functools.reduce(jnp.maximum, levels)
    weights = [jnp.exp(level - peak) for level in levels]
    total = functools.reduce(jnp.add, weights)
    value = functools.reduce(
        jnp.add, [w * ref[rows, cols].astype(F32) for w, (ref, _) in zip(weights, parts)]
    )
    return value * (1.0 / total), peak + jnp.log(total)


def anchor_kernel(info, tiles, earlier, groups, table_ref, q_ref, *refs):
    anchors, images, _, prows, _ = info
    key_refs, refs = refs[:tiles], refs[tiles:]
    early_refs, refs = refs[:2 * earlier], refs[2 * earlier:]
    wk_ref, wv_ref, *out_refs = refs[:2 + groups + 1]
    out_scr, level_scr, k_scr, v_scr = refs[3 + groups:]
    own_ref, own_level_ref, *sent_refs = out_refs
    table = Table(table_ref, anchors, images)
    if table.every_image:
        each = NSEL // prows
        times = [
            table.anchor_times(s, source_of(lax.axis_index("prow"), t, prows) * each + slot)
            for t in range(tiles) for s in range(images - 1) for slot in range(each)
        ]
    else:
        times = [table.anchor_times(t, slot) for t in range(tiles) for slot in range(NSEL)]
    normed = jnp.concatenate([ref[...] for ref in key_refs], axis=0)
    project(normed, times, wk_ref, wv_ref, k_scr, v_scr)
    channels = q_ref.shape[0]
    width = q_ref.shape[1] // groups
    attend_heads(q_ref, k_scr, v_scr, out_scr, level_scr, width)
    pairs = list(zip(early_refs[::2], early_refs[1::2])) + [(out_scr, level_scr)]
    parts = [
        (ref, lambda head, cols, level=level: level[head, 0:1, cols]) for ref, level in pairs
    ]
    heads = channels // HEAD_DIM
    row = lax.broadcasted_iota(jnp.int32, (2 * SUBLANES, width), 0)
    for n in range(groups):
        cols = slice(n * width, (n + 1) * width)
        ref = own_ref if n == 0 else sent_refs[n - 1]
        levels = jnp.zeros((2 * SUBLANES, width), F32)
        for head in range(heads):
            value, level = merge_head(parts, head, cols)
            ref[head * HEAD_DIM:(head + 1) * HEAD_DIM] = value.astype(BF16)
            levels = jnp.where(row == head, level, levels)
        if n == 0:
            own_level_ref[...] = levels
        else:
            for term in range(3):
                high = levels.astype(BF16)
                at = channels + term * 2 * SUBLANES
                ref[at:at + 2 * SUBLANES] = high
                levels = levels - high.astype(F32)


def attend_anchors(info, table, queries, keys, earlier, w_key, w_value, groups):
    size, channels = keys[0].shape
    rows = queries.shape[1]
    width = rows // groups
    flat = [leaf for part in earlier for leaf in part]
    heads = channels // HEAD_DIM
    return pl.pallas_call(
        functools.partial(anchor_kernel, info, len(keys), len(earlier), groups),
        out_shape=(shape(channels, width), shape(2 * SUBLANES, width, dtype=F32))
        + (shape(channels + 6 * SUBLANES, width),) * (groups - 1),
        in_specs=[SMEM] + [VMEM] * (len(keys) + len(flat) + 3),
        out_specs=(VMEM,) * (1 + groups),
        scratch_shapes=[
            pltpu.VMEM((channels, rows), BF16), pltpu.VMEM((heads, SUBLANES, rows), F32),
        ] + key_scratch(size * len(keys), channels),
        compiler_params=grant(24),
        cost_estimate=attend_cost(rows, size * len(keys), channels),
        name="attend_anchors",
    )(table, queries, *keys, *flat, w_key, w_value)


def finish_kernel(cores, own_ref, level_ref, *refs):
    *received, w_ref, out_ref, merged = refs
    channels, tokens = own_ref.shape

    def row_of(ref, base, terms):
        def level(head, cols):
            return functools.reduce(jnp.add, [
                ref[base + t * 2 * SUBLANES:base + (t + 1) * 2 * SUBLANES].astype(F32)
                for t in range(terms)
            ])[head:head + 1]

        return level

    parts = [(own_ref, row_of(level_ref, 0, 1))]
    parts += [(ref, row_of(ref, channels, 3)) for ref in received]
    every = slice(0, tokens)
    for head in range(channels // HEAD_DIM):
        value, _ = merge_head(parts, head, every)
        merged[head * HEAD_DIM:(head + 1) * HEAD_DIM] = value.astype(BF16)
    out = lax.dot_general(
        merged[...], w_ref[...], (((0,), (0,)), ((), ())), preferred_element_type=F32
    ).astype(BF16)
    core = lax.axis_index("pcol")
    per = BLOCK // cores
    blocks = tokens // BLOCK
    for s in range(cores):
        for b in range(blocks):
            at = b * BLOCK + lax.rem(core + s, cores) * per
            out_ref[pl.ds(pl.multiple_of(at, per), per)] = out[
                (s * blocks + b) * per:(s * blocks + b + 1) * per
            ]


def finish(own, level, received, w_out, cores):
    channels, tokens = own.shape
    return pl.pallas_call(
        functools.partial(finish_kernel, cores),
        out_shape=shape(tokens, channels),
        in_specs=[VMEM] * (3 + len(received)),
        out_specs=VMEM,
        scratch_shapes=[pltpu.VMEM((channels, tokens), BF16)],
        compiler_params=grant(16),
        cost_estimate=cost(2 * tokens * channels**2, 2 * channels * (channels + 3 * tokens)),
        name="finish",
    )(own, level, *received, w_out)


def slot_place(table, anchor, slot, info):
    cores, per_patch = info[2], info[4]
    per = BLOCK // cores
    block = table.block(anchor, jnp.where(slot < table.count(anchor), slot, 0))
    patch, inner = lax.div(block, per_patch), lax.rem(block, per_patch)
    part = lax.rem(lax.rem(patch, cores) - lax.axis_index("pcol") + cores, cores)
    return lax.div(patch, cores), pl.multiple_of((part * per_patch + inner) * per, per)


def offer_kernel(info, table_ref, key_ref, *out_refs):
    anchors, images, cores, prows, _ = info
    table = Table(table_ref, anchors, images)
    anchor = table.anchor_at(lax.axis_index("image"))
    per, each = BLOCK // cores, NSEL // prows
    for step, ref in enumerate(out_refs):
        target = target_of(lax.axis_index("prow"), step, prows)
        for n in range(each):
            _, at = slot_place(table, anchor, target * each + n, info)
            ref[n * per:(n + 1) * per] = key_ref[pl.ds(at, per)]


def offer(info, table, key):
    rows = NSEL // info[3] * (BLOCK // info[2])
    return pl.pallas_call(
        functools.partial(offer_kernel, info),
        out_shape=(shape(rows, key.shape[1]),) * info[3],
        in_specs=[SMEM, VMEM],
        out_specs=(VMEM,) * info[3],
        compiler_params=grant(8),
        name="offer",
    )(table, key)


def accept_kernel(info, table_ref, *refs):
    anchors, images, cores, prows, _ = info
    *offers, out_ref = refs
    table = Table(table_ref, anchors, images)
    anchor = table.anchor_at(lax.axis_index("image"))
    prow = lax.axis_index("prow")
    per, each = BLOCK // cores, NSEL // prows
    for n in range(each):
        holder, _ = slot_place(table, anchor, prow * each + n, info)
        rows = slice(n * per, (n + 1) * per)
        for step, ref in enumerate(offers):
            @pl.when(step_of(prow, holder, prows) == step)
            def _():
                out_ref[rows] = ref[rows]


def accept(info, table, offers):
    return pl.pallas_call(
        functools.partial(accept_kernel, info),
        out_shape=shape(*offers[0].shape),
        in_specs=[SMEM] + [VMEM] * len(offers),
        out_specs=VMEM,
        compiler_params=grant(8),
        name="accept",
    )(table, *offers)


def anchor_rows(key, anchor_index, block_order, block_count, cores, per_patch):
    per = BLOCK // cores
    live = jnp.arange(NSEL) < block_count[:, None]
    block = jnp.where(live, block_order[:, :NSEL], block_order[:, :1])
    patch = block // per_patch
    part = (patch % cores - lax.axis_index("pcol")) % cores
    rows = key.reshape(-1, per, key.shape[1])[part * per_patch + block % per_patch]
    held = (patch // cores == lax.axis_index("prow")) & (
        anchor_index == lax.axis_index("image"))[:, None]
    rows = jnp.where(held[..., None, None], rows, jnp.zeros_like(rows))
    return lax.psum(rows.reshape(len(block), NSEL * per, -1), ("image", "prow"))


def shards(
    latent, conv_weight, w_query, w_key, w_value, w_out, anchor_index, block_order, block_count
):
    tile_rows, tile_cols, _ = latent.shape[1:]
    cores, prows, images = (lax.axis_size(a) for a in ("pcol", "prow", "image"))
    anchors = anchor_index.shape[0]
    per_patch = tile_rows * tile_cols // BLOCK
    info = (anchors, images, cores, prows, per_patch)
    features, *parts = conv_norm(latent[0], halo(latent[0]), stage(conv_weight), cores)
    parts, *anchoring = lax.optimization_barrier((parts, anchor_index, block_count, block_order))
    anchor_index, block_count, block_order = anchoring
    table = Table.build(anchor_index, block_count, block_order[:, :NSEL])
    keys, queries = [parts[0]], list(parts)
    for s in range(1, cores):
        theirs = [None] * cores
        for t in [cores - s] + [t for t in range(cores) if t != cores - s]:
            theirs[t] = shifted(parts[t], "pcol", s)
        keys.append(theirs[cores - s])
        queries += theirs
    key = jnp.concatenate(keys, axis=0)
    every_image = anchors == images
    if every_image:
        mine, *offers = offer(info, table, key)
        received = [mine]
        for s, rows in enumerate(offers, 1):
            received.append(exchange(rows, "prow", s))
    plane = gathered(key)
    q, value, level = attend_own(info, table, queries, key, w_query, w_key, w_value)
    done = [(value, level)]
    if every_image:
        share = accept(info, table, received)
        across = []
        for s in range(1, images):
            across.append(exchange(share, "image", s))
        local = jnp.concatenate(across, axis=0)
        sources = [local]
        for s in range(1, prows):
            sources.append(exchange(local, "prow", s))
    else:
        joined = anchor_rows(key, anchor_index, block_order, block_count, cores, per_patch)
        sources = [joined[anchor] for anchor in range(anchors)]
    if plane:
        done.append(attend_plane(info, table, q, plane, w_key, w_value))
    own, level, *sent = attend_anchors(info, table, q, sources, done, w_key, w_value, cores)
    received = [shifted(block, "pcol", cores - s) for s, block in enumerate(sent, 1)]
    attended = finish(own, level, received, w_out, cores)
    return features.reshape(latent.shape), attended.reshape(latent.shape)


def solution(mesh):
    tiled = P(("group", "image"), "prow", "pcol", None)
    return jax.shard_map(
        shards,
        mesh=mesh,
        in_specs=(tiled, P(), P(), P(), P(), P(), P("group"), P("group", None), P("group")),
        out_specs=(tiled, tiled),
        check_vma=False,
    )
```

```python
import functools

import jax
import jax.numpy as jnp
from jax import lax
from jax.experimental import pallas as pl
from jax.experimental.pallas import tpu as pltpu
from jax.sharding import PartitionSpec as P

HEAD_DIM = 64
BLOCK = 128
NSEL = 4
LANES = 128
SUBLANES = 8
ONES = 16
AHEAD = 2
EDGE_FLOPS = 4 * 10**9
STAGE_MIB = 46
F32 = jnp.float32
BF16 = jnp.bfloat16
MIB = 1 << 20


VMEM = pl.BlockSpec(memory_space=pltpu.VMEM)
ANY = pl.BlockSpec(memory_space=pl.ANY)
SMEM = pl.BlockSpec(memory_space=pltpu.SMEM)


def shape(*dims, dtype=BF16):
    return jax.ShapeDtypeStruct(dims, dtype)


def cost(flops, moved, exps=0):
    return pl.CostEstimate(flops=flops, bytes_accessed=moved, transcendentals=exps)


def grant(mib):
    return pltpu.CompilerParams(vmem_limit_bytes=mib * MIB)


def source_of(index, step, count):
    if count & (count - 1) == 0:
        return index ^ step
    return lax.rem(index + step, count) if not isinstance(index, int) else (index + step) % count


def target_of(index, step, count):
    if count & (count - 1) == 0:
        return index ^ step
    return lax.rem(index - step + count, count)


def step_of(index, source, count):
    if count & (count - 1) == 0:
        return index ^ source
    return lax.rem(source - index + count, count)


def exchange(block, axis, step):
    count = lax.axis_size(axis)
    return lax.ppermute(block, axis, [(source_of(i, step, count), i) for i in range(count)])


def shifted(block, axis, step):
    count = lax.axis_size(axis)
    return lax.ppermute(block, axis, [((i + step) % count, i) for i in range(count)])


def crossed(core, entry, prows):
    if prows != 4 or entry not in (1, 2):
        return entry
    return jnp.where(lax.rem(core, 2) == 1, 3 - entry, entry)


def gathered(block):
    prows, cores = lax.axis_size("prow"), lax.axis_size("pcol")
    if prows != 4:
        return [exchange(block, "prow", s) for s in range(1, prows)]

    def hop(rows, entry):
        return lax.ppermute(rows, ("prow", "pcol"), [
            ((p ^ (entry if c % 2 == 0 else 3 - entry)) * cores + c, p * cores + c)
            for p in range(prows) for c in range(cores)
        ])

    near, side = hop(block, 1), hop(block, 2)
    return [near, side, hop(near, 2)]


def edges_kernel(x_ref, first_ref, last_ref, top_ref, bottom_ref):
    rows, cols, _ = x_ref.shape
    part = 2 * SUBLANES
    first_ref[...] = x_ref[:, :part].astype(F32)[:, 0].astype(BF16)
    last_ref[...] = x_ref[:, cols - part:].astype(F32)[:, part - 1].astype(BF16)
    top_ref[...] = x_ref[0]
    bottom_ref[...] = x_ref[rows - 1]


def edges(cells):
    rows, cols, channels = cells.shape
    return pl.pallas_call(
        edges_kernel,
        out_shape=(shape(rows, channels),) * 2 + (shape(cols, channels),) * 2,
        in_specs=[VMEM],
        out_specs=(VMEM,) * 4,
        compiler_params=grant(8),
        cost_estimate=cost(EDGE_FLOPS, cells.nbytes),
        name="edges",
    )(cells)


def halo(cells):
    core, cores = lax.axis_index("pcol"), lax.axis_size("pcol")
    prow, rows = lax.axis_index("prow"), lax.axis_size("prow")
    cells, left_core, right_core, upper, odd, second, third = lax.optimization_barrier((
        cells, core == 0, core == 1, prow < 2, lax.rem(prow, 2) == 1, prow == 1, prow == 2
    ))
    first, last, top, bottom = edges(cells)
    if cores == 2:
        other = shifted(jnp.where(left_core, last, first), "pcol", 1)
        zero = jnp.zeros_like(other)
        left = jnp.where(right_core, other, zero)
        right = jnp.where(left_core, other, zero)
    else:
        left = lax.ppermute(last, "pcol", [(i, i + 1) for i in range(cores - 1)])
        right = lax.ppermute(first, "pcol", [(i + 1, i) for i in range(cores - 1)])
    low = jnp.concatenate([bottom, left[-1:], right[-1:]], axis=0)
    high = jnp.concatenate([top, left[:1], right[:1]], axis=0)
    if rows != 4:
        above = lax.ppermute(low, "prow", [(i, i + 1) for i in range(rows - 1)])
        below = lax.ppermute(high, "prow", [(i + 1, i) for i in range(rows - 1)])
        return left, right, above, below
    near = exchange(jnp.concatenate([low, high], axis=0), "prow", 1)
    low, high = near[:len(low)], near[len(low):]
    far = exchange(jnp.where(upper, low, high), "prow", 2)
    zero = jnp.zeros_like(far)
    above = jnp.where(odd, low, jnp.where(third, far, zero))
    below = jnp.where(odd, jnp.where(second, far, zero), high)
    return left, right, above, below


def stage_kernel(row, in_ref, out_ref, sem):
    copy = pltpu.make_async_copy(in_ref.at[row], out_ref, sem)
    copy.start()
    copy.wait()


def stage(weights, row):
    taps = weights[row]
    return pl.pallas_call(
        functools.partial(stage_kernel, row),
        out_shape=shape(*taps.shape),
        in_specs=[ANY],
        out_specs=VMEM,
        scratch_shapes=[pltpu.SemaphoreType.DMA],
        compiler_params=grant(STAGE_MIB),
        cost_estimate=cost(0, 2 * taps.nbytes),
        name="stage",
    )(weights)


def conv_kernel(rows, cols, cores, x_ref, left_ref, right_ref, above_ref, below_ref, *refs):
    taps, anchoring, refs = refs[:3], refs[3:6], refs[6:]
    table_ref, features_ref, *half_refs, shift0, shift1, shift2 = refs

    Table.fill(table_ref, *anchoring)

    def silu(v):
        v = v.astype(F32)
        return (v / (1.0 + jnp.exp(-v))).astype(BF16).astype(F32)

    side = lax.broadcasted_iota(jnp.int32, (cols, x_ref.shape[1]), 0)
    for r in range(rows + 2):
        if r == 0 or r == rows + 1:
            ref = above_ref if r == 0 else below_ref
            cells, lcell, rcell = ref[:cols], ref[cols:cols + 1], ref[cols + 1:cols + 2]
        else:
            cells = x_ref[(r - 1) * cols:r * cols]
            lcell, rcell = left_ref[r - 1:r], right_ref[r - 1:r]
        cells, lcell, rcell = silu(cells), silu(lcell), silu(rcell)
        at = slice(r * cols, (r + 1) * cols)
        shift1[at] = cells.astype(BF16)
        shift0[at] = jnp.where(side == 0, lcell, pltpu.roll(cells, 1, 0)).astype(BF16)
        shift2[at] = jnp.where(side == cols - 1, rcell, pltpu.roll(cells, cols - 1, 0)).astype(BF16)
    total = x_ref[...].astype(F32)
    for a in range(3):
        for b, shift in enumerate((shift0, shift1, shift2)):
            total = total + jnp.dot(
                shift[a * cols:(a + rows) * cols], taps[a][b], preferred_element_type=F32
            )
    features = total.astype(BF16)
    features_ref[...] = features
    values = features.astype(F32)
    centered = values - jnp.mean(values, axis=-1, keepdims=True)
    spread = jnp.mean(centered * centered, axis=-1, keepdims=True)
    normed = (centered * lax.rsqrt(spread + 1e-05)).astype(BF16)
    core = lax.axis_index("pcol")
    per = BLOCK // cores
    for b in range(rows * cols // BLOCK):
        for h in range(cores):
            rows_of = normed[b * BLOCK + h * per:b * BLOCK + (h + 1) * per]
            for s, ref in enumerate(half_refs):
                @pl.when(lax.rem(core + s, cores) == h)
                def _():
                    ref[b * per:(b + 1) * per] = rows_of


def conv_norm(cells, sides, taps, anchoring, cores):
    rows, cols, channels = cells.shape
    tokens = rows * cols
    return pl.pallas_call(
        functools.partial(conv_kernel, rows, cols, cores),
        out_shape=(
            shape(anchoring[0].shape[0] * (2 + NSEL), dtype=jnp.int32), shape(tokens, channels),
        ) + (shape(tokens // cores, channels),) * cores,
        in_specs=[VMEM] * 8 + [SMEM] * 3,
        out_specs=(SMEM,) + (VMEM,) * (1 + cores),
        scratch_shapes=[pltpu.VMEM(((rows + 2) * cols, channels), BF16)] * 3,
        compiler_params=grant(24),
        cost_estimate=cost(18 * tokens * channels**2, 18 * channels**2, tokens * channels),
        name="conv_norm",
    )(cells.reshape(tokens, channels), *sides, *taps, *anchoring)


class Table:
    def __init__(self, ref, anchors, images):
        self.ref, self.anchors, self.images = ref, anchors, images
        self.every_image = anchors == images

    @staticmethod
    def fill(ref, index_ref, count_ref, order_ref):
        anchors = index_ref.shape[0]
        for a in range(anchors):
            ref[a] = index_ref[a]
            ref[anchors + a] = count_ref[a]
            for slot in range(NSEL):
                ref[2 * anchors + a * NSEL + slot] = order_ref[a, slot]

    def anchor_at(self, image):
        found = jnp.int32(0)
        for a in range(1, self.anchors):
            found = jnp.where(self.ref[a] == image, a, found)
        return found

    def count(self, anchor):
        return self.ref[self.anchors + anchor]

    def block(self, anchor, slot):
        return self.ref[2 * self.anchors + anchor * NSEL + slot]

    def own_times(self, step, group, cores, prows, per_patch):
        if not self.every_image:
            return jnp.float32(1.0)
        s, b = divmod(group, per_patch)
        core = lax.axis_index("pcol")
        patch = source_of(lax.axis_index("prow"), crossed(core, step, prows), prows) * cores
        block = (patch + lax.rem(core + s, cores)) * per_patch + b
        anchor = self.anchor_at(lax.axis_index("image"))
        times = jnp.float32(1.0)
        for slot in range(NSEL):
            hit = (slot < self.count(anchor)) & (self.block(anchor, slot) == block)
            times = jnp.where(hit, 2.0, times)
        return times

    def anchor_times(self, source, slot):
        if self.every_image:
            image = source_of(lax.axis_index("image"), source + 1, self.images)
            source = self.anchor_at(image)
        return jnp.where(slot < self.count(source), 1.0, 0.0).astype(F32)


def project(normed, times, wk_ref, wv_ref, k_scr, v_scr):
    keys, channels = normed.shape
    k = jnp.dot(normed, wk_ref[...], preferred_element_type=F32).astype(BF16)
    for pair in range(channels // LANES):
        k_scr[pair] = k[:, pair * LANES:(pair + 1) * LANES]
    v = jnp.dot(normed, wv_ref[...], preferred_element_type=F32).astype(BF16).T
    per = keys // len(times)
    lane = lax.broadcasted_iota(jnp.int32, (1, keys), 1)
    mult = jnp.full((1, keys), times[0], F32)
    for g in range(1, len(times)):
        mult = jnp.where(lane >= g * per, times[g], mult)
    v = v * mult.astype(BF16)
    ones = jnp.broadcast_to(mult, (ONES, keys)).astype(BF16)
    for head in range(channels // HEAD_DIM):
        v_scr[head, :HEAD_DIM] = v[head * HEAD_DIM:(head + 1) * HEAD_DIM]
        v_scr[head, HEAD_DIM:] = ones


def attend_heads(q_ref, k_scr, v_scr, out_ref, level_ref, width):
    zeros = jnp.zeros((HEAD_DIM, width), BF16)
    items = [
        (head, slice(at, at + width))
        for head in range(q_ref.shape[0] // HEAD_DIM)
        for at in range(0, q_ref.shape[1], width)
    ]

    def scores_of(head, cols):
        q = q_ref[head * HEAD_DIM:(head + 1) * HEAD_DIM, cols]
        q = jnp.concatenate([q, zeros] if head % 2 == 0 else [zeros, q], axis=0)
        return jnp.dot(k_scr[head // 2], q, preferred_element_type=F32)

    ahead = [scores_of(*item) for item in items[:AHEAD]]
    for n, (head, cols) in enumerate(items):
        scores = ahead.pop(0)
        if n + AHEAD < len(items):
            ahead.append(scores_of(*items[n + AHEAD]))
        peak = jnp.max(scores, axis=0, keepdims=True)
        probs = jnp.exp(scores - peak).astype(BF16)
        value = jnp.dot(v_scr[head], probs, preferred_element_type=F32)
        total = value[HEAD_DIM:HEAD_DIM + 1]
        out_ref[head * HEAD_DIM:(head + 1) * HEAD_DIM, cols] = (
            value[:HEAD_DIM] * (1.0 / total)
        ).astype(out_ref.dtype)
        level_ref[head, :, cols] = jnp.broadcast_to(peak + jnp.log(total), (SUBLANES, width))


def own_kernel(info, n_parts, table_ref, *refs):
    anchors, images, cores, prows, per_patch = info
    part_refs, key_ref = refs[:n_parts], refs[n_parts]
    wq_ref, wk_ref, wv_ref, q_ref, out_ref, level_ref, k_scr, v_scr = refs[n_parts + 1:]
    table = Table(table_ref, anchors, images)
    at = 0
    for ref in part_refs:
        q = jnp.dot(ref[...], wq_ref[...], preferred_element_type=F32).astype(BF16)
        q_ref[:, at:at + ref.shape[0]] = q.T * BF16(HEAD_DIM ** (-0.5))
        at += ref.shape[0]
    times = [table.own_times(0, g, cores, prows, per_patch) for g in range(cores * per_patch)]
    project(key_ref[...], times, wk_ref, wv_ref, k_scr, v_scr)
    attend_heads(q_ref, k_scr, v_scr, out_ref, level_ref, part_refs[0].shape[0] * cores)


def key_scratch(keys, channels):
    return [
        pltpu.VMEM((channels // LANES, keys, LANES), BF16),
        pltpu.VMEM((channels // HEAD_DIM, HEAD_DIM + ONES, keys), BF16),
    ]


def attend_cost(rows, keys, channels, extra=0):
    return cost(
        4 * keys * channels**2 + 16 * rows * keys * channels + extra,
        2 * channels * (2 * rows + keys),
        rows * keys * channels // HEAD_DIM,
    )


def attend_own(info, table, parts, key, w_query, w_key, w_value):
    size, channels = key.shape
    rows = sum(part.shape[0] for part in parts)
    return pl.pallas_call(
        functools.partial(own_kernel, info, len(parts)),
        out_shape=(
            shape(channels, rows), shape(channels, rows),
            shape(channels // HEAD_DIM, SUBLANES, rows, dtype=F32),
        ),
        in_specs=[SMEM] + [VMEM] * (len(parts) + 4),
        out_specs=(VMEM,) * 3,
        scratch_shapes=key_scratch(size, channels),
        compiler_params=grant(24),
        cost_estimate=attend_cost(rows, size, channels, 2 * rows * channels**2),
        name="attend_own",
    )(table, *parts, key, w_query, w_key, w_value)


def plane_kernel(info, tiles, table_ref, q_ref, *refs):
    anchors, images, cores, prows, per_patch = info
    key_refs = refs[:tiles]
    wk_ref, wv_ref, out_ref, level_ref, k_scr, v_scr = refs[tiles:]
    table = Table(table_ref, anchors, images)
    times = [
        table.own_times(t + 1, g, cores, prows, per_patch)
        for t in range(tiles) for g in range(cores * per_patch)
    ]
    normed = jnp.concatenate([ref[...] for ref in key_refs], axis=0)
    project(normed, times, wk_ref, wv_ref, k_scr, v_scr)
    attend_heads(q_ref, k_scr, v_scr, out_ref, level_ref, q_ref.shape[1] // cores)


def attend_plane(info, table, queries, keys, w_key, w_value):
    size, channels = keys[0].shape
    rows = queries.shape[1]
    return pl.pallas_call(
        functools.partial(plane_kernel, info, len(keys)),
        out_shape=(
            shape(channels, rows), shape(channels // HEAD_DIM, SUBLANES, rows, dtype=F32),
        ),
        in_specs=[SMEM] + [VMEM] * (len(keys) + 3),
        out_specs=(VMEM,) * 2,
        scratch_shapes=key_scratch(size * len(keys), channels),
        compiler_params=grant(24),
        cost_estimate=attend_cost(rows, size * len(keys), channels),
        name="attend_plane",
    )(table, queries, *keys, w_key, w_value)


def merge_head(parts, head, cols):
    rows = slice(head * HEAD_DIM, (head + 1) * HEAD_DIM)
    levels = [level(head, cols) for _, level in parts]
    peak = functools.reduce(jnp.maximum, levels)
    weights = [jnp.exp(level - peak) for level in levels]
    total = functools.reduce(jnp.add, weights)
    value = functools.reduce(
        jnp.add, [w * ref[rows, cols].astype(F32) for w, (ref, _) in zip(weights, parts)]
    )
    return value * (1.0 / total), peak + jnp.log(total)


def anchor_kernel(info, tiles, earlier, groups, table_ref, q_ref, *refs):
    anchors, images, _, prows, _ = info
    key_refs, refs = refs[:tiles], refs[tiles:]
    early_refs, refs = refs[:2 * earlier], refs[2 * earlier:]
    wk_ref, wv_ref, *out_refs = refs[:2 + groups + 1]
    out_scr, level_scr, k_scr, v_scr = refs[3 + groups:]
    own_ref, own_level_ref, *sent_refs = out_refs
    table = Table(table_ref, anchors, images)
    if table.every_image:
        each = NSEL // prows
        times = [
            table.anchor_times(s, source_of(lax.axis_index("prow"), t, prows) * each + slot)
            for t in range(tiles) for s in range(images - 1) for slot in range(each)
        ]
    else:
        times = [table.anchor_times(t, slot) for t in range(tiles) for slot in range(NSEL)]
    normed = jnp.concatenate([ref[...] for ref in key_refs], axis=0)
    project(normed, times, wk_ref, wv_ref, k_scr, v_scr)
    channels = q_ref.shape[0]
    width = q_ref.shape[1] // groups
    attend_heads(q_ref, k_scr, v_scr, out_scr, level_scr, width)
    pairs = list(zip(early_refs[::2], early_refs[1::2])) + [(out_scr, level_scr)]
    parts = [
        (ref, lambda head, cols, level=level: level[head, 0:1, cols]) for ref, level in pairs
    ]
    heads = channels // HEAD_DIM
    row = lax.broadcasted_iota(jnp.int32, (2 * SUBLANES, width), 0)
    for n in range(groups):
        cols = slice(n * width, (n + 1) * width)
        ref = own_ref if n == 0 else sent_refs[n - 1]
        levels = jnp.zeros((2 * SUBLANES, width), F32)
        for head in range(heads):
            value, level = merge_head(parts, head, cols)
            ref[head * HEAD_DIM:(head + 1) * HEAD_DIM] = value.astype(BF16)
            levels = jnp.where(row == head, level, levels)
        if n == 0:
            own_level_ref[...] = levels
        else:
            for term in range(3):
                high = levels.astype(BF16)
                at = channels + term * 2 * SUBLANES
                ref[at:at + 2 * SUBLANES] = high
                levels = levels - high.astype(F32)


def attend_anchors(info, table, queries, keys, earlier, w_key, w_value, groups):
    size, channels = keys[0].shape
    rows = queries.shape[1]
    width = rows // groups
    flat = [leaf for part in earlier for leaf in part]
    heads = channels // HEAD_DIM
    return pl.pallas_call(
        functools.partial(anchor_kernel, info, len(keys), len(earlier), groups),
        out_shape=(shape(channels, width), shape(2 * SUBLANES, width, dtype=F32))
        + (shape(channels + 6 * SUBLANES, width),) * (groups - 1),
        in_specs=[SMEM] + [VMEM] * (len(keys) + len(flat) + 3),
        out_specs=(VMEM,) * (1 + groups),
        scratch_shapes=[
            pltpu.VMEM((channels, rows), BF16), pltpu.VMEM((heads, SUBLANES, rows), F32),
        ] + key_scratch(size * len(keys), channels),
        compiler_params=grant(24),
        cost_estimate=attend_cost(rows, size * len(keys), channels),
        name="attend_anchors",
    )(table, queries, *keys, *flat, w_key, w_value)


def finish_kernel(cores, own_ref, level_ref, *refs):
    *received, w_ref, out_ref, merged = refs
    channels, tokens = own_ref.shape

    def row_of(ref, base, terms):
        def level(head, cols):
            return functools.reduce(jnp.add, [
                ref[base + t * 2 * SUBLANES:base + (t + 1) * 2 * SUBLANES].astype(F32)
                for t in range(terms)
            ])[head:head + 1]

        return level

    parts = [(own_ref, row_of(level_ref, 0, 1))]
    parts += [(ref, row_of(ref, channels, 3)) for ref in received]
    every = slice(0, tokens)
    for head in range(channels // HEAD_DIM):
        value, _ = merge_head(parts, head, every)
        merged[head * HEAD_DIM:(head + 1) * HEAD_DIM] = value.astype(BF16)
    out = lax.dot_general(
        merged[...], w_ref[...], (((0,), (0,)), ((), ())), preferred_element_type=F32
    ).astype(BF16)
    core = lax.axis_index("pcol")
    per = BLOCK // cores
    blocks = tokens // BLOCK
    for s in range(cores):
        for b in range(blocks):
            at = b * BLOCK + lax.rem(core + s, cores) * per
            out_ref[pl.ds(pl.multiple_of(at, per), per)] = out[
                (s * blocks + b) * per:(s * blocks + b + 1) * per
            ]


def finish(own, level, received, w_out, cores):
    channels, tokens = own.shape
    return pl.pallas_call(
        functools.partial(finish_kernel, cores),
        out_shape=shape(tokens, channels),
        in_specs=[VMEM] * (3 + len(received)),
        out_specs=VMEM,
        scratch_shapes=[pltpu.VMEM((channels, tokens), BF16)],
        compiler_params=grant(16),
        cost_estimate=cost(2 * tokens * channels**2, 2 * channels * (channels + 3 * tokens)),
        name="finish",
    )(own, level, *received, w_out)


def slot_place(table, anchor, slot, info):
    cores, per_patch = info[2], info[4]
    per = BLOCK // cores
    block = table.block(anchor, jnp.where(slot < table.count(anchor), slot, 0))
    patch, inner = lax.div(block, per_patch), lax.rem(block, per_patch)
    part = lax.rem(lax.rem(patch, cores) - lax.axis_index("pcol") + cores, cores)
    return lax.div(patch, cores), pl.multiple_of((part * per_patch + inner) * per, per)


def offer_kernel(info, table_ref, key_ref, *out_refs):
    anchors, images, cores, prows, _ = info
    table = Table(table_ref, anchors, images)
    anchor = table.anchor_at(lax.axis_index("image"))
    per, each = BLOCK // cores, NSEL // prows
    for step, ref in enumerate(out_refs):
        target = target_of(lax.axis_index("prow"), step, prows)
        for n in range(each):
            _, at = slot_place(table, anchor, target * each + n, info)
            ref[n * per:(n + 1) * per] = key_ref[pl.ds(at, per)]


def offer(info, table, key):
    rows = NSEL // info[3] * (BLOCK // info[2])
    return pl.pallas_call(
        functools.partial(offer_kernel, info),
        out_shape=(shape(rows, key.shape[1]),) * info[3],
        in_specs=[SMEM, VMEM],
        out_specs=(VMEM,) * info[3],
        compiler_params=grant(8),
        name="offer",
    )(table, key)


def accept_kernel(info, table_ref, *refs):
    anchors, images, cores, prows, _ = info
    *offers, out_ref = refs
    table = Table(table_ref, anchors, images)
    anchor = table.anchor_at(lax.axis_index("image"))
    prow = lax.axis_index("prow")
    per, each = BLOCK // cores, NSEL // prows
    for n in range(each):
        holder, _ = slot_place(table, anchor, prow * each + n, info)
        rows = slice(n * per, (n + 1) * per)
        for step, ref in enumerate(offers):
            @pl.when(step_of(prow, holder, prows) == step)
            def _():
                out_ref[rows] = ref[rows]


def accept(info, table, offers):
    return pl.pallas_call(
        functools.partial(accept_kernel, info),
        out_shape=shape(*offers[0].shape),
        in_specs=[SMEM] + [VMEM] * len(offers),
        out_specs=VMEM,
        compiler_params=grant(8),
        name="accept",
    )(table, *offers)


def anchor_rows(key, anchor_index, block_order, block_count, cores, per_patch):
    per = BLOCK // cores
    live = jnp.arange(NSEL) < block_count[:, None]
    block = jnp.where(live, block_order[:, :NSEL], block_order[:, :1])
    patch = block // per_patch
    part = (patch % cores - lax.axis_index("pcol")) % cores
    rows = key.reshape(-1, per, key.shape[1])[part * per_patch + block % per_patch]
    held = (patch // cores == lax.axis_index("prow")) & (
        anchor_index == lax.axis_index("image"))[:, None]
    rows = jnp.where(held[..., None, None], rows, jnp.zeros_like(rows))
    return lax.psum(rows.reshape(len(block), NSEL * per, -1), ("image", "prow"))


def shards(
    latent, conv_weight, w_query, w_key, w_value, w_out, anchor_index, block_order, block_count
):
    tile_rows, tile_cols, _ = latent.shape[1:]
    cores, prows, images = (lax.axis_size(a) for a in ("pcol", "prow", "image"))
    anchors = anchor_index.shape[0]
    per_patch = tile_rows * tile_cols // BLOCK
    info = (anchors, images, cores, prows, per_patch)
    taps = [stage(conv_weight, row) for row in range(3)]
    table, features, *parts = conv_norm(
        latent[0], halo(latent[0]), taps, (anchor_index, block_count, block_order), cores
    )
    keys, queries = [parts[0]], list(parts)
    for s in range(1, cores):
        theirs = [None] * cores
        for t in [cores - s] + [t for t in range(cores) if t != cores - s]:
            theirs[t] = shifted(parts[t], "pcol", s)
        keys.append(theirs[cores - s])
        queries += theirs
    key = jnp.concatenate(keys, axis=0)
    every_image = anchors == images
    if every_image:
        mine, *offers = offer(info, table, key)
        received = [mine]
        for s, rows in enumerate(offers, 1):
            received.append(exchange(rows, "prow", s))
    plane = gathered(key)
    q, value, level = attend_own(info, table, queries, key, w_query, w_key, w_value)
    done = [(value, level)]
    if every_image:
        share = accept(info, table, received)
        across = []
        for s in range(1, images):
            across.append(exchange(share, "image", s))
        local = jnp.concatenate(across, axis=0)
        sources = [local]
        for s in range(1, prows):
            sources.append(exchange(local, "prow", s))
    else:
        joined = anchor_rows(key, anchor_index, block_order, block_count, cores, per_patch)
        sources = [joined[anchor] for anchor in range(anchors)]
    if plane:
        done.append(attend_plane(info, table, q, plane, w_key, w_value))
    own, level, *sent = attend_anchors(info, table, q, sources, done, w_key, w_value, cores)
    received = [shifted(block, "pcol", cores - s) for s, block in enumerate(sent, 1)]
    attended = finish(own, level, received, w_out, cores)
    return features.reshape(latent.shape), attended.reshape(latent.shape)


def solution(mesh):
    tiled = P(("group", "image"), "prow", "pcol", None)
    return jax.shard_map(
        shards,
        mesh=mesh,
        in_specs=(tiled, P(), P(), P(), P(), P(), P("group"), P("group", None), P("group")),
        out_specs=(tiled, tiled),
        check_vma=False,
    )
```

```python
import functools

import jax
import jax.numpy as jnp
from jax import lax
from jax.experimental import pallas as pl
from jax.experimental.pallas import tpu as pltpu
from jax.sharding import PartitionSpec as P

HEAD_DIM = 64
BLOCK = 128
NSEL = 4
LANES = 128
SUBLANES = 8
ONES = 16
AHEAD = 2
EDGE_FLOPS = 4 * 10**9
STAGE_MIB = 46
F32 = jnp.float32
BF16 = jnp.bfloat16
MIB = 1 << 20


VMEM = pl.BlockSpec(memory_space=pltpu.VMEM)
ANY = pl.BlockSpec(memory_space=pl.ANY)
SMEM = pl.BlockSpec(memory_space=pltpu.SMEM)


def shape(*dims, dtype=BF16):
    return jax.ShapeDtypeStruct(dims, dtype)


def cost(flops, moved, exps=0):
    return pl.CostEstimate(flops=flops, bytes_accessed=moved, transcendentals=exps)


def grant(mib):
    return pltpu.CompilerParams(vmem_limit_bytes=mib * MIB)


def source_of(index, step, count):
    if count & (count - 1) == 0:
        return index ^ step
    return lax.rem(index + step, count) if not isinstance(index, int) else (index + step) % count


def target_of(index, step, count):
    if count & (count - 1) == 0:
        return index ^ step
    return lax.rem(index - step + count, count)


def step_of(index, source, count):
    if count & (count - 1) == 0:
        return index ^ source
    return lax.rem(source - index + count, count)


def exchange(block, axis, step):
    count = lax.axis_size(axis)
    return lax.ppermute(block, axis, [(source_of(i, step, count), i) for i in range(count)])


def shifted(block, axis, step):
    count = lax.axis_size(axis)
    return lax.ppermute(block, axis, [((i + step) % count, i) for i in range(count)])


def crossed(core, entry, prows):
    if prows != 4 or entry not in (1, 2):
        return entry
    return jnp.where(lax.rem(core, 2) == 1, 3 - entry, entry)


def gathered(block):
    prows, cores = lax.axis_size("prow"), lax.axis_size("pcol")
    if prows != 4:
        return [exchange(block, "prow", s) for s in range(1, prows)]

    def hop(rows, entry):
        return lax.ppermute(rows, ("prow", "pcol"), [
            ((p ^ (entry if c % 2 == 0 else 3 - entry)) * cores + c, p * cores + c)
            for p in range(prows) for c in range(cores)
        ])

    near, side = hop(block, 1), hop(block, 2)
    return [near, side, hop(near, 2)]


def edges_kernel(x_ref, first_ref, last_ref, top_ref, bottom_ref):
    rows, cols, _ = x_ref.shape
    part = 2 * SUBLANES
    first_ref[...] = x_ref[:, :part].astype(F32)[:, 0].astype(BF16)
    last_ref[...] = x_ref[:, cols - part:].astype(F32)[:, part - 1].astype(BF16)
    top_ref[...] = x_ref[0]
    bottom_ref[...] = x_ref[rows - 1]


def edges(cells):
    rows, cols, channels = cells.shape
    return pl.pallas_call(
        edges_kernel,
        out_shape=(shape(rows, channels),) * 2 + (shape(cols, channels),) * 2,
        in_specs=[VMEM],
        out_specs=(VMEM,) * 4,
        compiler_params=grant(8),
        cost_estimate=cost(EDGE_FLOPS, cells.nbytes),
        name="edges",
    )(cells)


def halo(cells):
    first, last, top, bottom = edges(cells)
    core, cores = lax.axis_index("pcol"), lax.axis_size("pcol")
    rows = lax.axis_size("prow")
    if cores == 2:
        other = shifted(jnp.where(core == 0, last, first), "pcol", 1)
        zero = jnp.zeros_like(other)
        left = jnp.where(core == 1, other, zero)
        right = jnp.where(core == 0, other, zero)
    else:
        left = lax.ppermute(last, "pcol", [(i, i + 1) for i in range(cores - 1)])
        right = lax.ppermute(first, "pcol", [(i + 1, i) for i in range(cores - 1)])
    low = jnp.concatenate([bottom, left[-1:], right[-1:]], axis=0)
    high = jnp.concatenate([top, left[:1], right[:1]], axis=0)
    odd = lax.rem(lax.axis_index("prow"), 2) == 1
    swaps = []
    for first in range(2):
        pairs = [(i, i + 1) for i in range(first, rows - 1, 2)]
        block = jnp.where(odd, high, low) if first == 0 else jnp.where(odd, low, high)
        swaps.append(lax.ppermute(block, "prow", pairs + [(j, i) for i, j in pairs]))
    above = jnp.where(odd, swaps[0], swaps[1])
    below = jnp.where(odd, swaps[1], swaps[0])
    return left, right, above, below


def stage_kernel(in_ref, out_ref, sem):
    copy = pltpu.make_async_copy(in_ref, out_ref, sem)
    copy.start()
    copy.wait()


def stage(array):
    return pl.pallas_call(
        stage_kernel,
        out_shape=shape(*array.shape),
        in_specs=[ANY],
        out_specs=VMEM,
        scratch_shapes=[pltpu.SemaphoreType.DMA],
        compiler_params=grant(STAGE_MIB),
        cost_estimate=cost(0, 2 * array.nbytes),
        name="stage",
    )(array)


def conv_kernel(rows, cols, cores, x_ref, left_ref, right_ref, above_ref, below_ref, w_ref, *refs):
    features_ref, *half_refs, shift0, shift1, shift2 = refs

    def silu(v):
        v = v.astype(F32)
        return (v / (1.0 + jnp.exp(-v))).astype(BF16).astype(F32)

    side = lax.broadcasted_iota(jnp.int32, (cols, x_ref.shape[1]), 0)
    for r in range(rows + 2):
        if r == 0 or r == rows + 1:
            ref = above_ref if r == 0 else below_ref
            cells, lcell, rcell = ref[:cols], ref[cols:cols + 1], ref[cols + 1:cols + 2]
        else:
            cells = x_ref[(r - 1) * cols:r * cols]
            lcell, rcell = left_ref[r - 1:r], right_ref[r - 1:r]
        cells, lcell, rcell = silu(cells), silu(lcell), silu(rcell)
        at = slice(r * cols, (r + 1) * cols)
        shift1[at] = cells.astype(BF16)
        shift0[at] = jnp.where(side == 0, lcell, pltpu.roll(cells, 1, 0)).astype(BF16)
        shift2[at] = jnp.where(side == cols - 1, rcell, pltpu.roll(cells, cols - 1, 0)).astype(BF16)
    total = x_ref[...].astype(F32)
    for a in range(3):
        for b, shift in enumerate((shift0, shift1, shift2)):
            total = total + jnp.dot(
                shift[a * cols:(a + rows) * cols], w_ref[a, b], preferred_element_type=F32
            )
    features = total.astype(BF16)
    features_ref[...] = features
    values = features.astype(F32)
    centered = values - jnp.mean(values, axis=-1, keepdims=True)
    spread = jnp.mean(centered * centered, axis=-1, keepdims=True)
    normed = (centered * lax.rsqrt(spread + 1e-05)).astype(BF16)
    core = lax.axis_index("pcol")
    per = BLOCK // cores
    for b in range(rows * cols // BLOCK):
        for h in range(cores):
            rows_of = normed[b * BLOCK + h * per:b * BLOCK + (h + 1) * per]
            for s, ref in enumerate(half_refs):
                @pl.when(lax.rem(core + s, cores) == h)
                def _():
                    ref[b * per:(b + 1) * per] = rows_of


def conv_norm(cells, sides, conv_weight, cores):
    rows, cols, channels = cells.shape
    tokens = rows * cols
    return pl.pallas_call(
        functools.partial(conv_kernel, rows, cols, cores),
        out_shape=(shape(tokens, channels),) + (shape(tokens // cores, channels),) * cores,
        in_specs=[VMEM] * 6,
        out_specs=(VMEM,) * (1 + cores),
        scratch_shapes=[pltpu.VMEM(((rows + 2) * cols, channels), BF16)] * 3,
        compiler_params=grant(24),
        cost_estimate=cost(18 * tokens * channels**2, 18 * channels**2, tokens * channels),
        name="conv_norm",
    )(cells.reshape(tokens, channels), *sides, conv_weight)


class Table:
    def __init__(self, ref, anchors, images):
        self.ref, self.anchors, self.images = ref, anchors, images
        self.every_image = anchors == images

    @staticmethod
    def build(anchor_index, block_count, order):
        return jnp.concatenate([anchor_index, block_count, order.reshape(-1)])

    def anchor_at(self, image):
        found = jnp.int32(0)
        for a in range(1, self.anchors):
            found = jnp.where(self.ref[a] == image, a, found)
        return found

    def count(self, anchor):
        return self.ref[self.anchors + anchor]

    def block(self, anchor, slot):
        return self.ref[2 * self.anchors + anchor * NSEL + slot]

    def own_times(self, step, group, cores, prows, per_patch):
        if not self.every_image:
            return jnp.float32(1.0)
        s, b = divmod(group, per_patch)
        core = lax.axis_index("pcol")
        patch = source_of(lax.axis_index("prow"), crossed(core, step, prows), prows) * cores
        block = (patch + lax.rem(core + s, cores)) * per_patch + b
        anchor = self.anchor_at(lax.axis_index("image"))
        times = jnp.float32(1.0)
        for slot in range(NSEL):
            hit = (slot < self.count(anchor)) & (self.block(anchor, slot) == block)
            times = jnp.where(hit, 2.0, times)
        return times

    def anchor_times(self, source, slot):
        if self.every_image:
            image = source_of(lax.axis_index("image"), source + 1, self.images)
            source = self.anchor_at(image)
        return jnp.where(slot < self.count(source), 1.0, 0.0).astype(F32)


def project(normed, times, wk_ref, wv_ref, k_scr, v_scr):
    keys, channels = normed.shape
    k = jnp.dot(normed, wk_ref[...], preferred_element_type=F32).astype(BF16)
    for pair in range(channels // LANES):
        k_scr[pair] = k[:, pair * LANES:(pair + 1) * LANES]
    v = jnp.dot(normed, wv_ref[...], preferred_element_type=F32).astype(BF16).T
    per = keys // len(times)
    lane = lax.broadcasted_iota(jnp.int32, (1, keys), 1)
    mult = jnp.full((1, keys), times[0], F32)
    for g in range(1, len(times)):
        mult = jnp.where(lane >= g * per, times[g], mult)
    v = v * mult.astype(BF16)
    ones = jnp.broadcast_to(mult, (ONES, keys)).astype(BF16)
    for head in range(channels // HEAD_DIM):
        v_scr[head, :HEAD_DIM] = v[head * HEAD_DIM:(head + 1) * HEAD_DIM]
        v_scr[head, HEAD_DIM:] = ones


def attend_heads(q_ref, k_scr, v_scr, out_ref, level_ref, width, span=None):
    zeros = jnp.zeros((HEAD_DIM, width), BF16)
    items = [
        (head, slice(at, at + width))
        for head in range(q_ref.shape[0] // HEAD_DIM)
        for at in range(*(span or (0, q_ref.shape[1])), width)
    ]

    def scores_of(head, cols):
        q = q_ref[head * HEAD_DIM:(head + 1) * HEAD_DIM, cols]
        q = jnp.concatenate([q, zeros] if head % 2 == 0 else [zeros, q], axis=0)
        return jnp.dot(k_scr[head // 2], q, preferred_element_type=F32)

    ahead = [scores_of(*item) for item in items[:AHEAD]]
    for n, (head, cols) in enumerate(items):
        scores = ahead.pop(0)
        if n + AHEAD < len(items):
            ahead.append(scores_of(*items[n + AHEAD]))
        peak = jnp.max(scores, axis=0, keepdims=True)
        probs = jnp.exp(scores - peak).astype(BF16)
        value = jnp.dot(v_scr[head], probs, preferred_element_type=F32)
        total = value[HEAD_DIM:HEAD_DIM + 1]
        out_ref[head * HEAD_DIM:(head + 1) * HEAD_DIM, cols] = (
            value[:HEAD_DIM] * (1.0 / total)
        ).astype(out_ref.dtype)
        level_ref[head, :, cols] = jnp.broadcast_to(peak + jnp.log(total), (SUBLANES, width))


def own_kernel(info, n_parts, table_ref, *refs):
    anchors, images, cores, prows, per_patch = info
    part_refs, key_ref = refs[:n_parts], refs[n_parts]
    wq_ref, wk_ref, wv_ref, q_ref, out_ref, level_ref, k_scr, v_scr = refs[n_parts + 1:]
    table = Table(table_ref, anchors, images)
    at = 0
    for ref in part_refs:
        q = jnp.dot(ref[...], wq_ref[...], preferred_element_type=F32).astype(BF16)
        q_ref[:, at:at + ref.shape[0]] = q.T * BF16(HEAD_DIM ** (-0.5))
        at += ref.shape[0]
    times = [table.own_times(0, g, cores, prows, per_patch) for g in range(cores * per_patch)]
    project(key_ref[...], times, wk_ref, wv_ref, k_scr, v_scr)
    attend_heads(q_ref, k_scr, v_scr, out_ref, level_ref, part_refs[0].shape[0] * cores)


def key_scratch(keys, channels):
    return [
        pltpu.VMEM((channels // LANES, keys, LANES), BF16),
        pltpu.VMEM((channels // HEAD_DIM, HEAD_DIM + ONES, keys), BF16),
    ]


def attend_cost(rows, keys, channels, extra=0):
    return cost(
        4 * keys * channels**2 + 16 * rows * keys * channels + extra,
        2 * channels * (2 * rows + keys),
        rows * keys * channels // HEAD_DIM,
    )


def attend_own(info, table, parts, key, w_query, w_key, w_value):
    size, channels = key.shape
    rows = sum(part.shape[0] for part in parts)
    return pl.pallas_call(
        functools.partial(own_kernel, info, len(parts)),
        out_shape=(
            shape(channels, rows), shape(channels, rows),
            shape(channels // HEAD_DIM, SUBLANES, rows, dtype=F32),
        ),
        in_specs=[SMEM] + [VMEM] * (len(parts) + 4),
        out_specs=(VMEM,) * 3,
        scratch_shapes=key_scratch(size, channels),
        compiler_params=grant(24),
        cost_estimate=attend_cost(rows, size, channels, 2 * rows * channels**2),
        name="attend_own",
    )(table, *parts, key, w_query, w_key, w_value)


def plane_kernel(info, tiles, table_ref, q_ref, *refs):
    anchors, images, cores, prows, per_patch = info
    key_refs = refs[:tiles]
    wk_ref, wv_ref, out_ref, level_ref, k_scr, v_scr = refs[tiles:]
    table = Table(table_ref, anchors, images)
    times = [
        table.own_times(t + 1, g, cores, prows, per_patch)
        for t in range(tiles) for g in range(cores * per_patch)
    ]
    normed = jnp.concatenate([ref[...] for ref in key_refs], axis=0)
    project(normed, times, wk_ref, wv_ref, k_scr, v_scr)
    attend_heads(q_ref, k_scr, v_scr, out_ref, level_ref, q_ref.shape[1] // cores)


def attend_plane(info, table, queries, keys, w_key, w_value):
    size, channels = keys[0].shape
    rows = queries.shape[1]
    return pl.pallas_call(
        functools.partial(plane_kernel, info, len(keys)),
        out_shape=(
            shape(channels, rows), shape(channels // HEAD_DIM, SUBLANES, rows, dtype=F32),
        ),
        in_specs=[SMEM] + [VMEM] * (len(keys) + 3),
        out_specs=(VMEM,) * 2,
        scratch_shapes=key_scratch(size * len(keys), channels),
        compiler_params=grant(24),
        cost_estimate=attend_cost(rows, size * len(keys), channels),
        name="attend_plane",
    )(table, queries, *keys, w_key, w_value)


def merge_head(parts, head, cols):
    rows = slice(head * HEAD_DIM, (head + 1) * HEAD_DIM)
    levels = [level(head, cols) for _, level in parts]
    peak = functools.reduce(jnp.maximum, levels)
    weights = [jnp.exp(level - peak) for level in levels]
    total = functools.reduce(jnp.add, weights)
    value = functools.reduce(
        jnp.add, [w * ref[rows, cols].astype(F32) for w, (ref, _) in zip(weights, parts)]
    )
    return value * (1.0 / total), peak + jnp.log(total)


def anchor_kernel(info, tiles, earlier, groups, table_ref, q_ref, *refs):
    anchors, images, _, prows, _ = info
    key_refs, refs = refs[:tiles], refs[tiles:]
    early_refs, refs = refs[:2 * earlier], refs[2 * earlier:]
    wk_ref, wv_ref, k_ref, v_ref = refs[:4]
    sent_refs, (out_scr, level_scr) = refs[4:-2], refs[-2:]
    table = Table(table_ref, anchors, images)
    if table.every_image:
        each = NSEL // prows
        times = [
            table.anchor_times(s, source_of(lax.axis_index("prow"), t, prows) * each + slot)
            for t in range(tiles) for s in range(images - 1) for slot in range(each)
        ]
    else:
        times = [table.anchor_times(t, slot) for t in range(tiles) for slot in range(NSEL)]
    normed = jnp.concatenate([ref[...] for ref in key_refs], axis=0)
    project(normed, times, wk_ref, wv_ref, k_ref, v_ref)
    channels = q_ref.shape[0]
    width = q_ref.shape[1] // groups
    if groups > 1:
        attend_heads(q_ref, k_ref, v_ref, out_scr, level_scr, width, (width, groups * width))
    for n in range(1, groups):
        ref, cols = sent_refs[n - 1], slice(n * width, (n + 1) * width)
        levels = merge_all(list(early_refs) + [out_scr, level_scr], ref, cols)
        for term in range(3):
            high = levels.astype(BF16)
            at = channels + term * 2 * SUBLANES
            ref[at:at + 2 * SUBLANES] = high
            levels = levels - high.astype(F32)


def merge_all(refs, out_ref, cols):
    parts = [
        (ref, lambda head, at, level=level: level[head, 0:1, at])
        for ref, level in zip(refs[::2], refs[1::2])
    ]
    width = cols.stop - cols.start
    row = lax.broadcasted_iota(jnp.int32, (2 * SUBLANES, width), 0)
    levels = jnp.zeros((2 * SUBLANES, width), F32)
    for head in range(refs[0].shape[0] // HEAD_DIM):
        value, level = merge_head(parts, head, cols)
        out_ref[head * HEAD_DIM:(head + 1) * HEAD_DIM] = value.astype(BF16)
        levels = jnp.where(row == head, level, levels)
    return levels


def result_scratch(channels, rows):
    return [
        pltpu.VMEM((channels, rows), BF16),
        pltpu.VMEM((channels // HEAD_DIM, SUBLANES, rows), F32),
    ]


def attend_anchors(info, table, queries, keys, earlier, w_key, w_value, groups):
    size, channels = keys[0].shape
    rows = queries.shape[1]
    count = size * len(keys)
    flat = [leaf for part in earlier for leaf in part]
    return pl.pallas_call(
        functools.partial(anchor_kernel, info, len(keys), len(earlier), groups),
        out_shape=(
            shape(channels // LANES, count, LANES),
            shape(channels // HEAD_DIM, HEAD_DIM + ONES, count),
        ) + (shape(channels + 6 * SUBLANES, rows // groups),) * (groups - 1),
        in_specs=[SMEM] + [VMEM] * (len(keys) + len(flat) + 3),
        out_specs=(VMEM,) * (1 + groups),
        scratch_shapes=result_scratch(channels, rows),
        compiler_params=grant(24),
        cost_estimate=attend_cost(rows, count, channels),
        name="attend_anchors",
    )(table, queries, *keys, *flat, w_key, w_value)


def own_anchor_kernel(groups, q_ref, k_ref, v_ref, *refs):
    *early_refs, own_ref, level_ref, out_scr, level_scr = refs
    width = q_ref.shape[1] // groups
    attend_heads(q_ref, k_ref, v_ref, out_scr, level_scr, width, (0, width))
    level_ref[...] = merge_all(early_refs + [out_scr, level_scr], own_ref, slice(0, width))


def attend_anchors_own(queries, k, v, earlier, groups):
    channels, rows = queries.shape
    width = rows // groups
    flat = [leaf for part in earlier for leaf in part]
    return pl.pallas_call(
        functools.partial(own_anchor_kernel, groups),
        out_shape=(shape(channels, width), shape(2 * SUBLANES, width, dtype=F32)),
        in_specs=[VMEM] * (3 + len(flat)),
        out_specs=(VMEM,) * 2,
        scratch_shapes=result_scratch(channels, width),
        compiler_params=grant(24),
        cost_estimate=attend_cost(width, k.shape[1], channels),
        name="attend_anchors_own",
    )(queries, k, v, *flat)


def finish_kernel(cores, own_ref, level_ref, *refs):
    *received, w_ref, out_ref, merged = refs
    channels, tokens = own_ref.shape

    def row_of(ref, base, terms):
        def level(head, cols):
            return functools.reduce(jnp.add, [
                ref[base + t * 2 * SUBLANES:base + (t + 1) * 2 * SUBLANES].astype(F32)
                for t in range(terms)
            ])[head:head + 1]

        return level

    parts = [(own_ref, row_of(level_ref, 0, 1))]
    parts += [(ref, row_of(ref, channels, 3)) for ref in received]
    every = slice(0, tokens)
    for head in range(channels // HEAD_DIM):
        value, _ = merge_head(parts, head, every)
        merged[head * HEAD_DIM:(head + 1) * HEAD_DIM] = value.astype(BF16)
    out = lax.dot_general(
        merged[...], w_ref[...], (((0,), (0,)), ((), ())), preferred_element_type=F32
    ).astype(BF16)
    core = lax.axis_index("pcol")
    per = BLOCK // cores
    blocks = tokens // BLOCK
    for s in range(cores):
        for b in range(blocks):
            at = b * BLOCK + lax.rem(core + s, cores) * per
            out_ref[pl.ds(pl.multiple_of(at, per), per)] = out[
                (s * blocks + b) * per:(s * blocks + b + 1) * per
            ]


def finish(own, level, received, w_out, cores):
    channels, tokens = own.shape
    return pl.pallas_call(
        functools.partial(finish_kernel, cores),
        out_shape=shape(tokens, channels),
        in_specs=[VMEM] * (3 + len(received)),
        out_specs=VMEM,
        scratch_shapes=[pltpu.VMEM((channels, tokens), BF16)],
        compiler_params=grant(16),
        cost_estimate=cost(2 * tokens * channels**2, 2 * channels * (channels + 3 * tokens)),
        name="finish",
    )(own, level, *received, w_out)


def slot_place(table, anchor, slot, info):
    cores, per_patch = info[2], info[4]
    per = BLOCK // cores
    block = table.block(anchor, jnp.where(slot < table.count(anchor), slot, 0))
    patch, inner = lax.div(block, per_patch), lax.rem(block, per_patch)
    part = lax.rem(lax.rem(patch, cores) - lax.axis_index("pcol") + cores, cores)
    return lax.div(patch, cores), pl.multiple_of((part * per_patch + inner) * per, per)


def offer_kernel(info, table_ref, key_ref, *out_refs):
    anchors, images, cores, prows, _ = info
    table = Table(table_ref, anchors, images)
    anchor = table.anchor_at(lax.axis_index("image"))
    per, each = BLOCK // cores, NSEL // prows
    for step, ref in enumerate(out_refs):
        target = target_of(lax.axis_index("prow"), step, prows)
        for n in range(each):
            _, at = slot_place(table, anchor, target * each + n, info)
            ref[n * per:(n + 1) * per] = key_ref[pl.ds(at, per)]


def offer(info, table, key):
    rows = NSEL // info[3] * (BLOCK // info[2])
    return pl.pallas_call(
        functools.partial(offer_kernel, info),
        out_shape=(shape(rows, key.shape[1]),) * info[3],
        in_specs=[SMEM, VMEM],
        out_specs=(VMEM,) * info[3],
        compiler_params=grant(8),
        name="offer",
    )(table, key)


def accept_kernel(info, table_ref, *refs):
    anchors, images, cores, prows, _ = info
    *offers, out_ref = refs
    table = Table(table_ref, anchors, images)
    anchor = table.anchor_at(lax.axis_index("image"))
    prow = lax.axis_index("prow")
    per, each = BLOCK // cores, NSEL // prows
    for n in range(each):
        holder, _ = slot_place(table, anchor, prow * each + n, info)
        rows = slice(n * per, (n + 1) * per)
        for step, ref in enumerate(offers):
            @pl.when(step_of(prow, holder, prows) == step)
            def _():
                out_ref[rows] = ref[rows]


def accept(info, table, offers):
    return pl.pallas_call(
        functools.partial(accept_kernel, info),
        out_shape=shape(*offers[0].shape),
        in_specs=[SMEM] + [VMEM] * len(offers),
        out_specs=VMEM,
        compiler_params=grant(8),
        name="accept",
    )(table, *offers)


def anchor_rows(key, anchor_index, block_order, block_count, cores, per_patch):
    per = BLOCK // cores
    live = jnp.arange(NSEL) < block_count[:, None]
    block = jnp.where(live, block_order[:, :NSEL], block_order[:, :1])
    patch = block // per_patch
    part = (patch % cores - lax.axis_index("pcol")) % cores
    rows = key.reshape(-1, per, key.shape[1])[part * per_patch + block % per_patch]
    held = (patch // cores == lax.axis_index("prow")) & (
        anchor_index == lax.axis_index("image"))[:, None]
    rows = jnp.where(held[..., None, None], rows, jnp.zeros_like(rows))
    return lax.psum(rows.reshape(len(block), NSEL * per, -1), ("image", "prow"))


def shards(
    latent, conv_weight, w_query, w_key, w_value, w_out, anchor_index, block_order, block_count
):
    tile_rows, tile_cols, _ = latent.shape[1:]
    cores, prows, images = (lax.axis_size(a) for a in ("pcol", "prow", "image"))
    anchors = anchor_index.shape[0]
    per_patch = tile_rows * tile_cols // BLOCK
    info = (anchors, images, cores, prows, per_patch)
    features, *parts = conv_norm(latent[0], halo(latent[0]), stage(conv_weight), cores)
    parts, *anchoring = lax.optimization_barrier((parts, anchor_index, block_count, block_order))
    anchor_index, block_count, block_order = anchoring
    table = Table.build(anchor_index, block_count, block_order[:, :NSEL])
    keys, queries = [parts[0]], list(parts)
    for s in range(1, cores):
        theirs = [None] * cores
        for t in [cores - s] + [t for t in range(cores) if t != cores - s]:
            theirs[t] = shifted(parts[t], "pcol", s)
        keys.append(theirs[cores - s])
        queries += theirs
    key = jnp.concatenate(keys, axis=0)
    every_image = anchors == images
    if every_image:
        mine, *offers = offer(info, table, key)
        received = [mine]
        for s, rows in enumerate(offers, 1):
            received.append(exchange(rows, "prow", s))
    plane = gathered(key)
    q, value, level = attend_own(info, table, queries, key, w_query, w_key, w_value)
    done = [(value, level)]
    if every_image:
        share = accept(info, table, received)
        across = []
        for s in range(1, images):
            across.append(exchange(share, "image", s))
        local = jnp.concatenate(across, axis=0)
        sources = [local]
        for s in range(1, prows):
            sources.append(exchange(local, "prow", s))
    else:
        joined = anchor_rows(key, anchor_index, block_order, block_count, cores, per_patch)
        sources = [joined[anchor] for anchor in range(anchors)]
    if plane:
        done.append(attend_plane(info, table, q, plane, w_key, w_value))
    k, v, *sent = attend_anchors(info, table, q, sources, done, w_key, w_value, cores)
    received = []
    for s, block in enumerate(sent, 1):
        received.append(shifted(block, "pcol", cores - s))
    own, level = attend_anchors_own(q, k, v, done, cores)
    attended = finish(own, level, received, w_out, cores)
    return features.reshape(latent.shape), attended.reshape(latent.shape)


def solution(mesh):
    tiled = P(("group", "image"), "prow", "pcol", None)
    return jax.shard_map(
        shards,
        mesh=mesh,
        in_specs=(tiled, P(), P(), P(), P(), P(), P("group"), P("group", None), P("group")),
        out_specs=(tiled, tiled),
        check_vma=False,
    )
```

```python
import functools

import jax
import jax.numpy as jnp
from jax import lax
from jax.experimental import pallas as pl
from jax.experimental.pallas import tpu as pltpu
from jax.sharding import PartitionSpec as P

HEAD_DIM = 64
BLOCK = 128
NSEL = 4
LANES = 128
SUBLANES = 8
ONES = 16
AHEAD = 3
EDGE_MIB = 60
EDGE_FLOPS = 4 * 10**9
STAGE_MIB = 46
F32 = jnp.float32
BF16 = jnp.bfloat16
MIB = 1 << 20


VMEM = pl.BlockSpec(memory_space=pltpu.VMEM)
ANY = pl.BlockSpec(memory_space=pl.ANY)
SMEM = pl.BlockSpec(memory_space=pltpu.SMEM)


def shape(*dims, dtype=BF16):
    return jax.ShapeDtypeStruct(dims, dtype)


def cost(flops, moved, exps=0):
    return pl.CostEstimate(flops=flops, bytes_accessed=moved, transcendentals=exps)


def grant(mib):
    return pltpu.CompilerParams(vmem_limit_bytes=mib * MIB)


def source_of(index, step, count):
    if count & (count - 1) == 0:
        return index ^ step
    return lax.rem(index + step, count) if not isinstance(index, int) else (index + step) % count


def target_of(index, step, count):
    if count & (count - 1) == 0:
        return index ^ step
    return lax.rem(index - step + count, count)


def step_of(index, source, count):
    if count & (count - 1) == 0:
        return index ^ source
    return lax.rem(source - index + count, count)


def exchange(block, axis, step):
    count = lax.axis_size(axis)
    return lax.ppermute(block, axis, [(source_of(i, step, count), i) for i in range(count)])


def shifted(block, axis, step):
    count = lax.axis_size(axis)
    return lax.ppermute(block, axis, [((i + step) % count, i) for i in range(count)])


def crossed(core, entry, prows):
    if prows != 4 or entry not in (1, 2):
        return entry
    return jnp.where(lax.rem(core, 2) == 1, 3 - entry, entry)


def gathered(block):
    prows, cores = lax.axis_size("prow"), lax.axis_size("pcol")
    if prows != 4:
        return [exchange(block, "prow", s) for s in range(1, prows)]

    def hop(rows, entry):
        return lax.ppermute(rows, ("prow", "pcol"), [
            ((p ^ (entry if c % 2 == 0 else 3 - entry)) * cores + c, p * cores + c)
            for p in range(prows) for c in range(cores)
        ])

    near, side = hop(block, 1), hop(block, 2)
    return [near, side, hop(near, 2)]


def edges_kernel(x_ref, first_ref, last_ref, top_ref, bottom_ref, strips, sem):
    rows, cols, _ = x_ref.shape
    part = strips.shape[2]
    copies = [
        pltpu.make_async_copy(source, target, sem.at[n])
        for n, (source, target) in enumerate((
            (x_ref.at[:, :part], strips.at[0]),
            (x_ref.at[:, cols - part:], strips.at[1]),
            (x_ref.at[0], top_ref),
            (x_ref.at[rows - 1], bottom_ref),
        ))
    ]
    for copy in copies:
        copy.start()
    for copy in copies:
        copy.wait()
    first_ref[...] = strips[0].astype(F32)[:, 0].astype(BF16)
    last_ref[...] = strips[1].astype(F32)[:, part - 1].astype(BF16)


def edges(cells):
    rows, cols, channels = cells.shape
    return pl.pallas_call(
        edges_kernel,
        out_shape=(shape(rows, channels),) * 2 + (shape(cols, channels),) * 2,
        in_specs=[ANY],
        out_specs=(VMEM,) * 4,
        scratch_shapes=[
            pltpu.VMEM((2, rows, 2 * SUBLANES, channels), BF16), pltpu.SemaphoreType.DMA((4,)),
        ],
        compiler_params=grant(EDGE_MIB),
        cost_estimate=cost(EDGE_FLOPS, cells.nbytes),
        name="edges",
    )(cells)


def halo(cells):
    first, last, top, bottom = edges(cells)
    core, cores = lax.axis_index("pcol"), lax.axis_size("pcol")
    rows = lax.axis_size("prow")
    if cores == 2:
        other = shifted(jnp.where(core == 0, last, first), "pcol", 1)
        zero = jnp.zeros_like(other)
        left = jnp.where(core == 1, other, zero)
        right = jnp.where(core == 0, other, zero)
    else:
        left = lax.ppermute(last, "pcol", [(i, i + 1) for i in range(cores - 1)])
        right = lax.ppermute(first, "pcol", [(i + 1, i) for i in range(cores - 1)])
    low = jnp.concatenate([bottom, left[-1:], right[-1:]], axis=0)
    high = jnp.concatenate([top, left[:1], right[:1]], axis=0)
    odd = lax.rem(lax.axis_index("prow"), 2) == 1
    swaps = []
    for first in range(2):
        pairs = [(i, i + 1) for i in range(first, rows - 1, 2)]
        block = jnp.where(odd, high, low) if first == 0 else jnp.where(odd, low, high)
        swaps.append(lax.ppermute(block, "prow", pairs + [(j, i) for i, j in pairs]))
    above = jnp.where(odd, swaps[0], swaps[1])
    below = jnp.where(odd, swaps[1], swaps[0])
    return left, right, above, below


def stage_kernel(in_ref, out_ref, sem):
    copy = pltpu.make_async_copy(in_ref, out_ref, sem)
    copy.start()
    copy.wait()


def stage(array):
    return pl.pallas_call(
        stage_kernel,
        out_shape=shape(*array.shape),
        in_specs=[ANY],
        out_specs=VMEM,
        scratch_shapes=[pltpu.SemaphoreType.DMA],
        compiler_params=grant(STAGE_MIB),
        cost_estimate=cost(0, 2 * array.nbytes),
        name="stage",
    )(array)


def conv_kernel(rows, cols, cores, x_ref, left_ref, right_ref, above_ref, below_ref, w_ref, *refs):
    features_ref, *half_refs, shift0, shift1, shift2 = refs

    def silu(v):
        v = v.astype(F32)
        return (v / (1.0 + jnp.exp(-v))).astype(BF16).astype(F32)

    side = lax.broadcasted_iota(jnp.int32, (cols, x_ref.shape[1]), 0)
    for r in range(rows + 2):
        if r == 0 or r == rows + 1:
            ref = above_ref if r == 0 else below_ref
            cells, lcell, rcell = ref[:cols], ref[cols:cols + 1], ref[cols + 1:cols + 2]
        else:
            cells = x_ref[(r - 1) * cols:r * cols]
            lcell, rcell = left_ref[r - 1:r], right_ref[r - 1:r]
        cells, lcell, rcell = silu(cells), silu(lcell), silu(rcell)
        at = slice(r * cols, (r + 1) * cols)
        shift1[at] = cells.astype(BF16)
        shift0[at] = jnp.where(side == 0, lcell, pltpu.roll(cells, 1, 0)).astype(BF16)
        shift2[at] = jnp.where(side == cols - 1, rcell, pltpu.roll(cells, cols - 1, 0)).astype(BF16)
    total = x_ref[...].astype(F32)
    for a in range(3):
        for b, shift in enumerate((shift0, shift1, shift2)):
            total = total + jnp.dot(
                shift[a * cols:(a + rows) * cols], w_ref[a, b], preferred_element_type=F32
            )
    features = total.astype(BF16)
    features_ref[...] = features
    values = features.astype(F32)
    centered = values - jnp.mean(values, axis=-1, keepdims=True)
    spread = jnp.mean(centered * centered, axis=-1, keepdims=True)
    normed = (centered * lax.rsqrt(spread + 1e-05)).astype(BF16)
    core = lax.axis_index("pcol")
    per = BLOCK // cores
    for b in range(rows * cols // BLOCK):
        for h in range(cores):
            rows_of = normed[b * BLOCK + h * per:b * BLOCK + (h + 1) * per]
            for s, ref in enumerate(half_refs):
                @pl.when(lax.rem(core + s, cores) == h)
                def _():
                    ref[b * per:(b + 1) * per] = rows_of


def conv_norm(cells, sides, conv_weight, cores):
    rows, cols, channels = cells.shape
    tokens = rows * cols
    return pl.pallas_call(
        functools.partial(conv_kernel, rows, cols, cores),
        out_shape=(shape(tokens, channels),) + (shape(tokens // cores, channels),) * cores,
        in_specs=[VMEM] * 6,
        out_specs=(VMEM,) * (1 + cores),
        scratch_shapes=[pltpu.VMEM(((rows + 2) * cols, channels), BF16)] * 3,
        compiler_params=grant(24),
        cost_estimate=cost(18 * tokens * channels**2, 18 * channels**2, tokens * channels),
        name="conv_norm",
    )(cells.reshape(tokens, channels), *sides, conv_weight)


class Table:
    def __init__(self, ref, anchors, images):
        self.ref, self.anchors, self.images = ref, anchors, images
        self.every_image = anchors == images

    @staticmethod
    def build(anchor_index, block_count, order):
        return jnp.concatenate([anchor_index, block_count, order.reshape(-1)])

    def anchor_at(self, image):
        found = jnp.int32(0)
        for a in range(1, self.anchors):
            found = jnp.where(self.ref[a] == image, a, found)
        return found

    def count(self, anchor):
        return self.ref[self.anchors + anchor]

    def block(self, anchor, slot):
        return self.ref[2 * self.anchors + anchor * NSEL + slot]

    def own_times(self, step, group, cores, prows, per_patch):
        if not self.every_image:
            return jnp.float32(1.0)
        s, b = divmod(group, per_patch)
        core = lax.axis_index("pcol")
        patch = source_of(lax.axis_index("prow"), crossed(core, step, prows), prows) * cores
        block = (patch + lax.rem(core + s, cores)) * per_patch + b
        anchor = self.anchor_at(lax.axis_index("image"))
        times = jnp.float32(1.0)
        for slot in range(NSEL):
            hit = (slot < self.count(anchor)) & (self.block(anchor, slot) == block)
            times = jnp.where(hit, 2.0, times)
        return times

    def anchor_times(self, source, slot):
        if self.every_image:
            image = source_of(lax.axis_index("image"), source + 1, self.images)
            source = self.anchor_at(image)
        return jnp.where(slot < self.count(source), 1.0, 0.0).astype(F32)


def project(normed, times, wk_ref, wv_ref, k_scr, v_scr):
    keys, channels = normed.shape
    k = jnp.dot(normed, wk_ref[...], preferred_element_type=F32).astype(BF16)
    for pair in range(channels // LANES):
        k_scr[pair] = k[:, pair * LANES:(pair + 1) * LANES]
    v = jnp.dot(normed, wv_ref[...], preferred_element_type=F32).astype(BF16).T
    per = keys // len(times)
    lane = lax.broadcasted_iota(jnp.int32, (1, keys), 1)
    mult = jnp.full((1, keys), times[0], F32)
    for g in range(1, len(times)):
        mult = jnp.where(lane >= g * per, times[g], mult)
    v = v * mult.astype(BF16)
    ones = jnp.broadcast_to(mult, (ONES, keys)).astype(BF16)
    for head in range(channels // HEAD_DIM):
        v_scr[head, :HEAD_DIM] = v[head * HEAD_DIM:(head + 1) * HEAD_DIM]
        v_scr[head, HEAD_DIM:] = ones


def attend_heads(q_ref, k_scr, v_scr, out_ref, level_ref, width, span=None):
    zeros = jnp.zeros((HEAD_DIM, width), BF16)
    items = [
        (head, slice(at, at + width))
        for head in range(q_ref.shape[0] // HEAD_DIM)
        for at in range(*(span or (0, q_ref.shape[1])), width)
    ]

    def scores_of(head, cols):
        q = q_ref[head * HEAD_DIM:(head + 1) * HEAD_DIM, cols]
        q = jnp.concatenate([q, zeros] if head % 2 == 0 else [zeros, q], axis=0)
        return jnp.dot(k_scr[head // 2], q, preferred_element_type=F32)

    ahead = [scores_of(*item) for item in items[:AHEAD]]
    for n, (head, cols) in enumerate(items):
        scores = ahead.pop(0)
        if n + AHEAD < len(items):
            ahead.append(scores_of(*items[n + AHEAD]))
        peak = jnp.max(scores, axis=0, keepdims=True)
        probs = jnp.exp(scores - peak).astype(BF16)
        value = jnp.dot(v_scr[head], probs, preferred_element_type=F32)
        total = value[HEAD_DIM:HEAD_DIM + 1]
        out_ref[head * HEAD_DIM:(head + 1) * HEAD_DIM, cols] = (
            value[:HEAD_DIM] * (1.0 / total)
        ).astype(out_ref.dtype)
        level_ref[head, :, cols] = jnp.broadcast_to(peak + jnp.log(total), (SUBLANES, width))


def own_kernel(info, n_parts, table_ref, *refs):
    anchors, images, cores, prows, per_patch = info
    part_refs, key_ref = refs[:n_parts], refs[n_parts]
    wq_ref, wk_ref, wv_ref, q_ref, out_ref, level_ref, k_scr, v_scr = refs[n_parts + 1:]
    table = Table(table_ref, anchors, images)
    at = 0
    for ref in part_refs:
        q = jnp.dot(ref[...], wq_ref[...], preferred_element_type=F32).astype(BF16)
        q_ref[:, at:at + ref.shape[0]] = q.T * BF16(HEAD_DIM ** (-0.5))
        at += ref.shape[0]
    times = [table.own_times(0, g, cores, prows, per_patch) for g in range(cores * per_patch)]
    project(key_ref[...], times, wk_ref, wv_ref, k_scr, v_scr)
    attend_heads(q_ref, k_scr, v_scr, out_ref, level_ref, part_refs[0].shape[0] * cores)


def key_scratch(keys, channels):
    return [
        pltpu.VMEM((channels // LANES, keys, LANES), BF16),
        pltpu.VMEM((channels // HEAD_DIM, HEAD_DIM + ONES, keys), BF16),
    ]


def attend_cost(rows, keys, channels, extra=0):
    return cost(
        4 * keys * channels**2 + 16 * rows * keys * channels + extra,
        2 * channels * (2 * rows + keys),
        rows * keys * channels // HEAD_DIM,
    )


def attend_own(info, table, parts, key, w_query, w_key, w_value):
    size, channels = key.shape
    rows = sum(part.shape[0] for part in parts)
    return pl.pallas_call(
        functools.partial(own_kernel, info, len(parts)),
        out_shape=(
            shape(channels, rows), shape(channels, rows),
            shape(channels // HEAD_DIM, SUBLANES, rows, dtype=F32),
        ),
        in_specs=[SMEM] + [VMEM] * (len(parts) + 4),
        out_specs=(VMEM,) * 3,
        scratch_shapes=key_scratch(size, channels),
        compiler_params=grant(24),
        cost_estimate=attend_cost(rows, size, channels, 2 * rows * channels**2),
        name="attend_own",
    )(table, *parts, key, w_query, w_key, w_value)


def plane_kernel(info, tiles, table_ref, q_ref, *refs):
    anchors, images, cores, prows, per_patch = info
    key_refs = refs[:tiles]
    wk_ref, wv_ref, out_ref, level_ref, k_scr, v_scr = refs[tiles:]
    table = Table(table_ref, anchors, images)
    times = [
        table.own_times(t + 1, g, cores, prows, per_patch)
        for t in range(tiles) for g in range(cores * per_patch)
    ]
    normed = jnp.concatenate([ref[...] for ref in key_refs], axis=0)
    project(normed, times, wk_ref, wv_ref, k_scr, v_scr)
    attend_heads(q_ref, k_scr, v_scr, out_ref, level_ref, q_ref.shape[1] // cores)


def attend_plane(info, table, queries, keys, w_key, w_value):
    size, channels = keys[0].shape
    rows = queries.shape[1]
    return pl.pallas_call(
        functools.partial(plane_kernel, info, len(keys)),
        out_shape=(
            shape(channels, rows), shape(channels // HEAD_DIM, SUBLANES, rows, dtype=F32),
        ),
        in_specs=[SMEM] + [VMEM] * (len(keys) + 3),
        out_specs=(VMEM,) * 2,
        scratch_shapes=key_scratch(size * len(keys), channels),
        compiler_params=grant(24),
        cost_estimate=attend_cost(rows, size * len(keys), channels),
        name="attend_plane",
    )(table, queries, *keys, w_key, w_value)


def merge_head(parts, head, cols):
    rows = slice(head * HEAD_DIM, (head + 1) * HEAD_DIM)
    levels = [level(head, cols) for _, level in parts]
    peak = functools.reduce(jnp.maximum, levels)
    weights = [jnp.exp(level - peak) for level in levels]
    total = functools.reduce(jnp.add, weights)
    value = functools.reduce(
        jnp.add, [w * ref[rows, cols].astype(F32) for w, (ref, _) in zip(weights, parts)]
    )
    return value * (1.0 / total), peak + jnp.log(total)


def anchor_kernel(info, tiles, earlier, groups, table_ref, q_ref, *refs):
    anchors, images, _, prows, _ = info
    key_refs, refs = refs[:tiles], refs[tiles:]
    early_refs, refs = refs[:2 * earlier], refs[2 * earlier:]
    wk_ref, wv_ref, k_ref, v_ref = refs[:4]
    sent_refs, (out_scr, level_scr) = refs[4:-2], refs[-2:]
    table = Table(table_ref, anchors, images)
    if table.every_image:
        each = NSEL // prows
        times = [
            table.anchor_times(s, source_of(lax.axis_index("prow"), t, prows) * each + slot)
            for t in range(tiles) for s in range(images - 1) for slot in range(each)
        ]
    else:
        times = [table.anchor_times(t, slot) for t in range(tiles) for slot in range(NSEL)]
    normed = jnp.concatenate([ref[...] for ref in key_refs], axis=0)
    project(normed, times, wk_ref, wv_ref, k_ref, v_ref)
    channels = q_ref.shape[0]
    width = q_ref.shape[1] // groups
    if groups > 1:
        attend_heads(q_ref, k_ref, v_ref, out_scr, level_scr, width, (width, groups * width))
    for n in range(1, groups):
        ref, cols = sent_refs[n - 1], slice(n * width, (n + 1) * width)
        levels = merge_all(list(early_refs) + [out_scr, level_scr], ref, cols)
        for term in range(3):
            high = levels.astype(BF16)
            at = channels + term * 2 * SUBLANES
            ref[at:at + 2 * SUBLANES] = high
            levels = levels - high.astype(F32)


def merge_all(refs, out_ref, cols):
    parts = [
        (ref, lambda head, at, level=level: level[head, 0:1, at])
        for ref, level in zip(refs[::2], refs[1::2])
    ]
    width = cols.stop - cols.start
    row = lax.broadcasted_iota(jnp.int32, (2 * SUBLANES, width), 0)
    levels = jnp.zeros((2 * SUBLANES, width), F32)
    for head in range(refs[0].shape[0] // HEAD_DIM):
        value, level = merge_head(parts, head, cols)
        out_ref[head * HEAD_DIM:(head + 1) * HEAD_DIM] = value.astype(BF16)
        levels = jnp.where(row == head, level, levels)
    return levels


def result_scratch(channels, rows):
    return [
        pltpu.VMEM((channels, rows), BF16),
        pltpu.VMEM((channels // HEAD_DIM, SUBLANES, rows), F32),
    ]


def attend_anchors(info, table, queries, keys, earlier, w_key, w_value, groups):
    size, channels = keys[0].shape
    rows = queries.shape[1]
    count = size * len(keys)
    flat = [leaf for part in earlier for leaf in part]
    return pl.pallas_call(
        functools.partial(anchor_kernel, info, len(keys), len(earlier), groups),
        out_shape=(
            shape(channels // LANES, count, LANES),
            shape(channels // HEAD_DIM, HEAD_DIM + ONES, count),
        ) + (shape(channels + 6 * SUBLANES, rows // groups),) * (groups - 1),
        in_specs=[SMEM] + [VMEM] * (len(keys) + len(flat) + 3),
        out_specs=(VMEM,) * (1 + groups),
        scratch_shapes=result_scratch(channels, rows),
        compiler_params=grant(24),
        cost_estimate=attend_cost(rows, count, channels),
        name="attend_anchors",
    )(table, queries, *keys, *flat, w_key, w_value)


def own_anchor_kernel(groups, q_ref, k_ref, v_ref, *refs):
    *early_refs, own_ref, level_ref, out_scr, level_scr = refs
    width = q_ref.shape[1] // groups
    attend_heads(q_ref, k_ref, v_ref, out_scr, level_scr, width, (0, width))
    level_ref[...] = merge_all(early_refs + [out_scr, level_scr], own_ref, slice(0, width))


def attend_anchors_own(queries, k, v, earlier, groups):
    channels, rows = queries.shape
    width = rows // groups
    flat = [leaf for part in earlier for leaf in part]
    return pl.pallas_call(
        functools.partial(own_anchor_kernel, groups),
        out_shape=(shape(channels, width), shape(2 * SUBLANES, width, dtype=F32)),
        in_specs=[VMEM] * (3 + len(flat)),
        out_specs=(VMEM,) * 2,
        scratch_shapes=result_scratch(channels, width),
        compiler_params=grant(24),
        cost_estimate=attend_cost(width, k.shape[1], channels),
        name="attend_anchors_own",
    )(queries, k, v, *flat)


def finish_kernel(cores, own_ref, level_ref, *refs):
    *received, w_ref, out_ref, merged = refs
    channels, tokens = own_ref.shape

    def row_of(ref, base, terms):
        def level(head, cols):
            return functools.reduce(jnp.add, [
                ref[base + t * 2 * SUBLANES:base + (t + 1) * 2 * SUBLANES].astype(F32)
                for t in range(terms)
            ])[head:head + 1]

        return level

    parts = [(own_ref, row_of(level_ref, 0, 1))]
    parts += [(ref, row_of(ref, channels, 3)) for ref in received]
    every = slice(0, tokens)
    for head in range(channels // HEAD_DIM):
        value, _ = merge_head(parts, head, every)
        merged[head * HEAD_DIM:(head + 1) * HEAD_DIM] = value.astype(BF16)
    out = lax.dot_general(
        merged[...], w_ref[...], (((0,), (0,)), ((), ())), preferred_element_type=F32
    ).astype(BF16)
    core = lax.axis_index("pcol")
    per = BLOCK // cores
    blocks = tokens // BLOCK
    for s in range(cores):
        for b in range(blocks):
            at = b * BLOCK + lax.rem(core + s, cores) * per
            out_ref[pl.ds(pl.multiple_of(at, per), per)] = out[
                (s * blocks + b) * per:(s * blocks + b + 1) * per
            ]


def finish(own, level, received, w_out, cores):
    channels, tokens = own.shape
    return pl.pallas_call(
        functools.partial(finish_kernel, cores),
        out_shape=shape(tokens, channels),
        in_specs=[VMEM] * (3 + len(received)),
        out_specs=VMEM,
        scratch_shapes=[pltpu.VMEM((channels, tokens), BF16)],
        compiler_params=grant(16),
        cost_estimate=cost(2 * tokens * channels**2, 2 * channels * (channels + 3 * tokens)),
        name="finish",
    )(own, level, *received, w_out)


def slot_place(table, anchor, slot, info):
    cores, per_patch = info[2], info[4]
    per = BLOCK // cores
    block = table.block(anchor, jnp.where(slot < table.count(anchor), slot, 0))
    patch, inner = lax.div(block, per_patch), lax.rem(block, per_patch)
    part = lax.rem(lax.rem(patch, cores) - lax.axis_index("pcol") + cores, cores)
    return lax.div(patch, cores), pl.multiple_of((part * per_patch + inner) * per, per)


def offer_kernel(info, table_ref, key_ref, *out_refs):
    anchors, images, cores, prows, _ = info
    table = Table(table_ref, anchors, images)
    anchor = table.anchor_at(lax.axis_index("image"))
    per, each = BLOCK // cores, NSEL // prows
    for step, ref in enumerate(out_refs):
        target = target_of(lax.axis_index("prow"), step, prows)
        for n in range(each):
            _, at = slot_place(table, anchor, target * each + n, info)
            ref[n * per:(n + 1) * per] = key_ref[pl.ds(at, per)]


def offer(info, table, key):
    rows = NSEL // info[3] * (BLOCK // info[2])
    return pl.pallas_call(
        functools.partial(offer_kernel, info),
        out_shape=(shape(rows, key.shape[1]),) * info[3],
        in_specs=[SMEM, VMEM],
        out_specs=(VMEM,) * info[3],
        compiler_params=grant(8),
        name="offer",
    )(table, key)


def accept_kernel(info, table_ref, *refs):
    anchors, images, cores, prows, _ = info
    *offers, out_ref = refs
    table = Table(table_ref, anchors, images)
    anchor = table.anchor_at(lax.axis_index("image"))
    prow = lax.axis_index("prow")
    per, each = BLOCK // cores, NSEL // prows
    for n in range(each):
        holder, _ = slot_place(table, anchor, prow * each + n, info)
        rows = slice(n * per, (n + 1) * per)
        for step, ref in enumerate(offers):
            @pl.when(step_of(prow, holder, prows) == step)
            def _():
                out_ref[rows] = ref[rows]


def accept(info, table, offers):
    return pl.pallas_call(
        functools.partial(accept_kernel, info),
        out_shape=shape(*offers[0].shape),
        in_specs=[SMEM] + [VMEM] * len(offers),
        out_specs=VMEM,
        compiler_params=grant(8),
        name="accept",
    )(table, *offers)


def anchor_rows(key, anchor_index, block_order, block_count, cores, per_patch):
    per = BLOCK // cores
    live = jnp.arange(NSEL) < block_count[:, None]
    block = jnp.where(live, block_order[:, :NSEL], block_order[:, :1])
    patch = block // per_patch
    part = (patch % cores - lax.axis_index("pcol")) % cores
    rows = key.reshape(-1, per, key.shape[1])[part * per_patch + block % per_patch]
    held = (patch // cores == lax.axis_index("prow")) & (
        anchor_index == lax.axis_index("image"))[:, None]
    rows = jnp.where(held[..., None, None], rows, jnp.zeros_like(rows))
    return lax.psum(rows.reshape(len(block), NSEL * per, -1), ("image", "prow"))


def shards(
    latent, conv_weight, w_query, w_key, w_value, w_out, anchor_index, block_order, block_count
):
    tile_rows, tile_cols, _ = latent.shape[1:]
    cores, prows, images = (lax.axis_size(a) for a in ("pcol", "prow", "image"))
    anchors = anchor_index.shape[0]
    per_patch = tile_rows * tile_cols // BLOCK
    info = (anchors, images, cores, prows, per_patch)
    features, *parts = conv_norm(latent[0], halo(latent[0]), stage(conv_weight), cores)
    parts, *anchoring = lax.optimization_barrier((parts, anchor_index, block_count, block_order))
    anchor_index, block_count, block_order = anchoring
    table = Table.build(anchor_index, block_count, block_order[:, :NSEL])
    keys, queries = [parts[0]], list(parts)
    for s in range(1, cores):
        theirs = [None] * cores
        for t in [cores - s] + [t for t in range(cores) if t != cores - s]:
            theirs[t] = shifted(parts[t], "pcol", s)
        keys.append(theirs[cores - s])
        queries += theirs
    key = jnp.concatenate(keys, axis=0)
    every_image = anchors == images
    if every_image:
        mine, *offers = offer(info, table, key)
        received = [mine]
        for s, rows in enumerate(offers, 1):
            received.append(exchange(rows, "prow", s))
    plane = gathered(key)
    q, value, level = attend_own(info, table, queries, key, w_query, w_key, w_value)
    done = [(value, level)]
    if every_image:
        share = accept(info, table, received)
        across = []
        for s in range(1, images):
            across.append(exchange(share, "image", s))
        local = jnp.concatenate(across, axis=0)
        sources = [local]
        for s in range(1, prows):
            sources.append(exchange(local, "prow", s))
    else:
        joined = anchor_rows(key, anchor_index, block_order, block_count, cores, per_patch)
        sources = [joined[anchor] for anchor in range(anchors)]
    if plane:
        done.append(attend_plane(info, table, q, plane, w_key, w_value))
    k, v, *sent = attend_anchors(info, table, q, sources, done, w_key, w_value, cores)
    received = []
    for s, block in enumerate(sent, 1):
        received.append(shifted(block, "pcol", cores - s))
    own, level = attend_anchors_own(q, k, v, done, cores)
    attended = finish(own, level, received, w_out, cores)
    return features.reshape(latent.shape), attended.reshape(latent.shape)


def solution(mesh):
    tiled = P(("group", "image"), "prow", "pcol", None)
    return jax.shard_map(
        shards,
        mesh=mesh,
        in_specs=(tiled, P(), P(), P(), P(), P(), P("group"), P("group", None), P("group")),
        out_specs=(tiled, tiled),
        check_vma=False,
    )
```
